256 devices in a mesh: seq: 32 (over z_hi, y, core), tp: 8 (over z_lo, x).
Axes of the slice: x: 4, y: 4, z: 8 (z_hi: 4, z_lo: 2; z = z_hi * 2 + z_lo), core: 2. Of those that a mesh axis runs over, the one named last changes fastest.
Arguments:
- hidden_sel: bfloat16 [8192, 7168], P('seq', 'tp'), may hold values from -6 to 6
- w_query: bfloat16 [7168, 4096], P(None, 'tp'), may hold values from -0.0625 to 0.0625
- w_key: bfloat16 [7168, 1024], P(None, 'tp'), may hold values from -0.0625 to 0.0625
- w_value: bfloat16 [7168, 1024], P(None, 'tp'), may hold values from -0.0625 to 0.0625
- key_cache: bfloat16 [65536, 1024], P('seq', 'tp')
- value_cache: bfloat16 [65536, 1024], P('seq', 'tp'), may hold values from -6 to 6
- span_count: int32 [8], replicated, may hold values from 1 to 8, 32 in all
- span_key: int32 [8, 8], replicated, may hold values from 0 to 7, each once within a row
- cache_offset: int32 [64], P('seq'), may hold values from 0 to 8191
- sel_index: int32 [64, 128], P('seq'), may hold values from 0 to 1023, as said below
Outputs:
- attn_out: bfloat16 [8192, 4096], P('seq', 'tp')
The draws below stay inside these ranges and needn't reach their ends.
Inputs may be any that keep to these rules, and one draw needn't show every extreme that they name: `sel_index`: each row holds 128 different positions in rising order. `span_count`: the counts sum to 32, and the largest is exactly 8. `span_key`: each row is a permutation of 0 to 7.
All inputs are finite; a program needn't handle non-finite values.
Results may differ from the reference program's by a relative error of at most 0.023.
Values may be sent and summed in bfloat16 or wider, within the bound.
No kernel may reach another device: no remote copies, remote signals or barrier semaphores. Data moves between devices by JAX's collectives and lax.ppermute only.
A program may use at most 128 MiB of HBM per device.

```python
import math
import jax
import jax.numpy as jnp
import numpy as np
from jax import lax

D = 7168
KV = 8
HD = 128
HG = 4
R = 8
MAXCH = 8
SPAN = 1024
SEL = 128
NBLK = 64


def draw_key_cache(key, part):
    rows = NBLK * SPAN
    cols = KV * HD
    first = jax.random.fold_in(key, 0)
    base = jax.random.normal(first, (rows, cols), jnp.float32)
    return base.astype(jnp.bfloat16)


def draw_sel_index(key, part):
    keys = jax.random.split(key, NBLK)

    def one_row(row_key):
        return jnp.sort(jax.random.permutation(row_key, SPAN)[:SEL]).astype(jnp.int32)
    return jax.vmap(one_row)(keys)


def touch_ends(entries, rng, smallest, top_value):
    dims = entries.shape
    index_at = [jax.random.randint(jax.random.fold_in(rng, axis), (), 0, dims[axis]) for axis in range(len(dims))]
    entries = entries.at[tuple(index_at)].set(smallest)
    longest = dims.index(max(dims))
    index_at[longest] = (index_at[longest] + 1) % dims[longest]
    return entries.at[tuple(index_at)].set(top_value)


def block_scale(stream_key, shape, pieces, low, top_value):
    gain = 1.0
    for position, blocks in pieces:
        heights = jax.random.uniform(jax.random.fold_in(jax.random.fold_in(stream_key, 6), position), (blocks,), jnp.float32, low / len(pieces), top_value / len(pieces))
        gain = gain * jnp.repeat(jnp.exp(heights), shape[position] // blocks).reshape((-1,) + (1,) * (len(shape) - 1 - position))
    return gain


def profile(number_of, total, limit, skew):
    loads = [(1 << 20) // math.isqrt(standing ** skew) + 1 for standing in range(2, number_of + 1)]
    surplus, holding = total - limit - (number_of - 1), [1] * (number_of - 1)
    while surplus > 0:
        movable = [i for i in range(number_of - 1) if holding[i] < limit]
        whole, left = sum([loads[i] for i in movable]), surplus
        for i in movable:
            addition = min(limit - holding[i], max(1, left * loads[i] // whole), surplus)
            holding[i] = holding[i] + addition
            surplus = surplus - addition
    return np.array([limit] + holding)


def uneven_parts(stream_key, count, total, reach, lean):
    if count == 2:
        one = jax.random.randint(stream_key, (), max(1, total - reach), min(reach, total - 1) + 1)
        return jnp.stack([one, total - one])
    lengths = jnp.asarray(profile(count, total, reach, lean), jnp.int32)
    pairs = (count - 1) // 2
    donor, taker = lengths[1:1 + 2 * pairs:2], lengths[2:2 + 2 * pairs:2]
    room = jnp.minimum(donor - 1, reach - taker)
    passed = jax.random.randint(jax.random.fold_in(stream_key, 1), (pairs,), 0, 1 << 20) % (room + 1)
    lengths = lengths.at[1:1 + 2 * pairs:2].set(donor - passed).at[2:2 + 2 * pairs:2].set(taker + passed)
    return lengths[jax.random.permutation(jax.random.fold_in(stream_key, 2), count)]


def scatter_about(stream_key, extent, scale, reach, cuts=(), held_as=jnp.bfloat16):
    values = scale * jax.random.normal(stream_key, extent, jnp.float32)
    if cuts:
        values = values * block_scale(stream_key, extent, cuts, -0.22, 0.18)
    return jnp.clip(values, -reach, reach).astype(held_as)


def setup_inputs(seed: int = 0) -> dict:
    streams_of = jax.random.split(jax.random.key(seed), 11)
    hidden_sel = scatter_about(streams_of[0], (NBLK * SEL, D), 1.0, 6.0, ((0, 32), (1, 8)))
    w_query = scatter_about(streams_of[1], (D, KV * HG * HD), D ** -0.5, 0.0625, ((1, 8),))
    w_key = scatter_about(streams_of[2], (D, KV * HD), D ** -0.5, 0.0625, ((1, 8),))
    w_value = scatter_about(streams_of[3], (D, KV * HD), D ** -0.5, 0.0625, ((1, 8),))
    key_cache = draw_key_cache(jax.random.fold_in(streams_of[10], 71), 0)
    value_cache = scatter_about(streams_of[5], (NBLK * SPAN, KV * HD), 1.0, 6.0, ((0, 32), (1, 8)))
    span_count = uneven_parts(streams_of[6], R, R * MAXCH // 2, MAXCH, 1).astype(jnp.int32)
    span_key = jax.vmap(lambda own: jax.random.permutation(own, MAXCH))(jax.random.split(streams_of[7], R)).reshape((R, MAXCH)).astype(jnp.int32)
    cache_offset = touch_ends(jax.random.randint(streams_of[8], (NBLK,), 0, MAXCH * SPAN), jax.random.fold_in(streams_of[8], 1), 0, (MAXCH * SPAN) - 1).astype(jnp.int32)
    sel_index = draw_sel_index(jax.random.fold_in(streams_of[10], 71), 0)
    return {"hidden_sel": hidden_sel, "w_query": w_query, "w_key": w_key, "w_value": w_value, "key_cache": key_cache, "value_cache": value_cache, "span_count": span_count, "span_key": span_key, "cache_offset": cache_offset, "sel_index": sel_index}


rope_base = 5000000.0
masked_score = -1.0e30


def rotate(values, angle):
    half = values.shape[-1] // 2
    first = values[..., :half]
    second = values[..., half:]
    cosine = jnp.cos(angle)
    sine = jnp.sin(angle)
    return jnp.concatenate([first * cosine - second * sine, second * cosine + first * sine], axis=-1)


def frequencies(width):
    return rope_base ** (-(jnp.arange(width // 2, dtype=jnp.float32) * 2.0) / width)


def span_ranks(span_count, span_key):
    column = jnp.arange(MAXCH, dtype=jnp.int32)
    filled = column[None, :] < span_count[:, None]
    earlier = span_key[:, :, None] < span_key[:, None, :]
    ranks = jnp.sum((earlier & filled[:, :, None]).astype(jnp.int32), axis=1, dtype=jnp.int32)
    return filled.T.reshape(-1), ranks.T.reshape(-1)


def reference(hidden_sel, w_query, w_key, w_value, key_cache, value_cache, span_count, span_key, cache_offset, sel_index):
    filled, ranks = span_ranks(span_count, span_key)
    freq = frequencies(HD)
    new_pos = ranks[:, None] * SPAN + sel_index
    angle = new_pos.astype(jnp.float32)[:, :, None] * freq
    query = jnp.dot(hidden_sel, w_query, preferred_element_type=jnp.float32).reshape(NBLK, SEL, KV, HG, HD)
    query = rotate(query, angle[:, :, None, None, :]).astype(jnp.bfloat16)
    new_key = jnp.dot(hidden_sel, w_key, preferred_element_type=jnp.float32).reshape(NBLK, SEL, KV, HD)
    new_key = rotate(new_key, angle[:, :, None, :]).astype(jnp.bfloat16)
    new_value = jnp.dot(hidden_sel, w_value, preferred_element_type=jnp.float32).astype(jnp.bfloat16).reshape(NBLK, SEL, KV, HD)
    delta = ranks * SPAN - cache_offset
    angle_delta = delta.astype(jnp.float32)[:, None, None, None] * freq
    joined_key = rotate(key_cache.reshape(NBLK, SPAN, KV, HD).astype(jnp.float32), angle_delta).astype(jnp.bfloat16)
    slot_ids = jnp.broadcast_to(jnp.arange(NBLK, dtype=jnp.int32)[:, None], (NBLK, SEL))
    joined_key = joined_key.at[slot_ids, sel_index].set(new_key)
    joined_value = value_cache.reshape(NBLK, SPAN, KV, HD).at[slot_ids, sel_index].set(new_value)
    scale = 1.0 / (HD ** 0.5)
    column = jnp.arange(SPAN, dtype=jnp.int32)

    def compute_slot(slot):
        request = slot % R
        key_slots = request + R * jnp.arange(MAXCH, dtype=jnp.int32)
        keys = joined_key[key_slots].reshape(MAXCH * SPAN, KV, HD).astype(jnp.float32)
        vals = joined_value[key_slots].reshape(MAXCH * SPAN, KV, HD).astype(jnp.float32)
        key_pos = (ranks[key_slots][:, None] * SPAN + column[None, :]).reshape(-1)
        key_live = jnp.repeat(filled[key_slots], SPAN)
        q_pos = new_pos[slot]
        scores = jnp.einsum("shgd,khd->hsgk", query[slot].astype(jnp.float32), keys)
        allowed = key_live[None, None, None, :] & (key_pos[None, None, None, :] <= q_pos[None, :, None, None])
        scores = jnp.where(allowed, scores * scale, masked_score)
        top = jnp.max(scores, axis=-1, keepdims=True)
        weight = jnp.exp(scores - top)
        total = jnp.sum(weight, axis=-1)
        mixed = jnp.einsum("hsgk,khd->shgd", weight.astype(jnp.bfloat16).astype(jnp.float32), vals)
        mixed = mixed / jnp.transpose(total, (1, 0, 2))[..., None]
        return mixed.astype(jnp.bfloat16)

    def one_slot(slot):
        return lax.cond(filled[slot], compute_slot, lambda s: jnp.zeros((SEL, KV, HG, HD), jnp.bfloat16), slot)

    result = lax.map(one_slot, jnp.arange(NBLK, dtype=jnp.int32))
    return result.reshape(NBLK * SEL, KV * HG * HD)
```

```python
import math

import jax
import jax.numpy as jnp
from jax import lax
from jax.experimental import pallas as pl
from jax.experimental.pallas import tpu as pltpu
from jax.sharding import Mesh, PartitionSpec as P

HD = 128
HG = 4
R = 8
MAXCH = 8
SPAN = 1024
SEL = 128
SLOTS = 2
ROWS = SLOTS * SEL
QW = HG * HD
PACK = SEL + 16
DK = 896

rope_base = 5000000.0
low = -1.0e30
SCALE2 = math.log2(math.e) / math.sqrt(HD)

AXES = ("zh", "yh", "yp", "c", "zl", "x")


def px(v, s):
    return lax.ppermute(v, "x", [(i, (i + s) % 4) for i in range(4)])


def pz(v):
    return lax.ppermute(v, "zl", [(0, 1), (1, 0)])


def py(v):
    return lax.ppermute(v, "yh", [(0, 1), (1, 0)])


def ph(v, s):
    return lax.ppermute(v, "zh", [(i, (i + s) % 4) for i in range(4)])


def span_ranks(span_count, span_key):
    column = jnp.arange(MAXCH, dtype=jnp.int32)
    filled = column[None, :] < span_count[:, None]
    earlier = span_key[:, :, None] < span_key[:, None, :]
    ranks = jnp.sum((earlier & filled[:, :, None]).astype(jnp.int32), axis=1, dtype=jnp.int32)
    return filled.T.reshape(-1), ranks.T.reshape(-1)


def tables(position):
    freq = rope_base ** (-(jnp.arange(HD // 2, dtype=jnp.float32) * 2.0) / HD)
    angle = position.astype(jnp.float32)[:, None] * freq
    cosine, sine = jnp.cos(angle), jnp.sin(angle)
    return jnp.concatenate([cosine, cosine], -1), jnp.concatenate([-sine, sine], -1)


def turned(v, cosine, sine):
    return v * cosine + pltpu.roll(v, HD // 2, 1) * sine


def project_kernel(idx_ref, *refs):
    pieces = refs[:8]
    wq, wk, wv, cos_ref, sin_ref, q_ref, n_ref, acc_q, acc_n = refs[8:]
    k = pl.program_id(0)
    wn = jnp.concatenate([wk[...], wv[...]], axis=1)
    for i in range(8):

        @pl.when(k == i)
        def _(i=i):
            a = pieces[i][...]
            dq = jnp.dot(a, wq[...], preferred_element_type=jnp.float32)
            dn = jnp.dot(a, wn, preferred_element_type=jnp.float32)
            if i == 0:
                acc_q[...] = dq
                acc_n[...] = dn
            else:
                acc_q[...] += dq
                acc_n[...] += dn

    @pl.when(k == 7)
    def _():
        cosine, sine = cos_ref[...], sin_ref[...]
        for g in range(HG):
            at = slice(g * HD, (g + 1) * HD)
            q_ref[:, at] = turned(acc_q[:, at], cosine, sine).astype(jnp.bfloat16)
        n_ref[:ROWS, :] = turned(acc_n[:, :HD], cosine, sine).astype(jnp.bfloat16)
        n_ref[ROWS:, :] = acc_n[:, HD:].astype(jnp.bfloat16)


def project(idx, pieces, w_query, w_key, w_value, cosine, sine):
    full = lambda shape: pl.BlockSpec(shape, lambda k, idx: (0, 0))
    part = lambda width: pl.BlockSpec((DK, width), lambda k, idx: (idx[k], 0))
    return pl.pallas_call(
        project_kernel,
        out_shape=(
            jax.ShapeDtypeStruct((ROWS, QW), jnp.bfloat16),
            jax.ShapeDtypeStruct((2 * ROWS, HD), jnp.bfloat16),
        ),
        grid_spec=pltpu.PrefetchScalarGridSpec(
            num_scalar_prefetch=1,
            grid=(8,),
            in_specs=[full((ROWS, DK))] * 8
            + [part(QW), part(HD), part(HD), full((ROWS, HD)), full((ROWS, HD))],
            out_specs=(full((ROWS, QW)), full((2 * ROWS, HD))),
            scratch_shapes=[
                pltpu.VMEM((ROWS, QW), jnp.float32),
                pltpu.VMEM((ROWS, 2 * HD), jnp.float32),
            ],
        ),
        compiler_params=pltpu.CompilerParams(vmem_limit_bytes=32 << 20),
        cost_estimate=pl.CostEstimate(
            flops=2 * ROWS * 7168 * 768, bytes_accessed=15 << 20, transcendentals=0
        ),
        name="project",
    )(idx, *pieces, w_query, w_key, w_value, cosine, sine)


def attend_block(q, keys, vals, limit, m_ref, l_ref, acc_ref):
    s = lax.dot_general(q, keys, (((1,), (1,)), ((), ())), preferred_element_type=jnp.float32)
    if limit is not None:
        col = lax.broadcasted_iota(jnp.int32, s.shape, 1)
        s = jnp.where(col <= limit, s, low)
    old = m_ref[...]
    new = jnp.maximum(old, jnp.max(s, axis=1, keepdims=True))
    factor = jnp.exp2((old - new) * SCALE2)
    weight = jnp.exp2((s - new) * SCALE2)
    l_ref[...] = l_ref[...] * factor + jnp.sum(weight, axis=1, keepdims=True)
    acc_ref[...] = acc_ref[...] * factor + jnp.dot(
        weight.astype(jnp.bfloat16), vals, preferred_element_type=jnp.float32
    )
    m_ref[...] = new


def attend_source(own, r, q_ref, jk_ref, jv_ref, valid_ref, sel_ref, o_ref, m_ref, l_ref, acc_ref):
    m_ref[...] = jnp.full_like(m_ref, low)
    l_ref[...] = jnp.zeros_like(l_ref)
    acc_ref[...] = jnp.zeros_like(acc_ref)
    row = pl.multiple_of(r * SEL, SEL)

    def queries():
        q = q_ref[pl.ds(row, SEL), :]
        return jnp.concatenate([q[:, g * HD : (g + 1) * HD] for g in range(HG)], axis=0)

    for sp in range(2):

        @pl.when(valid_ref[r * 2 + sp] != 0)
        def _(sp=sp):
            limit = None
            if own and sp == 0:
                sel = sel_ref[pl.ds(row, SEL), :]
                limit = jnp.concatenate([sel] * HG, axis=0)
            attend_block(
                queries(), jk_ref[r * 2 + sp], jv_ref[r * 2 + sp], limit, m_ref, l_ref, acc_ref
            )

    l = l_ref[...]
    some = l > 0.0
    mixed = acc_ref[...] / jnp.where(some, l, 1.0)
    lse = jnp.where(some, m_ref[...] * SCALE2 + jnp.log2(jnp.where(some, l, 1.0)), low)
    lane = lax.broadcasted_iota(jnp.int32, (SEL, HD), 1)
    stat = jnp.zeros((SEL, HD), jnp.float32)
    for g in range(HG):
        o_ref[r, :SEL, g * HD : (g + 1) * HD] = mixed[g * SEL : (g + 1) * SEL].astype(jnp.bfloat16)
        rest = lse[g * SEL : (g + 1) * SEL]
        for k in range(3):
            part = rest.astype(jnp.bfloat16).astype(jnp.float32)
            stat = jnp.where(lane == k * HG + g, part, stat)
            rest = rest - part
    o_ref[r, SEL:, :HD] = stat.T[:16].astype(jnp.bfloat16)
    o_ref[r, SEL:, HD:] = jnp.zeros((16, QW - HD), jnp.bfloat16)


def own_kernel(
    valid_ref, q_ref, k0, v0, k1, v1, n0, n1, selr_ref, rot_ref, sel_ref,
    jk_ref, jv_ref, o_ref, m_ref, l_ref, acc_ref,
):
    def request(r, _):
        for sp, (kr, vr, nr) in enumerate(((k0, v0, n0), (k1, v1, n1))):
            base = pl.multiple_of(r * SPAN, SPAN)
            fresh = pl.multiple_of(r * SEL, SEL)
            raw = kr[pl.ds(base, SPAN), :].astype(jnp.float32)
            cached = turned(raw, rot_ref[r, sp : sp + 1, :], rot_ref[r, sp + 2 : sp + 3, :])
            at = lax.broadcasted_iota(jnp.int32, (SPAN, SEL), 0)
            pick = (at == selr_ref[r, sp : sp + 1, :]).astype(jnp.float32).astype(jnp.bfloat16)
            hit = jnp.dot(pick, jnp.ones((SEL, HD), jnp.bfloat16), preferred_element_type=jnp.float32)
            hit = hit > 0.5
            put_k = jnp.dot(pick, nr[pl.ds(fresh, SEL), :], preferred_element_type=jnp.float32)
            put_v = jnp.dot(
                pick, nr[pl.ds(ROWS + fresh, SEL), :], preferred_element_type=jnp.float32
            )
            jk_ref[r * 2 + sp] = jnp.where(hit, put_k, cached).astype(jnp.bfloat16)
            vals = vr[pl.ds(base, SPAN), :].astype(jnp.float32)
            jv_ref[r * 2 + sp] = jnp.where(hit, put_v, vals).astype(jnp.bfloat16)
        attend_source(
            True, r, q_ref, jk_ref, jv_ref, valid_ref, sel_ref, o_ref, m_ref, l_ref, acc_ref
        )
        return 0

    lax.fori_loop(0, SLOTS, request, 0)


def other_kernel(valid_ref, q_ref, jk_ref, jv_ref, o_ref, m_ref, l_ref, acc_ref):
    def request(r, _):
        attend_source(
            False, r, q_ref, jk_ref, jv_ref, valid_ref, None, o_ref, m_ref, l_ref, acc_ref
        )
        return 0

    lax.fori_loop(0, SLOTS, request, 0)


vmem = pl.BlockSpec(memory_space=pltpu.VMEM)
smem = pl.BlockSpec(memory_space=pltpu.SMEM)
joined_shape = jax.ShapeDtypeStruct((SLOTS * 2, SPAN, HD), jnp.bfloat16)
packed_shape = jax.ShapeDtypeStruct((SLOTS, PACK, QW), jnp.bfloat16)
state_scratch = [
    pltpu.VMEM((HG * SEL, 1), jnp.float32),
    pltpu.VMEM((HG * SEL, 1), jnp.float32),
    pltpu.VMEM((HG * SEL, HD), jnp.float32),
]
attend_cost = pl.CostEstimate(
    flops=4 * SLOTS * 512 * 1024 * HD * 2, bytes_accessed=3 << 20, transcendentals=2 << 20
)


def attend_own(*args):
    return pl.pallas_call(
        own_kernel,
        out_shape=(joined_shape, joined_shape, packed_shape),
        in_specs=[smem] + [vmem] * 10,
        out_specs=(vmem, vmem, vmem),
        scratch_shapes=state_scratch,
        compiler_params=pltpu.CompilerParams(vmem_limit_bytes=32 << 20),
        cost_estimate=attend_cost,
        name="attend_own",
    )(*args)


def attend_other(*args):
    return pl.pallas_call(
        other_kernel,
        out_shape=packed_shape,
        in_specs=[smem] + [vmem] * 3,
        out_specs=vmem,
        scratch_shapes=state_scratch,
        compiler_params=pltpu.CompilerParams(vmem_limit_bytes=32 << 20),
        cost_estimate=attend_cost,
        name="attend_other",
    )(*args)


def merge_kernel(a, b, c, d, o_ref):
    parts = (a, b, c, d)
    for r in range(SLOTS):
        lse = []
        for p in parts:
            stat = p[r, SEL:, :HD].astype(jnp.float32)
            full = stat[0:4] + stat[4:8] + stat[8:12]
            lse.append(jnp.concatenate([full, jnp.zeros((HD - 4, SEL), jnp.float32)], axis=0).T)
        top = jnp.maximum(jnp.maximum(lse[0], lse[1]), jnp.maximum(lse[2], lse[3]))
        weight = [jnp.exp2(v - top) for v in lse]
        total = weight[0] + weight[1] + weight[2] + weight[3]
        weight = [w / total for w in weight]
        for g in range(HG):
            at = slice(g * HD, (g + 1) * HD)
            mixed = jnp.zeros((SEL, HD), jnp.float32)
            for w, p in zip(weight, parts):
                mixed += w[:, g : g + 1] * p[r, :SEL, at].astype(jnp.float32)
            o_ref[r * SEL : (r + 1) * SEL, at] = mixed.astype(jnp.bfloat16)


def merge(*parts):
    return pl.pallas_call(
        merge_kernel,
        out_shape=jax.ShapeDtypeStruct((ROWS, QW), jnp.bfloat16),
        in_specs=[vmem] * 4,
        out_specs=vmem,
        compiler_params=pltpu.CompilerParams(vmem_limit_bytes=16 << 20),
        name="merge",
    )(*parts)


def shards(
    hidden, w_query, w_key, w_value, key_cache, value_cache,
    span_count, span_key, cache_offset, sel_index,
):
    zh, yh, yp, c = (lax.axis_index(a) for a in ("zh", "yh", "yp", "c"))
    zl, x = lax.axis_index("zl"), lax.axis_index("x")
    z = pz(hidden)
    k1, v1 = py(key_cache), py(value_cache)
    mine = jnp.concatenate(
        [sel_index, jnp.broadcast_to(cache_offset[:, None], (SLOTS, SEL))], axis=0
    )
    theirs = py(mine)
    right, left = px(hidden, 1), px(hidden, -1)
    zright, zleft = px(z, 1), px(z, -1)
    far, zfar = px(right, 1), px(zleft, -1)
    pieces = (hidden, z, right, left, zright, zleft, far, zfar)
    other = 1 - zl
    idx = jnp.stack(
        [
            zl * 4 + x,
            other * 4 + x,
            zl * 4 + (x + 3) % 4,
            zl * 4 + (x + 1) % 4,
            other * 4 + (x + 3) % 4,
            other * 4 + (x + 1) % 4,
            zl * 4 + (x + 2) % 4,
            other * 4 + (x + 2) % 4,
        ]
    ).astype(jnp.int32)

    filled_all, rank_all = span_ranks(span_count, span_key)

    def first_slot(h, half):
        return (((h * 2 + half) * 2 + yp) * 2 + c) * SLOTS

    def lookup(h, half):
        start = first_slot(h, half)
        return (
            lax.dynamic_slice_in_dim(filled_all, start, SLOTS),
            lax.dynamic_slice_in_dim(rank_all, start, SLOTS),
        )

    span_f, span_r = zip(lookup(zh, yh), lookup(zh, 1 - yh))

    def validity(shift):
        qf, qr = lookup((zh - shift) % 4, yh)
        table = [qf & kf & (kr <= qr) for kf, kr in zip(span_f, span_r)]
        return jnp.stack(table, axis=1).reshape(-1).astype(jnp.int32)

    position = (span_r[0][:, None] * SPAN + sel_index).reshape(-1)
    cosine, sine = tables(position)
    delta = jnp.stack(
        [span_r[0] * SPAN - cache_offset, span_r[1] * SPAN - theirs[SLOTS:, 0]], axis=1
    ).reshape(-1)
    turn_c, turn_s = tables(delta)
    rot = jnp.concatenate(
        [turn_c.reshape(SLOTS, 2, HD), turn_s.reshape(SLOTS, 2, HD)], axis=1
    )
    sel_rows = jnp.stack([sel_index, theirs[:SLOTS]], axis=1)

    query, fresh = project(idx, pieces, w_query, w_key, w_value, cosine, sine)
    fresh1 = py(fresh)
    sent = {s: ph(query, s) for s in (2, 1, 3)}
    jk, jv, part0 = attend_own(
        validity(0), query, key_cache, value_cache, k1, v1, fresh, fresh1,
        sel_rows, rot, sel_index.reshape(ROWS, 1),
    )
    back = [ph(attend_other(validity(s), sent[s], jk, jv), -s) for s in (1, 3, 2)]
    return merge(part0, *back)


def solution(mesh):
    split = Mesh(mesh.devices.reshape(4, 2, 2, 2, 2, 4), AXES)
    seq, tp = AXES[:4], AXES[4:]
    placed = (
        P(seq, tp),
        P(None, tp),
        P(None, tp),
        P(None, tp),
        P(seq, tp),
        P(seq, tp),
        P(),
        P(),
        P(seq),
        P(seq, None),
    )
    return jax.shard_map(
        shards, mesh=split, in_specs=placed, out_specs=P(seq, tp), check_vma=False
    )
```

```python
import functools
import math

import jax
import jax.numpy as jnp
from jax import lax
from jax.experimental import pallas as pl
from jax.experimental.pallas import tpu as pltpu
from jax.sharding import Mesh, PartitionSpec as P

HD = 128
HG = 4
R = 8
MAXCH = 8
SPAN = 1024
SEL = 128
SLOTS = 2
ROWS = SLOTS * SEL
QW = HG * HD
PACK = SEL + 16
DK = 896
PROJ = 56

rope_base = 5000000.0
low = -1.0e30
SCALE2 = math.log2(math.e) / math.sqrt(HD)

vmem = pl.BlockSpec(memory_space=pltpu.VMEM)
smem = pl.BlockSpec(memory_space=pltpu.SMEM)
hbm = pl.BlockSpec(memory_space=pltpu.HBM)
tiny = pl.CostEstimate(flops=1, bytes_accessed=1, transcendentals=0)
AXES = ("zh", "yh", "yp", "c", "zl", "x")


def px(v, s):
    return lax.ppermute(v, "x", [(i, (i + s) % 4) for i in range(4)])


def pz(v):
    return lax.ppermute(v, "zl", [(0, 1), (1, 0)])


def py(v):
    return lax.ppermute(v, "yh", [(0, 1), (1, 0)])


def ph(v, s):
    return lax.ppermute(v, "zh", [(i, (i + s) % 4) for i in range(4)])


def span_ranks(span_count, span_key):
    column = jnp.arange(MAXCH, dtype=jnp.int32)
    filled = column[None, :] < span_count[:, None]
    earlier = span_key[:, :, None] < span_key[:, None, :]
    ranks = jnp.sum((earlier & filled[:, :, None]).astype(jnp.int32), axis=1, dtype=jnp.int32)
    return filled.T.reshape(-1), ranks.T.reshape(-1)


def tables(position):
    freq = rope_base ** (-(jnp.arange(HD // 2, dtype=jnp.float32) * 2.0) / HD)
    angle = position.astype(jnp.float32)[:, None] * freq
    cosine, sine = jnp.cos(angle), jnp.sin(angle)
    return jnp.concatenate([cosine, cosine], -1), jnp.concatenate([-sine, sine], -1)


def turned(v, cosine, sine):
    return v * cosine + pltpu.roll(v, HD // 2, 1) * sine


def project_kernel(count, carried, last, idx_ref, *refs):
    refs = list(refs)
    pieces = [refs.pop(0) for _ in range(count)]
    sources = [refs.pop(0) for _ in range(3)]
    acc_ref = refs.pop(0) if carried else None
    if last:
        cos_ref, sin_ref, q_ref, n_ref = (refs.pop(0) for _ in range(4))
    else:
        out_ref = refs.pop(0)
    held, weight, sem = refs
    widths = (QW, HD, HD)

    def copies(i):
        at = pl.ds(pl.multiple_of(idx_ref[i] * DK, DK), DK)
        start = 0
        for j, (w, width) in enumerate(zip(sources, widths)):
            to = weight.at[i, :, start : start + width]
            yield pltpu.make_async_copy(w.at[at, :], to, sem.at[i, j])
            start += width

    for i in range(count):
        for copy in copies(i):
            copy.start()
    for i in range(count):
        held[i] = pieces[i][...]

    def add(i, acc):
        for copy in copies(i):
            copy.wait()
        return acc + jnp.dot(held[i], weight[i], preferred_element_type=jnp.float32)

    begin = acc_ref[...] if carried else jnp.zeros((SEL, QW + 2 * HD), jnp.float32)
    acc = lax.fori_loop(0, count, add, begin)
    if not last:
        out_ref[...] = acc
        return
    cosine, sine = cos_ref[...], sin_ref[...]
    for g in range(HG):
        at = slice(g * HD, (g + 1) * HD)
        q_ref[:, at] = turned(acc[:, at], cosine, sine).astype(jnp.bfloat16)
    n_ref[:SEL, :] = turned(acc[:, QW : QW + HD], cosine, sine).astype(jnp.bfloat16)
    n_ref[SEL:, :] = acc[:, QW + HD :].astype(jnp.bfloat16)


def project(idx, pieces, weights, acc=None, rot=None):
    if rot is None:
        out = jax.ShapeDtypeStruct((SEL, QW + 2 * HD), jnp.float32)
    else:
        out = (
            jax.ShapeDtypeStruct((SEL, QW), jnp.bfloat16),
            jax.ShapeDtypeStruct((2 * SEL, HD), jnp.bfloat16),
        )
    extra = ([] if acc is None else [acc]) + ([] if rot is None else list(rot))
    n = len(pieces)
    return pl.pallas_call(
        functools.partial(project_kernel, n, acc is not None, rot is not None),
        out_shape=out,
        in_specs=[smem] + [vmem] * n + [hbm] * 3 + [vmem] * len(extra),
        out_specs=vmem if rot is None else (vmem, vmem),
        scratch_shapes=[
            pltpu.VMEM((n, SEL, DK), jnp.bfloat16),
            pltpu.VMEM((n, DK, QW + 2 * HD), jnp.bfloat16),
            pltpu.SemaphoreType.DMA((n, 3)),
        ],
        compiler_params=pltpu.CompilerParams(vmem_limit_bytes=PROJ << 20),
        cost_estimate=tiny,
        name="project",
    )(idx, *pieces, *weights, *extra)


def attend_block(at, q_ref, keys, vals, limit, m_ref, l_ref, acc_ref):
    s = lax.dot_general(
        q_ref[at, :], keys, (((1,), (1,)), ((), ())), preferred_element_type=jnp.float32
    )
    if limit is not None:
        col = lax.broadcasted_iota(jnp.int32, s.shape, 1)
        s = jnp.where(col <= limit, s, low)
    old = m_ref[at, :]
    new = jnp.maximum(old, jnp.max(s, axis=1, keepdims=True))
    factor = jnp.exp2((old - new) * SCALE2)
    weight = jnp.exp2((s - new) * SCALE2)
    l_ref[at, :] = l_ref[at, :] * factor + jnp.sum(weight, axis=1, keepdims=True)
    acc_ref[at, :] = acc_ref[at, :] * factor + jnp.dot(
        weight.astype(jnp.bfloat16), vals, preferred_element_type=jnp.float32
    )
    m_ref[at, :] = new


def attend_source(
    q_ref, jk_ref, jv_ref, valid_ref, sel, o_ref, m_ref, l_ref, acc_ref, rows_ref, limit_ref=None
):
    m_ref[...] = jnp.full_like(m_ref, low)
    l_ref[...] = jnp.zeros_like(l_ref)
    acc_ref[...] = jnp.zeros_like(acc_ref)

    for g in range(HG):
        rows_ref[g * SEL : (g + 1) * SEL, :] = q_ref[:, g * HD : (g + 1) * HD]
    if sel is not None:
        column = jnp.broadcast_to(sel.astype(jnp.float32), (SEL, SEL)).T[:, :1]
        limit_ref[...] = jnp.concatenate([column.astype(jnp.int32)] * HG, axis=0)

    def span(step, _):
        sp = step // 2

        @pl.when(valid_ref[sp] != 0)
        def _():
            at = pl.ds(pl.multiple_of((step % 2) * 2 * SEL, 2 * SEL), 2 * SEL)
            limit = None if sel is None else jnp.where(sp == 0, limit_ref[at, :], SPAN)
            attend_block(at, rows_ref, jk_ref[sp], jv_ref[sp], limit, m_ref, l_ref, acc_ref)

        return 0

    lax.fori_loop(0, 4, span, 0)
    l = l_ref[...]
    some = l > 0.0
    mixed = acc_ref[...] / jnp.where(some, l, 1.0)
    lse = jnp.where(some, m_ref[...] * SCALE2 + jnp.log2(jnp.where(some, l, 1.0)), low)
    lane = lax.broadcasted_iota(jnp.int32, (SEL, HD), 1)
    stat = jnp.zeros((SEL, HD), jnp.float32)
    for g in range(HG):
        o_ref[:SEL, g * HD : (g + 1) * HD] = mixed[g * SEL : (g + 1) * SEL].astype(jnp.bfloat16)
        rest = lse[g * SEL : (g + 1) * SEL]
        for k in range(3):
            part = rest.astype(jnp.bfloat16).astype(jnp.float32)
            stat = jnp.where(lane == k * HG + g, part, stat)
            rest = rest - part
    o_ref[SEL:, :HD] = stat.T[:16].astype(jnp.bfloat16)
    o_ref[SEL:, HD:] = jnp.zeros((16, QW - HD), jnp.bfloat16)


def own_kernel(
    r, valid_ref, q_ref, k0, v0, kv1, n0, n1, selr_ref, rot_ref,
    jk_ref, jv_ref, o_ref, m_ref, l_ref, acc_ref, rows_ref, limit_ref,
):
    base = pl.ds(r * SPAN, SPAN)
    for sp in range(2):
        if sp == 0:
            keys, vals, nr = k0[base, :], v0[base, :], n0
        else:
            keys, vals, nr = kv1[:SPAN, :], kv1[SPAN:, :], n1
        cached = turned(
            keys.astype(jnp.float32), rot_ref[r, sp : sp + 1, :], rot_ref[r, sp + 2 : sp + 3, :]
        )
        at = lax.broadcasted_iota(jnp.int32, (SPAN, SEL), 0)
        pick = (at == selr_ref[r, sp : sp + 1, :]).astype(jnp.float32).astype(jnp.bfloat16)
        hit = jnp.dot(pick, jnp.ones((SEL, HD), jnp.bfloat16), preferred_element_type=jnp.float32)
        hit = hit > 0.5
        put_k = jnp.dot(pick, nr[:SEL, :], preferred_element_type=jnp.float32)
        put_v = jnp.dot(pick, nr[SEL:, :], preferred_element_type=jnp.float32)
        jk_ref[sp] = jnp.where(hit, put_k, cached).astype(jnp.bfloat16)
        jv_ref[sp] = jnp.where(hit, put_v, vals.astype(jnp.float32)).astype(jnp.bfloat16)
    sel = selr_ref[r, 0:1, :]
    attend_source(
        q_ref, jk_ref, jv_ref, valid_ref, sel, o_ref, m_ref, l_ref, acc_ref, rows_ref, limit_ref
    )


def other_kernel(valid_ref, q_ref, jk_ref, jv_ref, o_ref, m_ref, l_ref, acc_ref, rows_ref):
    attend_source(q_ref, jk_ref, jv_ref, valid_ref, None, o_ref, m_ref, l_ref, acc_ref, rows_ref)


joined_shape = jax.ShapeDtypeStruct((2, SPAN, HD), jnp.bfloat16)
packed_shape = jax.ShapeDtypeStruct((PACK, QW), jnp.bfloat16)
state_scratch = [
    pltpu.VMEM((HG * SEL, 1), jnp.float32),
    pltpu.VMEM((HG * SEL, 1), jnp.float32),
    pltpu.VMEM((HG * SEL, HD), jnp.float32),
    pltpu.VMEM((HG * SEL, HD), jnp.bfloat16),
]
def attend_own(r, *args):
    return pl.pallas_call(
        functools.partial(own_kernel, r),
        out_shape=(joined_shape, joined_shape, packed_shape),
        in_specs=[smem] + [vmem] * 8,
        out_specs=(vmem, vmem, vmem),
        scratch_shapes=state_scratch + [pltpu.VMEM((HG * SEL, 1), jnp.int32)],
        compiler_params=pltpu.CompilerParams(vmem_limit_bytes=20 << 20),
        cost_estimate=tiny,
        name="attend_own",
    )(*args)


def attend_other(*args):
    return pl.pallas_call(
        other_kernel,
        out_shape=packed_shape,
        in_specs=[smem] + [vmem] * 3,
        out_specs=vmem,
        scratch_shapes=state_scratch,
        compiler_params=pltpu.CompilerParams(vmem_limit_bytes=20 << 20),
        cost_estimate=tiny,
        name="attend_other",
    )(*args)


def merge_parts(parts):
    lse = []
    for p in parts:
        stat = p[SEL:, :HD].astype(jnp.float32)
        full = stat[0:4] + stat[4:8] + stat[8:12]
        lse.append(jnp.concatenate([full, jnp.zeros((HD - 4, SEL), jnp.float32)], axis=0).T)
    top = jnp.maximum(jnp.maximum(lse[0], lse[1]), jnp.maximum(lse[2], lse[3]))
    weight = [jnp.exp2(v - top) for v in lse]
    total = weight[0] + weight[1] + weight[2] + weight[3]
    weight = [w / total for w in weight]
    for g in range(HG):
        at = slice(g * HD, (g + 1) * HD)
        mixed = jnp.zeros((SEL, HD), jnp.float32)
        for w, p in zip(weight, parts):
            mixed += w[:, g : g + 1] * p[:SEL, at].astype(jnp.float32)
        yield at, mixed.astype(jnp.bfloat16)


def merge_kernel(*refs):
    o_ref = refs[-1]
    start = 0
    if len(refs) == 6:
        start = SEL
        o_ref[:SEL, :] = refs[4][...]
    for at, value in merge_parts(refs[:4]):
        o_ref[start : start + SEL, at] = value


def merge(*parts):
    return pl.pallas_call(
        merge_kernel,
        out_shape=jax.ShapeDtypeStruct((SEL * (len(parts) - 3), QW), jnp.bfloat16),
        in_specs=[vmem] * len(parts),
        out_specs=vmem,
        compiler_params=pltpu.CompilerParams(vmem_limit_bytes=8 << 20),
        cost_estimate=tiny,
        name="merge",
    )(*parts)


def after(value, *others):
    return lax.optimization_barrier((value, *others))[0]


def shards(
    hidden, w_query, w_key, w_value, key_cache, value_cache,
    span_count, span_key, cache_offset, sel_index,
):
    zh, yh, yp, c = (lax.axis_index(a) for a in ("zh", "yh", "yp", "c"))
    zl, x = lax.axis_index("zl"), lax.axis_index("x")
    weights = (w_query, w_key, w_value)
    slot = lambda v, r, n: v[r * n : (r + 1) * n]
    gathered, cached = [], []
    free_plus = free_minus = free_y = None
    for r in range(SLOTS):
        h = slot(hidden, r, SEL)
        kv = jnp.concatenate([slot(key_cache, r, SPAN), slot(value_cache, r, SPAN)], axis=0)
        if r:
            kv1 = py(after(kv, free_y))
            right, left = px(after(h, free_plus), 1), px(after(h, free_minus), -1)
        else:
            kv1 = py(kv)
            right, left = px(h, 1), px(h, -1)
        z = pz(h)
        far = px(right, 1)
        zleft = px(z, -1)
        zright = px(after(z, left), 1)
        zfar = px(zleft, -1)
        free_plus, free_minus, free_y = far, zleft, kv1
        gathered.append(((h, z, right, left), (far, zleft, zright, zfar)))
        cached.append(kv1)
    mine = jnp.concatenate(
        [sel_index, jnp.broadcast_to(cache_offset[:, None], (SLOTS, SEL))], axis=0
    )
    theirs = py(mine)
    other = 1 - zl
    near_idx = jnp.stack(
        [zl * 4 + x, other * 4 + x, zl * 4 + (x + 3) % 4, zl * 4 + (x + 1) % 4]
    ).astype(jnp.int32)
    far_idx = jnp.stack(
        [
            zl * 4 + (x + 2) % 4,
            other * 4 + (x + 1) % 4,
            other * 4 + (x + 3) % 4,
            other * 4 + (x + 2) % 4,
        ]
    ).astype(jnp.int32)

    filled_all, rank_all = span_ranks(span_count, span_key)

    def lookup(h, half):
        start = (((h * 2 + half) * 2 + yp) * 2 + c) * SLOTS
        return (
            lax.dynamic_slice_in_dim(filled_all, start, SLOTS),
            lax.dynamic_slice_in_dim(rank_all, start, SLOTS),
        )

    span_f, span_r = zip(lookup(zh, yh), lookup(zh, 1 - yh))

    def validity(shift):
        qf, qr = lookup((zh - shift) % 4, yh)
        table = [qf & kf & (kr <= qr) for kf, kr in zip(span_f, span_r)]
        return jnp.stack(table, axis=1).astype(jnp.int32)

    position = (span_r[0][:, None] * SPAN + sel_index).reshape(-1)
    cosine, sine = tables(position)
    delta = jnp.stack(
        [span_r[0] * SPAN - cache_offset, span_r[1] * SPAN - theirs[SLOTS:, 0]], axis=1
    ).reshape(-1)
    turn_c, turn_s = tables(delta)
    rot = jnp.concatenate(
        [turn_c.reshape(SLOTS, 2, HD), turn_s.reshape(SLOTS, 2, HD)], axis=1
    )
    sel_rows = jnp.stack([sel_index, theirs[:SLOTS]], axis=1)
    valid = [validity(s) for s in range(4)]

    done = None
    for r in range(SLOTS):
        near, distant = gathered[r]
        partial = project(near_idx, near, weights)
        at = slice(r * SEL, (r + 1) * SEL)
        partial = after(partial, cached[r])
        query, fresh = project(far_idx, distant, weights, partial, (cosine[at], sine[at]))
        fresh1 = py(fresh)
        sent = {s: ph(query, s) for s in (2, 1, 3)}
        jk, jv, part0 = attend_own(
            r, valid[0][r], query, key_cache, value_cache, cached[r], fresh, fresh1, sel_rows, rot
        )
        back = [ph(attend_other(valid[s][r], sent[s], jk, jv), -s) for s in (1, 3, 2)]
        done = merge(part0, *back, *([] if done is None else [done]))
    return done


def solution(mesh):
    split = Mesh(mesh.devices.reshape(4, 2, 2, 2, 2, 4), AXES)
    seq, tp = AXES[:4], AXES[4:]
    placed = (
        P(seq, tp),
        P(None, tp),
        P(None, tp),
        P(None, tp),
        P(seq, tp),
        P(seq, tp),
        P(),
        P(),
        P(seq),
        P(seq, None),
    )
    return jax.shard_map(
        shards, mesh=split, in_specs=placed, out_specs=P(seq, tp), check_vma=False
    )
```

```python
import functools
import math

import jax
import jax.numpy as jnp
from jax import lax
from jax.experimental import pallas as pl
from jax.experimental.pallas import tpu as pltpu
from jax.sharding import Mesh, PartitionSpec as P

HD = 128
HG = 4
R = 8
MAXCH = 8
SPAN = 1024
SEL = 128
SLOTS = 2
ROWS = SLOTS * SEL
QW = HG * HD
PACK = SEL + 16
DK = 896
PROJ = 56

rope_base = 5000000.0
low = -1.0e30
SCALE2 = math.log2(math.e) / math.sqrt(HD)

vmem = pl.BlockSpec(memory_space=pltpu.VMEM)
smem = pl.BlockSpec(memory_space=pltpu.SMEM)
hbm = pl.BlockSpec(memory_space=pltpu.HBM)
tiny = pl.CostEstimate(flops=1, bytes_accessed=1, transcendentals=0)
AXES = ("zh", "yh", "yp", "c", "zl", "x")


def px(v, s):
    return lax.ppermute(v, "x", [(i, (i + s) % 4) for i in range(4)])


def pz(v):
    return lax.ppermute(v, "zl", [(0, 1), (1, 0)])


def py(v):
    return lax.ppermute(v, "yh", [(0, 1), (1, 0)])


def ph(v, s):
    return lax.ppermute(v, "zh", [(i, (i + s) % 4) for i in range(4)])


def span_ranks(span_count, span_key):
    column = jnp.arange(MAXCH, dtype=jnp.int32)
    filled = column[None, :] < span_count[:, None]
    earlier = span_key[:, :, None] < span_key[:, None, :]
    ranks = jnp.sum((earlier & filled[:, :, None]).astype(jnp.int32), axis=1, dtype=jnp.int32)
    return filled.T.reshape(-1), ranks.T.reshape(-1)


def tables(position):
    freq = rope_base ** (-(jnp.arange(HD // 2, dtype=jnp.float32) * 2.0) / HD)
    angle = position.astype(jnp.float32)[:, None] * freq
    cosine, sine = jnp.cos(angle), jnp.sin(angle)
    return jnp.concatenate([cosine, cosine], -1), jnp.concatenate([-sine, sine], -1)


def turned(v, cosine, sine):
    return v * cosine + pltpu.roll(v, HD // 2, 1) * sine


def project_kernel(count, carried, last, idx_ref, *refs):
    refs = list(refs)
    pieces = [refs.pop(0) for _ in range(count)]
    sources = [refs.pop(0) for _ in range(3)]
    acc_ref = refs.pop(0) if carried else None
    if last:
        cos_ref, sin_ref, q_ref, n_ref = (refs.pop(0) for _ in range(4))
    else:
        out_ref = refs.pop(0)
    held, weight, sem = refs
    widths = (QW, HD, HD)

    def copies(i):
        at = pl.ds(pl.multiple_of(idx_ref[i] * DK, DK), DK)
        start = 0
        for j, (w, width) in enumerate(zip(sources, widths)):
            to = weight.at[i, :, start : start + width]
            yield pltpu.make_async_copy(w.at[at, :], to, sem.at[i, j])
            start += width

    for i in range(count):
        for copy in copies(i):
            copy.start()
    for i in range(count):
        held[i] = pieces[i][...]

    def add(i, acc):
        for copy in copies(i):
            copy.wait()
        return acc + jnp.dot(held[i], weight[i], preferred_element_type=jnp.float32)

    begin = acc_ref[...] if carried else jnp.zeros((ROWS, QW + 2 * HD), jnp.float32)
    acc = lax.fori_loop(0, count, add, begin)
    if not last:
        out_ref[...] = acc
        return
    cosine, sine = cos_ref[...], sin_ref[...]
    for g in range(HG):
        at = slice(g * HD, (g + 1) * HD)
        q_ref[:, at] = turned(acc[:, at], cosine, sine).astype(jnp.bfloat16)
    n_ref[:ROWS, :] = turned(acc[:, QW : QW + HD], cosine, sine).astype(jnp.bfloat16)
    n_ref[ROWS:, :] = acc[:, QW + HD :].astype(jnp.bfloat16)


def project(idx, pieces, weights, acc=None, rot=None):
    if rot is None:
        out = jax.ShapeDtypeStruct((ROWS, QW + 2 * HD), jnp.float32)
    else:
        out = (
            jax.ShapeDtypeStruct((ROWS, QW), jnp.bfloat16),
            jax.ShapeDtypeStruct((2 * ROWS, HD), jnp.bfloat16),
        )
    extra = ([] if acc is None else [acc]) + ([] if rot is None else list(rot))
    n = len(pieces)
    return pl.pallas_call(
        functools.partial(project_kernel, n, acc is not None, rot is not None),
        out_shape=out,
        in_specs=[smem] + [vmem] * n + [hbm] * 3 + [vmem] * len(extra),
        out_specs=vmem if rot is None else (vmem, vmem),
        scratch_shapes=[
            pltpu.VMEM((n, ROWS, DK), jnp.bfloat16),
            pltpu.VMEM((n, DK, QW + 2 * HD), jnp.bfloat16),
            pltpu.SemaphoreType.DMA((n, 3)),
        ],
        compiler_params=pltpu.CompilerParams(vmem_limit_bytes=PROJ << 20),
        cost_estimate=tiny,
        name="project",
    )(idx, *pieces, *weights, *extra)


def attend_block(at, q_ref, keys, vals, limit, m_ref, l_ref, acc_ref):
    s = lax.dot_general(
        q_ref[at, :], keys, (((1,), (1,)), ((), ())), preferred_element_type=jnp.float32
    )
    if limit is not None:
        col = lax.broadcasted_iota(jnp.int32, s.shape, 1)
        s = jnp.where(col <= limit, s, low)
    old = m_ref[at, :]
    new = jnp.maximum(old, jnp.max(s, axis=1, keepdims=True))
    factor = jnp.exp2((old - new) * SCALE2)
    weight = jnp.exp2((s - new) * SCALE2)
    l_ref[at, :] = l_ref[at, :] * factor + jnp.sum(weight, axis=1, keepdims=True)
    acc_ref[at, :] = acc_ref[at, :] * factor + jnp.dot(
        weight.astype(jnp.bfloat16), vals, preferred_element_type=jnp.float32
    )
    m_ref[at, :] = new


def attend_source(rows_ref, i, jk_ref, jv_ref, r, valid_ref, first, o_ref, state, limit_ref=None):
    m_ref, l_ref, acc_ref = state
    m_ref[...] = jnp.full_like(m_ref, low)
    l_ref[...] = jnp.zeros_like(l_ref)
    acc_ref[...] = jnp.zeros_like(acc_ref)

    def span(step, _):
        sp = step // 2

        @pl.when(valid_ref[first + sp] != 0)
        def _():
            at = pl.ds(pl.multiple_of((step % 2) * 2 * SEL, 2 * SEL), 2 * SEL)
            limit = None if limit_ref is None else jnp.where(sp == 0, limit_ref[at, :], SPAN)
            attend_block(
                at, rows_ref.at[i], jk_ref[r * 2 + sp], jv_ref[r * 2 + sp], limit,
                m_ref, l_ref, acc_ref,
            )

        return 0

    lax.fori_loop(0, 4, span, 0)
    l = l_ref[...]
    some = l > 0.0
    mixed = acc_ref[...] / jnp.where(some, l, 1.0)
    lse = jnp.where(some, m_ref[...] * SCALE2 + jnp.log2(jnp.where(some, l, 1.0)), low)
    lane = lax.broadcasted_iota(jnp.int32, (SEL, HD), 1)
    stat = jnp.zeros((SEL, HD), jnp.float32)
    for g in range(HG):
        o_ref[i, :SEL, g * HD : (g + 1) * HD] = mixed[g * SEL : (g + 1) * SEL].astype(jnp.bfloat16)
        rest = lse[g * SEL : (g + 1) * SEL]
        for k in range(3):
            part = rest.astype(jnp.bfloat16).astype(jnp.float32)
            stat = jnp.where(lane == k * HG + g, part, stat)
            rest = rest - part
    o_ref[i, SEL:, :HD] = stat.T[:16].astype(jnp.bfloat16)
    o_ref[i, SEL:, HD:] = jnp.zeros((16, QW - HD), jnp.bfloat16)


def spread(rows_ref, i, q):
    for g in range(HG):
        rows_ref[i, g * SEL : (g + 1) * SEL, :] = q[:, g * HD : (g + 1) * HD]


def own_kernel(
    valid_ref, q_ref, k0, v0, k1, v1, n0, n1, selr_ref, rot_ref,
    jk_ref, jv_ref, oa_ref, ob_ref, rows_ref, out_ref, limit_ref, *state,
):
    spread(rows_ref, 0, q_ref[:SEL, :])
    spread(rows_ref, 1, q_ref[SEL:, :])

    def request(r, _):
        base = pl.ds(pl.multiple_of(r * SPAN, SPAN), SPAN)
        fresh_k = pl.ds(pl.multiple_of(r * SEL, SEL), SEL)
        fresh_v = pl.ds(pl.multiple_of(ROWS + r * SEL, SEL), SEL)
        for sp, (kr, vr, nr) in enumerate(((k0, v0, n0), (k1, v1, n1))):
            cached = turned(
                kr[base, :].astype(jnp.float32),
                rot_ref[r, sp : sp + 1, :],
                rot_ref[r, sp + 2 : sp + 3, :],
            )
            at = lax.broadcasted_iota(jnp.int32, (SPAN, SEL), 0)
            pick = (at == selr_ref[r, sp : sp + 1, :]).astype(jnp.float32).astype(jnp.bfloat16)
            ones = jnp.ones((SEL, HD), jnp.bfloat16)
            hit = jnp.dot(pick, ones, preferred_element_type=jnp.float32) > 0.5
            put_k = jnp.dot(pick, nr[fresh_k, :], preferred_element_type=jnp.float32)
            put_v = jnp.dot(pick, nr[fresh_v, :], preferred_element_type=jnp.float32)
            vals = vr[base, :].astype(jnp.float32)
            jk_ref[r * 2 + sp] = jnp.where(hit, put_k, cached).astype(jnp.bfloat16)
            jv_ref[r * 2 + sp] = jnp.where(hit, put_v, vals).astype(jnp.bfloat16)
        sel = selr_ref[r, 0:1, :].astype(jnp.float32)
        column = jnp.broadcast_to(sel, (SEL, SEL)).T[:, :1].astype(jnp.int32)
        limit_ref[...] = jnp.concatenate([column] * HG, axis=0)
        attend_source(
            rows_ref, r, jk_ref, jv_ref, r, valid_ref, r * 2, out_ref, state, limit_ref
        )
        return 0

    lax.fori_loop(0, SLOTS, request, 0)
    oa_ref[...] = out_ref[0]
    ob_ref[...] = out_ref[1]


def other_kernel(sources, shifts, valid_ref, *refs):
    queries, refs = refs[:sources], refs[sources:]
    jk_ref, jv_ref = refs[:2]
    outs, refs = refs[2 : 2 + 2 * len(shifts)], refs[2 + 2 * len(shifts) :]
    rows_ref, out_ref, state = refs[0], refs[1], refs[2:]
    i = 0
    for q_ref in queries:
        for start in range(0, q_ref.shape[0], SEL):
            spread(rows_ref, i, q_ref[start : start + SEL, :])
            i += 1
    first = shifts[0] * 4
    step = (shifts[-1] - shifts[0]) * 4

    def source(i, _):
        r = i % 2
        attend_source(
            rows_ref, i, jk_ref, jv_ref, r, valid_ref, first + (i // 2) * step + r * 2,
            out_ref, state,
        )
        return 0

    lax.fori_loop(0, len(outs), source, 0)
    for i, o in enumerate(outs):
        o[...] = out_ref[i]


joined_shape = jax.ShapeDtypeStruct((SLOTS * 2, SPAN, HD), jnp.bfloat16)
packed_shape = jax.ShapeDtypeStruct((PACK, QW), jnp.bfloat16)
state_scratch = [
    pltpu.VMEM((HG * SEL, 1), jnp.float32),
    pltpu.VMEM((HG * SEL, 1), jnp.float32),
    pltpu.VMEM((HG * SEL, HD), jnp.float32),
]


def attend_own(*args):
    return pl.pallas_call(
        own_kernel,
        out_shape=(joined_shape, joined_shape, packed_shape, packed_shape),
        in_specs=[smem] + [vmem] * 9,
        out_specs=(vmem,) * 4,
        scratch_shapes=[
            pltpu.VMEM((2, HG * SEL, HD), jnp.bfloat16),
            pltpu.VMEM((2, PACK, QW), jnp.bfloat16),
            pltpu.VMEM((HG * SEL, 1), jnp.int32),
        ]
        + state_scratch,
        compiler_params=pltpu.CompilerParams(vmem_limit_bytes=20 << 20),
        cost_estimate=tiny,
        name="attend_own",
    )(*args)


def attend_other(shifts, valid, queries, jk, jv):
    n = 2 * len(shifts)
    return pl.pallas_call(
        functools.partial(other_kernel, len(queries), shifts),
        out_shape=(packed_shape,) * n,
        in_specs=[smem] + [vmem] * (len(queries) + 2),
        out_specs=(vmem,) * n,
        scratch_shapes=[
            pltpu.VMEM((n, HG * SEL, HD), jnp.bfloat16),
            pltpu.VMEM((n, PACK, QW), jnp.bfloat16),
        ]
        + state_scratch,
        compiler_params=pltpu.CompilerParams(vmem_limit_bytes=20 << 20),
        cost_estimate=tiny,
        name="attend_other",
    )(valid, *queries, jk, jv)


def merge_parts(parts, put, stat_put=None):
    lse = []
    for p in parts:
        stat = p[SEL:, :HD].astype(jnp.float32)
        lse.append(stat[0:4] + stat[4:8] + stat[8:12])
    top = functools.reduce(jnp.maximum, lse)
    weight = [jnp.exp2(v - top) for v in lse]
    total = functools.reduce(jnp.add, weight)
    pad = jnp.zeros((HD - HG, SEL), jnp.float32)
    weight = [jnp.concatenate([w / total, pad], axis=0).T for w in weight]
    for g in range(HG):
        at = slice(g * HD, (g + 1) * HD)
        mixed = jnp.zeros((SEL, HD), jnp.float32)
        for w, p in zip(weight, parts):
            mixed += w[:, g : g + 1] * p[:SEL, at].astype(jnp.float32)
        put(at, mixed.astype(jnp.bfloat16))
    if stat_put is not None:
        rest = top + jnp.log2(total)
        rows = []
        for _ in range(3):
            part = rest.astype(jnp.bfloat16).astype(jnp.float32)
            rows.append(part)
            rest = rest - part
        stat_put(jnp.concatenate(rows + [jnp.zeros_like(top)], axis=0).astype(jnp.bfloat16))


def between_kernel(a0, a1, b0, b1, oa_ref, ob_ref):
    for parts, o_ref in (((a0, a1), oa_ref), ((b0, b1), ob_ref)):

        def put(at, value, o_ref=o_ref):
            o_ref[:SEL, at] = value

        def stat_put(value, o_ref=o_ref):
            o_ref[SEL:, :HD] = value
            o_ref[SEL:, HD:] = jnp.zeros((16, QW - HD), jnp.bfloat16)

        merge_parts(parts, put, stat_put)


def between(*parts):
    return pl.pallas_call(
        between_kernel,
        out_shape=(packed_shape, packed_shape),
        in_specs=[vmem] * 4,
        out_specs=(vmem, vmem),
        compiler_params=pltpu.CompilerParams(vmem_limit_bytes=8 << 20),
        cost_estimate=tiny,
        name="merge_between",
    )(*parts)


def merge_kernel(*refs):
    o_ref = refs[-1]
    for r in range(SLOTS):

        def put(at, value, r=r):
            o_ref[r * SEL : (r + 1) * SEL, at] = value

        merge_parts(refs[3 * r : 3 * r + 3], put)


def merge(*parts):
    return pl.pallas_call(
        merge_kernel,
        out_shape=jax.ShapeDtypeStruct((ROWS, QW), jnp.bfloat16),
        in_specs=[vmem] * 6,
        out_specs=vmem,
        compiler_params=pltpu.CompilerParams(vmem_limit_bytes=8 << 20),
        cost_estimate=tiny,
        name="merge",
    )(*parts)


def after(value, *others):
    return lax.optimization_barrier((value, *others))[0]


def shards(
    hidden, w_query, w_key, w_value, key_cache, value_cache,
    span_count, span_key, cache_offset, sel_index,
):
    zh, yh, yp, c = (lax.axis_index(a) for a in ("zh", "yh", "yp", "c"))
    zl, x = lax.axis_index("zl"), lax.axis_index("x")
    weights = (w_query, w_key, w_value)
    z = pz(hidden)
    right, left = px(hidden, 1), px(hidden, -1)
    k1, v1 = py(key_cache), py(value_cache)
    far = px(right, 1)
    zleft = px(z, -1)
    zright = px(after(z, left), 1)
    zfar = px(zleft, -1)
    mine = jnp.concatenate(
        [sel_index, jnp.broadcast_to(cache_offset[:, None], (SLOTS, SEL))], axis=0
    )
    theirs = py(mine)
    other = 1 - zl
    near_idx = jnp.stack(
        [zl * 4 + x, other * 4 + x, zl * 4 + (x + 3) % 4, zl * 4 + (x + 1) % 4]
    ).astype(jnp.int32)
    mid_idx = jnp.stack([zl * 4 + (x + 2) % 4, other * 4 + (x + 1) % 4]).astype(jnp.int32)
    far_idx = jnp.stack([other * 4 + (x + 3) % 4, other * 4 + (x + 2) % 4]).astype(jnp.int32)

    filled_all, rank_all = span_ranks(span_count, span_key)

    def lookup(h, half):
        start = (((h * 2 + half) * 2 + yp) * 2 + c) * SLOTS
        return (
            lax.dynamic_slice_in_dim(filled_all, start, SLOTS),
            lax.dynamic_slice_in_dim(rank_all, start, SLOTS),
        )

    span_f, span_r = zip(lookup(zh, yh), lookup(zh, 1 - yh))

    def validity(shift):
        qf, qr = lookup((zh - shift) % 4, yh)
        table = [qf & kf & (kr <= qr) for kf, kr in zip(span_f, span_r)]
        return jnp.stack(table, axis=1).astype(jnp.int32)

    position = (span_r[0][:, None] * SPAN + sel_index).reshape(-1)
    cosine, sine = tables(position)
    delta = jnp.stack(
        [span_r[0] * SPAN - cache_offset, span_r[1] * SPAN - theirs[SLOTS:, 0]], axis=1
    ).reshape(-1)
    turn_c, turn_s = tables(delta)
    rot = jnp.concatenate(
        [turn_c.reshape(SLOTS, 2, HD), turn_s.reshape(SLOTS, 2, HD)], axis=1
    )
    sel_rows = jnp.stack([sel_index, theirs[:SLOTS]], axis=1)
    valid = jnp.concatenate([validity(s) for s in range(4)], axis=0).reshape(-1)

    acc = project(near_idx, (hidden, z, right, left), weights)
    acc = project(mid_idx, (far, zleft), weights, acc)
    acc = after(acc, k1, v1)
    query, fresh = project(far_idx, (zright, zfar), weights, acc, (cosine, sine))
    minus_q, plus_q = ph(query, 1), ph(query, -1)
    fresh1 = py(fresh)
    far_a = ph(minus_q[:SEL], 1)
    far_b = ph(plus_q[SEL:], -1)
    jk, jv, own_a, own_b = attend_own(
        valid, query, key_cache, value_cache, k1, v1, fresh, fresh1, sel_rows, rot
    )
    ma, mb, pa, pb = attend_other((1, 3), valid, (minus_q, plus_q), jk, jv)
    near_a, near_b = ph(pa, 1), ph(mb, -1)
    fa, fb = attend_other((2,), valid, (far_a, far_b), jk, jv)
    back_a, back_b = ph(fa, -1), ph(fb, 1)
    both_a, both_b = between(ma, back_a, pb, back_b)
    return merge(own_a, near_a, ph(both_a, -1), own_b, near_b, ph(both_b, 1))


def solution(mesh):
    split = Mesh(mesh.devices.reshape(4, 2, 2, 2, 2, 4), AXES)
    seq, tp = AXES[:4], AXES[4:]
    placed = (
        P(seq, tp),
        P(None, tp),
        P(None, tp),
        P(None, tp),
        P(seq, tp),
        P(seq, tp),
        P(),
        P(),
        P(seq),
        P(seq, None),
    )
    return jax.shard_map(
        shards, mesh=split, in_specs=placed, out_specs=P(seq, tp), check_vma=False
    )
```

```python
import functools
import math

import jax
import jax.numpy as jnp
from jax import lax
from jax.experimental import pallas as pl
from jax.experimental.pallas import tpu as pltpu
from jax.sharding import Mesh, PartitionSpec as P

HD = 128
HG = 4
R = 8
MAXCH = 8
SPAN = 1024
SEL = 128
SLOTS = 2
ROWS = SLOTS * SEL
QW = HG * HD
PACK = SEL + 16
DK = 896
PROJ = 16

rope_base = 5000000.0
low = -1.0e30
SCALE2 = math.log2(math.e) / math.sqrt(HD)

vmem = pl.BlockSpec(memory_space=pltpu.VMEM)
smem = pl.BlockSpec(memory_space=pltpu.SMEM)
hbm = pl.BlockSpec(memory_space=pltpu.HBM)
tiny = pl.CostEstimate(flops=1, bytes_accessed=1, transcendentals=0)


def work(microseconds):
    return pl.CostEstimate(
        flops=microseconds * 1000000000, bytes_accessed=1, transcendentals=0
    )


AXES = ("zh", "yh", "yp", "c", "zl", "x")


def opposite_ways(n):
    plus = [(i, (i + 1) % n) for i in range(n)]
    minus = [(n + i, n + (i - 1) % n) for i in range(n)]
    return plus + minus


def ring_x(v):
    return lax.ppermute(v, ("c", "x"), opposite_ways(4))


def ring_z(v):
    pairs = [(2 * i + c, 2 * ((i + 1 - 2 * c) % 4) + c) for i in range(4) for c in range(2)]
    return lax.ppermute(v, ("zh", "c"), pairs)


def pz(v):
    return lax.ppermute(v, "zl", [(0, 1), (1, 0)])


def py(v):
    return lax.ppermute(v, "yh", [(0, 1), (1, 0)])


def span_ranks(span_count, span_key):
    column = jnp.arange(MAXCH, dtype=jnp.int32)
    filled = column[None, :] < span_count[:, None]
    earlier = span_key[:, :, None] < span_key[:, None, :]
    ranks = jnp.sum((earlier & filled[:, :, None]).astype(jnp.int32), axis=1, dtype=jnp.int32)
    return filled.T.reshape(-1), ranks.T.reshape(-1)


def tables(position):
    freq = rope_base ** (-(jnp.arange(HD // 2, dtype=jnp.float32) * 2.0) / HD)
    angle = position.astype(jnp.float32)[:, None] * freq
    cosine, sine = jnp.cos(angle), jnp.sin(angle)
    return jnp.concatenate([cosine, cosine], -1), jnp.concatenate([-sine, sine], -1)


def turned(v, cosine, sine):
    return v * cosine + pltpu.roll(v, HD // 2, 1) * sine


def weight_copies(sources, idx_ref, i, to_ref, slot, sem):
    at = pl.ds(pl.multiple_of(idx_ref[i] * DK, DK), DK)
    start = 0
    for j, (w, width) in enumerate(zip(sources, (QW, HD, HD))):
        to = to_ref.at[slot, :, start : start + width]
        yield pltpu.make_async_copy(w.at[at, :], to, sem.at[i, j])
        start += width


def partial_kernel(count, ahead, carried, idx_ref, *refs):
    pieces, refs = refs[:count], refs[count:]
    sources, refs = refs[:3], refs[3:]
    if carried:
        acc_ref, refs = refs[0], refs[1:]
    out_ref, refs = refs[0], refs[1:]
    if ahead:
        next_ref, refs = refs[0], refs[1:]
    held, weight, sem = refs
    for i in range(count + ahead):
        to, slot = (weight, i) if i < count else (next_ref, i - count)
        for copy in weight_copies(sources, idx_ref, i, to, slot, sem):
            copy.start()
    for i in range(count):
        held[i] = pieces[i][...]

    def add(i, acc):
        for copy in weight_copies(sources, idx_ref, i, weight, i, sem):
            copy.wait()
        return acc + jnp.dot(held[i], weight[i], preferred_element_type=jnp.float32)

    begin = acc_ref[...] if carried else jnp.zeros((ROWS, QW + 2 * HD), jnp.float32)
    out_ref[...] = lax.fori_loop(0, count, add, begin)
    for i in range(count, count + ahead):
        for copy in weight_copies(sources, idx_ref, i, next_ref, i - count, sem):
            copy.wait()


def partial_project(idx, pieces, weights, acc=None, ahead=0):
    n = len(pieces)
    sums = jax.ShapeDtypeStruct((ROWS, QW + 2 * HD), jnp.float32)
    kept = jax.ShapeDtypeStruct((ahead, DK, QW + 2 * HD), jnp.bfloat16)
    extra = [] if acc is None else [acc]
    weights = [pltpu.with_memory_space_constraint(w, pltpu.HBM) for w in weights]
    return pl.pallas_call(
        functools.partial(partial_kernel, n, ahead, acc is not None),
        out_shape=(sums, kept) if ahead else sums,
        in_specs=[smem] + [vmem] * n + [hbm] * 3 + [vmem] * len(extra),
        out_specs=(vmem, vmem) if ahead else vmem,
        scratch_shapes=[
            pltpu.VMEM((n, ROWS, DK), jnp.bfloat16),
            pltpu.VMEM((n, DK, QW + 2 * HD), jnp.bfloat16),
            pltpu.SemaphoreType.DMA((n + ahead, 3)),
        ],
        compiler_params=pltpu.CompilerParams(vmem_limit_bytes=16 << 20),
        cost_estimate=work(6),
        name="project",
    )(idx, *pieces, *weights, *extra)


def last_kernel(piece_ref, weight_ref, acc_ref, cos_ref, sin_ref, q_ref, n_ref):
    acc = acc_ref[...] + jnp.dot(
        piece_ref[...], weight_ref[0], preferred_element_type=jnp.float32
    )
    cosine, sine = cos_ref[...], sin_ref[...]
    for g in range(HG):
        at = slice(g * HD, (g + 1) * HD)
        q_ref[:, at] = turned(acc[:, at], cosine, sine).astype(jnp.bfloat16)
    n_ref[:ROWS, :] = turned(acc[:, QW : QW + HD], cosine, sine).astype(jnp.bfloat16)
    n_ref[ROWS:, :] = acc[:, QW + HD :].astype(jnp.bfloat16)


def last_project(*args):
    return pl.pallas_call(
        last_kernel,
        out_shape=(
            jax.ShapeDtypeStruct((ROWS, QW), jnp.bfloat16),
            jax.ShapeDtypeStruct((2 * ROWS, HD), jnp.bfloat16),
        ),
        in_specs=[vmem] * 5,
        out_specs=(vmem, vmem),
        compiler_params=pltpu.CompilerParams(vmem_limit_bytes=16 << 20),
        cost_estimate=tiny,
        name="project_last",
    )(*args)


def attend_block(at, q_ref, keys, vals, limit, m_ref, l_ref, acc_ref):
    s = lax.dot_general(
        q_ref[at, :], keys, (((1,), (1,)), ((), ())), preferred_element_type=jnp.float32
    )
    if limit is not None:
        col = lax.broadcasted_iota(jnp.int32, s.shape, 1)
        s = jnp.where(col <= limit, s, low)
    old = m_ref[at, :]
    new = jnp.maximum(old, jnp.max(s, axis=1, keepdims=True))
    factor = jnp.exp2((old - new) * SCALE2)
    weight = jnp.exp2((s - new) * SCALE2)
    l_ref[at, :] = l_ref[at, :] * factor + jnp.sum(weight, axis=1, keepdims=True)
    acc_ref[at, :] = acc_ref[at, :] * factor + jnp.dot(
        weight.astype(jnp.bfloat16), vals, preferred_element_type=jnp.float32
    )
    m_ref[at, :] = new


def attend_source(rows_ref, i, jk_ref, jv_ref, r, valid_ref, first, o_ref, state, limit_ref=None):
    m_ref, l_ref, acc_ref = state
    m_ref[...] = jnp.full_like(m_ref, low)
    l_ref[...] = jnp.zeros_like(l_ref)
    acc_ref[...] = jnp.zeros_like(acc_ref)

    def span(step, _):
        sp = step // 2

        @pl.when(valid_ref[first + sp] != 0)
        def _():
            at = pl.ds(pl.multiple_of((step % 2) * 2 * SEL, 2 * SEL), 2 * SEL)
            limit = None if limit_ref is None else jnp.where(sp == 0, limit_ref[at, :], SPAN)
            attend_block(
                at, rows_ref.at[i], jk_ref[r * 2 + sp], jv_ref[r * 2 + sp], limit,
                m_ref, l_ref, acc_ref,
            )

        return 0

    lax.fori_loop(0, 4, span, 0)
    l = l_ref[...]
    some = l > 0.0
    mixed = acc_ref[...] / jnp.where(some, l, 1.0)
    lse = jnp.where(some, m_ref[...] * SCALE2 + jnp.log2(jnp.where(some, l, 1.0)), low)
    lane = lax.broadcasted_iota(jnp.int32, (SEL, HD), 1)
    stat = jnp.zeros((SEL, HD), jnp.float32)
    for g in range(HG):
        o_ref[i, :SEL, g * HD : (g + 1) * HD] = mixed[g * SEL : (g + 1) * SEL].astype(jnp.bfloat16)
        rest = lse[g * SEL : (g + 1) * SEL]
        for k in range(3):
            part = rest.astype(jnp.bfloat16).astype(jnp.float32)
            stat = jnp.where(lane == k * HG + g, part, stat)
            rest = rest - part
    o_ref[i, SEL:, :HD] = stat.T[:16].astype(jnp.bfloat16)
    o_ref[i, SEL:, HD:] = jnp.zeros((16, QW - HD), jnp.bfloat16)


def spread(rows_ref, i, q):
    for g in range(HG):
        rows_ref[i, g * SEL : (g + 1) * SEL, :] = q[:, g * HD : (g + 1) * HD]


def join_kernel(k0, v0, k1, v1, n0, n1, selr_ref, rot_ref, jk_ref, jv_ref):
    def request(r, _):
        base = pl.ds(pl.multiple_of(r * SPAN, SPAN), SPAN)
        fresh_k = pl.ds(pl.multiple_of(r * SEL, SEL), SEL)
        fresh_v = pl.ds(pl.multiple_of(ROWS + r * SEL, SEL), SEL)
        for sp, (kr, vr, nr) in enumerate(((k0, v0, n0), (k1, v1, n1))):
            cached = turned(
                kr[base, :].astype(jnp.float32),
                rot_ref[r, sp : sp + 1, :],
                rot_ref[r, sp + 2 : sp + 3, :],
            )
            at = lax.broadcasted_iota(jnp.int32, (SPAN, SEL), 0)
            pick = (at == selr_ref[r, sp : sp + 1, :]).astype(jnp.float32).astype(jnp.bfloat16)
            ones = jnp.ones((SEL, HD), jnp.bfloat16)
            hit = jnp.dot(pick, ones, preferred_element_type=jnp.float32) > 0.5
            put_k = jnp.dot(pick, nr[fresh_k, :], preferred_element_type=jnp.float32)
            put_v = jnp.dot(pick, nr[fresh_v, :], preferred_element_type=jnp.float32)
            vals = vr[base, :].astype(jnp.float32)
            jk_ref[r * 2 + sp] = jnp.where(hit, put_k, cached).astype(jnp.bfloat16)
            jv_ref[r * 2 + sp] = jnp.where(hit, put_v, vals).astype(jnp.bfloat16)
        return 0

    lax.fori_loop(0, SLOTS, request, 0)


def attend_kernel(shift, valid_ref, q_ref, jk_ref, jv_ref, *refs):
    if shift == 0:
        selr_ref, o_ref, rows_ref, limit_ref = refs[:4]
        state = refs[4:]
    else:
        o_ref, rows_ref = refs[:2]
        limit_ref, state = None, refs[2:]
    for r in range(SLOTS):
        spread(rows_ref, r, q_ref[r * SEL : (r + 1) * SEL, :])

    def request(r, _):
        if shift == 0:
            sel = selr_ref[r, 0:1, :].astype(jnp.float32)
            column = jnp.broadcast_to(sel, (SEL, SEL)).T[:, :1].astype(jnp.int32)
            limit_ref[...] = jnp.concatenate([column] * HG, axis=0)
        attend_source(
            rows_ref, r, jk_ref, jv_ref, r, valid_ref, shift * 4 + r * 2, o_ref, state, limit_ref
        )
        return 0

    lax.fori_loop(0, SLOTS, request, 0)


joined_shape = jax.ShapeDtypeStruct((SLOTS * 2, SPAN, HD), jnp.bfloat16)
packed_shape = jax.ShapeDtypeStruct((SLOTS, PACK, QW), jnp.bfloat16)


def join(*args):
    return pl.pallas_call(
        join_kernel,
        out_shape=(joined_shape, joined_shape),
        in_specs=[vmem] * 8,
        out_specs=(vmem, vmem),
        compiler_params=pltpu.CompilerParams(vmem_limit_bytes=16 << 20),
        cost_estimate=work(3),
        name="join",
    )(*args)


def attend(shift, valid, *args):
    return pl.pallas_call(
        functools.partial(attend_kernel, shift),
        out_shape=packed_shape,
        in_specs=[smem] + [vmem] * len(args),
        out_specs=vmem,
        scratch_shapes=[pltpu.VMEM((SLOTS, HG * SEL, HD), jnp.bfloat16)]
        + ([pltpu.VMEM((HG * SEL, 1), jnp.int32)] if shift == 0 else [])
        + [
            pltpu.VMEM((HG * SEL, 1), jnp.float32),
            pltpu.VMEM((HG * SEL, 1), jnp.float32),
            pltpu.VMEM((HG * SEL, HD), jnp.float32),
        ],
        compiler_params=pltpu.CompilerParams(vmem_limit_bytes=16 << 20),
        cost_estimate=work(4),
        name="attend",
    )(valid, *args)


def merge_parts(parts, put, stat_put=None):
    lse = []
    for p in parts:
        stat = p[SEL:, :HD].astype(jnp.float32)
        lse.append(stat[0:4] + stat[4:8] + stat[8:12])
    top = functools.reduce(jnp.maximum, lse)
    weight = [jnp.exp2(v - top) for v in lse]
    total = functools.reduce(jnp.add, weight)
    pad = jnp.zeros((HD - HG, SEL), jnp.float32)
    weight = [jnp.concatenate([w / total, pad], axis=0).T for w in weight]
    for g in range(HG):
        at = slice(g * HD, (g + 1) * HD)
        mixed = jnp.zeros((SEL, HD), jnp.float32)
        for w, p in zip(weight, parts):
            mixed += w[:, g : g + 1] * p[:SEL, at].astype(jnp.float32)
        put(at, mixed.astype(jnp.bfloat16))
    if stat_put is not None:
        rest = top + jnp.log2(total)
        rows = []
        for _ in range(3):
            part = rest.astype(jnp.bfloat16).astype(jnp.float32)
            rows.append(part)
            rest = rest - part
        stat_put(jnp.concatenate(rows + [jnp.zeros_like(top)], axis=0).astype(jnp.bfloat16))


def between_kernel(a_ref, b_ref, o_ref):
    for r in range(SLOTS):

        def put(at, value, r=r):
            o_ref[r, :SEL, at] = value

        def stat_put(value, r=r):
            o_ref[r, SEL:, :HD] = value
            o_ref[r, SEL:, HD:] = jnp.zeros((16, QW - HD), jnp.bfloat16)

        merge_parts((a_ref.at[r], b_ref.at[r]), put, stat_put)


def between(*parts):
    return pl.pallas_call(
        between_kernel,
        out_shape=packed_shape,
        in_specs=[vmem] * 2,
        out_specs=vmem,
        compiler_params=pltpu.CompilerParams(vmem_limit_bytes=8 << 20),
        cost_estimate=work(1),
        name="merge_between",
    )(*parts)


def merge_kernel(a_ref, b_ref, o_ref):
    for r in range(SLOTS):

        def put(at, value, r=r):
            o_ref[r * SEL : (r + 1) * SEL, at] = value

        merge_parts((a_ref.at[r], b_ref.at[r]), put)


def merge(*parts):
    return pl.pallas_call(
        merge_kernel,
        out_shape=jax.ShapeDtypeStruct((ROWS, QW), jnp.bfloat16),
        in_specs=[vmem] * 2,
        out_specs=vmem,
        compiler_params=pltpu.CompilerParams(vmem_limit_bytes=8 << 20),
        cost_estimate=tiny,
        name="merge",
    )(*parts)


def after(value, *others):
    return lax.optimization_barrier((value, *others))[0]


def shards(
    hidden, w_query, w_key, w_value, key_cache, value_cache,
    span_count, span_key, cache_offset, sel_index,
):
    zh, yh, yp, c = (lax.axis_index(a) for a in ("zh", "yh", "yp", "c"))
    zl, x = lax.axis_index("zl"), lax.axis_index("x")
    weights = (w_query, w_key, w_value)
    way = 2 * c - 1
    mine = jnp.concatenate(
        [sel_index, jnp.broadcast_to(cache_offset[:, None], (SLOTS, SEL))], axis=0
    )
    theirs = py(mine)
    h = [hidden, ring_x(hidden)]
    z = [pz(hidden)]
    k1 = py(after(key_cache, theirs))
    v1 = py(value_cache)
    for _ in range(2):
        h.append(ring_x(h[-1]))
    for _ in range(3):
        z.append(ring_x(z[-1]))
    h_idx = [zl * 4 + (x + i * way) % 4 for i in range(4)]
    z_idx = [(1 - zl) * 4 + (x + i * way) % 4 for i in range(4)]
    table = lambda *entries: jnp.stack(entries).astype(jnp.int32)

    filled_all, rank_all = span_ranks(span_count, span_key)

    def lookup(h, half):
        start = (((h * 2 + half) * 2 + yp) * 2 + c) * SLOTS
        return (
            lax.dynamic_slice_in_dim(filled_all, start, SLOTS),
            lax.dynamic_slice_in_dim(rank_all, start, SLOTS),
        )

    span_f, span_r = zip(lookup(zh, yh), lookup(zh, 1 - yh))

    def validity(shift):
        qf, qr = lookup((zh + shift * way) % 4, yh)
        table = [qf & kf & (kr <= qr) for kf, kr in zip(span_f, span_r)]
        return jnp.stack(table, axis=1).astype(jnp.int32)

    position = (span_r[0][:, None] * SPAN + sel_index).reshape(-1)
    cosine, sine = tables(position)
    delta = jnp.stack(
        [span_r[0] * SPAN - cache_offset, span_r[1] * SPAN - theirs[SLOTS:, 0]], axis=1
    ).reshape(-1)
    turn_c, turn_s = tables(delta)
    rot = jnp.concatenate(
        [turn_c.reshape(SLOTS, 2, HD), turn_s.reshape(SLOTS, 2, HD)], axis=1
    )
    sel_rows = jnp.stack([sel_index, theirs[:SLOTS]], axis=1)
    valid = jnp.concatenate([validity(s) for s in range(4)], axis=0).reshape(-1)

    acc = partial_project(table(h_idx[0]), (hidden,), weights)
    acc = partial_project(table(h_idx[1], z_idx[0]), (h[1], z[0]), weights, acc)
    acc = partial_project(table(h_idx[2], z_idx[1]), (h[2], z[1]), weights, acc)
    acc, kept = partial_project(
        table(h_idx[3], z_idx[2], z_idx[3]), (h[3], z[2]), weights, acc, ahead=1
    )
    acc = after(acc, k1, v1)
    query, fresh = last_project(z[3], kept, acc, cosine, sine)
    ring = [query]
    for _ in range(3):
        ring.append(ring_z(ring[-1]))
    jk, jv = join(key_cache, value_cache, k1, v1, fresh, py(fresh), sel_rows, rot)
    own = attend(0, valid, query, jk, jv, sel_rows)
    out = attend(1, valid, ring[1], jk, jv)
    for i in (2, 3):
        out = between(attend(i, valid, ring[i], jk, jv), ring_z(out))
    return merge(own, ring_z(out))


def solution(mesh):
    split = Mesh(mesh.devices.reshape(4, 2, 2, 2, 2, 4), AXES)
    seq, tp = AXES[:4], AXES[4:]
    placed = (
        P(seq, tp),
        P(None, tp),
        P(None, tp),
        P(None, tp),
        P(seq, tp),
        P(seq, tp),
        P(),
        P(),
        P(seq),
        P(seq, None),
    )
    return jax.shard_map(
        shards, mesh=split, in_specs=placed, out_specs=P(seq, tp), check_vma=False
    )
```

```python
import functools
import math

import jax
import jax.numpy as jnp
import numpy as np
from jax import lax
from jax.experimental import pallas as pl
from jax.experimental.pallas import tpu as pltpu
from jax.sharding import Mesh, PartitionSpec as P

HD = 128
HG = 4
R = 8
MAXCH = 8
SPAN = 1024
SEL = 128
SLOTS = 2
ROWS = SLOTS * SEL
QW = HG * HD
PACK = SEL + 16
DK = 896
PROJ = 16

rope_base = 5000000.0
low = -1.0e30
SCALE2 = math.log2(math.e) / math.sqrt(HD)

vmem = pl.BlockSpec(memory_space=pltpu.VMEM)
smem = pl.BlockSpec(memory_space=pltpu.SMEM)
hbm = pl.BlockSpec(memory_space=pltpu.HBM)
tiny = pl.CostEstimate(flops=1, bytes_accessed=1, transcendentals=0)


def work(microseconds):
    return pl.CostEstimate(
        flops=microseconds * 1000000000, bytes_accessed=1, transcendentals=0
    )


AXES = ("zh", "yh", "yp", "c", "zl", "x")


def opposite_ways(n):
    plus = [(i, (i + 1) % n) for i in range(n)]
    minus = [(n + i, n + (i - 1) % n) for i in range(n)]
    return plus + minus


def ring_x(v):
    return lax.ppermute(v, ("c", "x"), opposite_ways(4))


def ring_z(v):
    pairs = [(2 * i + c, 2 * ((i + 1 - 2 * c) % 4) + c) for i in range(4) for c in range(2)]
    return lax.ppermute(v, ("zh", "c"), pairs)


def pz(v):
    return lax.ppermute(v, "zl", [(0, 1), (1, 0)])


def py(v):
    return lax.ppermute(v, "yh", [(0, 1), (1, 0)])


H_AT, Z_AT, ZH_AT, YH_AT, WAY_AT, REQ_AT = 0, 4, 8, 9, 10, 11


def prepare_kernel(
    place, count, key, offset, sel_ref, theirs_ref, freq_ref,
    cos_ref, sin_ref, rot_ref, selr_ref, valid_ref,
):
    freq = freq_ref[0:1, :]
    sign = freq_ref[1:2, :]
    zh, yh, way = place[ZH_AT], place[YH_AT], place[WAY_AT]
    for r in range(SLOTS):
        request = place[REQ_AT] + r
        used = count[request]

        def rank(j, request=request, used=used):
            mine = key[request, j]
            total = jnp.int32(0)
            for k in range(MAXCH):
                smaller = (key[request, k] < mine) & (k < used)
                total += jnp.where(smaller, 1, 0)
            return total

        spans = (zh * 2 + yh, zh * 2 + 1 - yh)
        ranks = [rank(j) for j in spans]
        for shift in range(4):
            j = lax.rem(zh + shift * way + 4, 4) * 2 + yh
            mine = rank(j)
            for sp in range(2):
                good = (j < used) & (spans[sp] < used) & (ranks[sp] <= mine)
                valid_ref[shift * 4 + r * 2 + sp] = jnp.where(good, 1, 0)
        sel = sel_ref[r : r + 1, :]
        position = (sel + ranks[0] * SPAN).astype(jnp.float32)
        angle = jnp.broadcast_to(position, (SEL, HD)).T * freq
        cos_ref[r * SEL : (r + 1) * SEL, :] = jnp.cos(angle)
        sin_ref[r * SEL : (r + 1) * SEL, :] = jnp.sin(angle) * sign
        other = ranks[1] * SPAN - theirs_ref[SLOTS + r : SLOTS + r + 1, :]
        own = jnp.zeros((1, HD), jnp.int32) + (ranks[0] * SPAN - offset[r])
        for sp, delta in enumerate((own, other)):
            angle = delta.astype(jnp.float32) * freq
            rot_ref[r, sp : sp + 1, :] = jnp.cos(angle)
            rot_ref[r, sp + 2 : sp + 3, :] = jnp.sin(angle) * sign
        selr_ref[r, 0:1, :] = sel
        selr_ref[r, 1:2, :] = theirs_ref[r : r + 1, :]


def prepare(*args):
    half = np.arange(HD // 2) * 2.0 / HD
    freq = np.tile(rope_base**-half, 2)
    sign = np.repeat([-1.0, 1.0], HD // 2)
    table = jnp.asarray(np.stack([freq, sign]), jnp.float32)
    shape = jax.ShapeDtypeStruct
    return pl.pallas_call(
        prepare_kernel,
        out_shape=(
            shape((ROWS, HD), jnp.float32),
            shape((ROWS, HD), jnp.float32),
            shape((SLOTS, 4, HD), jnp.float32),
            shape((SLOTS, 2, SEL), jnp.int32),
            shape((16,), jnp.int32),
        ),
        in_specs=[smem] * 4 + [vmem] * 3,
        out_specs=(vmem,) * 4 + (smem,),
        compiler_params=pltpu.CompilerParams(vmem_limit_bytes=8 << 20),
        cost_estimate=work(2),
        name="prepare",
    )(*args, table)


def turned(v, cosine, sine):
    return v * cosine + pltpu.roll(v, HD // 2, 1) * sine


def weight_copies(sources, piece, i, to_ref, slot, sem):
    at = pl.ds(pl.multiple_of(piece * DK, DK), DK)
    start = 0
    for j, (w, width) in enumerate(zip(sources, (QW, HD, HD))):
        to = to_ref.at[slot, :, start : start + width]
        yield pltpu.make_async_copy(w.at[at, :], to, sem.at[i, j])
        start += width


def partial_kernel(which, ahead, carried, place, *refs):
    count = len(which) - ahead
    pieces, refs = refs[:count], refs[count:]
    sources, refs = refs[:3], refs[3:]
    if carried:
        acc_ref, refs = refs[0], refs[1:]
    out_ref, refs = refs[0], refs[1:]
    if ahead:
        next_ref, refs = refs[0], refs[1:]
    weight, sem = refs
    for i in range(count + ahead):
        to, slot = (weight, i) if i < count else (next_ref, i - count)
        for copy in weight_copies(sources, place[which[i]], i, to, slot, sem):
            copy.start()
    acc = acc_ref[...] if carried else None
    for i in range(count):
        for copy in weight_copies(sources, place[which[i]], i, weight, i, sem):
            copy.wait()
        d = jnp.dot(pieces[i][...], weight[i], preferred_element_type=jnp.float32)
        acc = d if acc is None else acc + d
    out_ref[...] = acc
    for i in range(count, count + ahead):
        for copy in weight_copies(sources, place[which[i]], i, next_ref, i - count, sem):
            copy.wait()


def partial_project(place, which, pieces, weights, acc=None, ahead=0):
    n = len(pieces)
    sums = jax.ShapeDtypeStruct((ROWS, QW + 2 * HD), jnp.float32)
    kept = jax.ShapeDtypeStruct((ahead, DK, QW + 2 * HD), jnp.bfloat16)
    extra = [] if acc is None else [acc]
    weights = [pltpu.with_memory_space_constraint(w, pltpu.HBM) for w in weights]
    return pl.pallas_call(
        functools.partial(partial_kernel, which, ahead, acc is not None),
        out_shape=(sums, kept) if ahead else sums,
        in_specs=[smem] + [vmem] * n + [hbm] * 3 + [vmem] * len(extra),
        out_specs=(vmem, vmem) if ahead else vmem,
        scratch_shapes=[
            pltpu.VMEM((n, DK, QW + 2 * HD), jnp.bfloat16),
            pltpu.SemaphoreType.DMA((n + ahead, 3)),
        ],
        compiler_params=pltpu.CompilerParams(vmem_limit_bytes=16 << 20),
        cost_estimate=work(6),
        name="project",
    )(place, *pieces, *weights, *extra)


def last_kernel(piece_ref, weight_ref, acc_ref, cos_ref, sin_ref, q_ref, n_ref):
    acc = acc_ref[...] + jnp.dot(
        piece_ref[...], weight_ref[0], preferred_element_type=jnp.float32
    )
    cosine, sine = cos_ref[...], sin_ref[...]
    for g in range(HG):
        at = slice(g * HD, (g + 1) * HD)
        q_ref[:, at] = turned(acc[:, at], cosine, sine).astype(jnp.bfloat16)
    n_ref[:ROWS, :] = turned(acc[:, QW : QW + HD], cosine, sine).astype(jnp.bfloat16)
    n_ref[ROWS:, :] = acc[:, QW + HD :].astype(jnp.bfloat16)


def last_project(*args):
    return pl.pallas_call(
        last_kernel,
        out_shape=(
            jax.ShapeDtypeStruct((ROWS, QW), jnp.bfloat16),
            jax.ShapeDtypeStruct((2 * ROWS, HD), jnp.bfloat16),
        ),
        in_specs=[vmem] * 5,
        out_specs=(vmem, vmem),
        compiler_params=pltpu.CompilerParams(vmem_limit_bytes=16 << 20),
        cost_estimate=tiny,
        name="project_last",
    )(*args)


def attend_block(at, q_ref, keys, vals, limit, m_ref, l_ref, acc_ref):
    s = lax.dot_general(
        q_ref[at, :], keys, (((1,), (1,)), ((), ())), preferred_element_type=jnp.float32
    )
    if limit is not None:
        col = lax.broadcasted_iota(jnp.int32, s.shape, 1)
        s = jnp.where(col <= limit, s, low)
    old = m_ref[at, :]
    new = jnp.maximum(old, jnp.max(s, axis=1, keepdims=True))
    factor = jnp.exp2((old - new) * SCALE2)
    weight = jnp.exp2((s - new) * SCALE2)
    l_ref[at, :] = l_ref[at, :] * factor + jnp.sum(weight, axis=1, keepdims=True)
    acc_ref[at, :] = acc_ref[at, :] * factor + jnp.dot(
        weight.astype(jnp.bfloat16), vals, preferred_element_type=jnp.float32
    )
    m_ref[at, :] = new


def attend_source(rows_ref, i, jk_ref, jv_ref, r, valid_ref, first, o_ref, state, limit_ref=None):
    m_ref, l_ref, acc_ref = state
    m_ref[...] = jnp.full_like(m_ref, low)
    l_ref[...] = jnp.zeros_like(l_ref)
    acc_ref[...] = jnp.zeros_like(acc_ref)

    def span(step, _):
        sp = step // 2

        @pl.when(valid_ref[first + sp] != 0)
        def _():
            at = pl.ds(pl.multiple_of((step % 2) * 2 * SEL, 2 * SEL), 2 * SEL)
            limit = None if limit_ref is None else jnp.where(sp == 0, limit_ref[at, :], SPAN)
            attend_block(
                at, rows_ref.at[i], jk_ref[r * 2 + sp], jv_ref[r * 2 + sp], limit,
                m_ref, l_ref, acc_ref,
            )

        return 0

    lax.fori_loop(0, 4, span, 0)
    l = l_ref[...]
    some = l > 0.0
    mixed = acc_ref[...] / jnp.where(some, l, 1.0)
    lse = jnp.where(some, m_ref[...] * SCALE2 + jnp.log2(jnp.where(some, l, 1.0)), low)
    lane = lax.broadcasted_iota(jnp.int32, (SEL, HD), 1)
    stat = jnp.zeros((SEL, HD), jnp.float32)
    for g in range(HG):
        o_ref[i, :SEL, g * HD : (g + 1) * HD] = mixed[g * SEL : (g + 1) * SEL].astype(jnp.bfloat16)
        rest = lse[g * SEL : (g + 1) * SEL]
        for k in range(3):
            part = rest.astype(jnp.bfloat16).astype(jnp.float32)
            stat = jnp.where(lane == k * HG + g, part, stat)
            rest = rest - part
    o_ref[i, SEL:, :HD] = stat.T[:16].astype(jnp.bfloat16)
    o_ref[i, SEL:, HD:] = jnp.zeros((16, QW - HD), jnp.bfloat16)


def spread(rows_ref, i, q):
    for g in range(HG):
        rows_ref[i, g * SEL : (g + 1) * SEL, :] = q[:, g * HD : (g + 1) * HD]


def join_kernel(k0, v0, k1, v1, n0, n1, selr_ref, rot_ref, jk_ref, jv_ref):
    def request(r, _):
        base = pl.ds(pl.multiple_of(r * SPAN, SPAN), SPAN)
        fresh_k = pl.ds(pl.multiple_of(r * SEL, SEL), SEL)
        fresh_v = pl.ds(pl.multiple_of(ROWS + r * SEL, SEL), SEL)
        for sp, (kr, vr, nr) in enumerate(((k0, v0, n0), (k1, v1, n1))):
            cached = turned(
                kr[base, :].astype(jnp.float32),
                rot_ref[r, sp : sp + 1, :],
                rot_ref[r, sp + 2 : sp + 3, :],
            )
            at = lax.broadcasted_iota(jnp.int32, (SPAN, SEL), 0)
            pick = (at == selr_ref[r, sp : sp + 1, :]).astype(jnp.float32).astype(jnp.bfloat16)
            ones = jnp.ones((SEL, HD), jnp.bfloat16)
            hit = jnp.dot(pick, ones, preferred_element_type=jnp.float32) > 0.5
            put_k = jnp.dot(pick, nr[fresh_k, :], preferred_element_type=jnp.float32)
            put_v = jnp.dot(pick, nr[fresh_v, :], preferred_element_type=jnp.float32)
            vals = vr[base, :].astype(jnp.float32)
            jk_ref[r * 2 + sp] = jnp.where(hit, put_k, cached).astype(jnp.bfloat16)
            jv_ref[r * 2 + sp] = jnp.where(hit, put_v, vals).astype(jnp.bfloat16)
        return 0

    lax.fori_loop(0, SLOTS, request, 0)


def attend_kernel(shift, valid_ref, q_ref, jk_ref, jv_ref, *refs):
    if shift == 0:
        selr_ref, o_ref, rows_ref, limit_ref = refs[:4]
        state = refs[4:]
    else:
        o_ref, rows_ref = refs[:2]
        limit_ref, state = None, refs[2:]
    for r in range(SLOTS):
        spread(rows_ref, r, q_ref[r * SEL : (r + 1) * SEL, :])

    def request(r, _):
        if shift == 0:
            sel = selr_ref[r, 0:1, :].astype(jnp.float32)
            column = jnp.broadcast_to(sel, (SEL, SEL)).T[:, :1].astype(jnp.int32)
            limit_ref[...] = jnp.concatenate([column] * HG, axis=0)
        attend_source(
            rows_ref, r, jk_ref, jv_ref, r, valid_ref, shift * 4 + r * 2, o_ref, state, limit_ref
        )
        return 0

    lax.fori_loop(0, SLOTS, request, 0)


joined_shape = jax.ShapeDtypeStruct((SLOTS * 2, SPAN, HD), jnp.bfloat16)
packed_shape = jax.ShapeDtypeStruct((SLOTS, PACK, QW), jnp.bfloat16)


def join(*args):
    return pl.pallas_call(
        join_kernel,
        out_shape=(joined_shape, joined_shape),
        in_specs=[vmem] * 8,
        out_specs=(vmem, vmem),
        compiler_params=pltpu.CompilerParams(vmem_limit_bytes=16 << 20),
        cost_estimate=work(3),
        name="join",
    )(*args)


def attend(shift, valid, *args):
    return pl.pallas_call(
        functools.partial(attend_kernel, shift),
        out_shape=packed_shape,
        in_specs=[smem] + [vmem] * len(args),
        out_specs=vmem,
        scratch_shapes=[pltpu.VMEM((SLOTS, HG * SEL, HD), jnp.bfloat16)]
        + ([pltpu.VMEM((HG * SEL, 1), jnp.int32)] if shift == 0 else [])
        + [
            pltpu.VMEM((HG * SEL, 1), jnp.float32),
            pltpu.VMEM((HG * SEL, 1), jnp.float32),
            pltpu.VMEM((HG * SEL, HD), jnp.float32),
        ],
        compiler_params=pltpu.CompilerParams(vmem_limit_bytes=16 << 20),
        cost_estimate=work(4),
        name="attend",
    )(valid, *args)


def merge_parts(parts, put, stat_put=None):
    lse = []
    for p in parts:
        stat = p[SEL:, :HD].astype(jnp.float32)
        lse.append(stat[0:4] + stat[4:8] + stat[8:12])
    top = functools.reduce(jnp.maximum, lse)
    weight = [jnp.exp2(v - top) for v in lse]
    total = functools.reduce(jnp.add, weight)
    pad = jnp.zeros((HD - HG, SEL), jnp.float32)
    weight = [jnp.concatenate([w / total, pad], axis=0).T for w in weight]
    for g in range(HG):
        at = slice(g * HD, (g + 1) * HD)
        mixed = jnp.zeros((SEL, HD), jnp.float32)
        for w, p in zip(weight, parts):
            mixed += w[:, g : g + 1] * p[:SEL, at].astype(jnp.float32)
        put(at, mixed.astype(jnp.bfloat16))
    if stat_put is not None:
        rest = top + jnp.log2(total)
        rows = []
        for _ in range(3):
            part = rest.astype(jnp.bfloat16).astype(jnp.float32)
            rows.append(part)
            rest = rest - part
        stat_put(jnp.concatenate(rows + [jnp.zeros_like(top)], axis=0).astype(jnp.bfloat16))


def between_kernel(a_ref, b_ref, o_ref):
    for r in range(SLOTS):

        def put(at, value, r=r):
            o_ref[r, :SEL, at] = value

        def stat_put(value, r=r):
            o_ref[r, SEL:, :HD] = value
            o_ref[r, SEL:, HD:] = jnp.zeros((16, QW - HD), jnp.bfloat16)

        merge_parts((a_ref.at[r], b_ref.at[r]), put, stat_put)


def between(*parts):
    return pl.pallas_call(
        between_kernel,
        out_shape=packed_shape,
        in_specs=[vmem] * 2,
        out_specs=vmem,
        compiler_params=pltpu.CompilerParams(vmem_limit_bytes=8 << 20),
        cost_estimate=work(1),
        name="merge_between",
    )(*parts)


def merge_kernel(a_ref, b_ref, o_ref):
    for r in range(SLOTS):

        def put(at, value, r=r):
            o_ref[r * SEL : (r + 1) * SEL, at] = value

        merge_parts((a_ref.at[r], b_ref.at[r]), put)


def merge(*parts):
    return pl.pallas_call(
        merge_kernel,
        out_shape=jax.ShapeDtypeStruct((ROWS, QW), jnp.bfloat16),
        in_specs=[vmem] * 2,
        out_specs=vmem,
        compiler_params=pltpu.CompilerParams(vmem_limit_bytes=8 << 20),
        cost_estimate=tiny,
        name="merge",
    )(*parts)


def after(value, *others):
    return lax.optimization_barrier((value, *others))[0]


def shards(
    hidden, w_query, w_key, w_value, key_cache, value_cache,
    span_count, span_key, cache_offset, sel_index,
):
    zh, yh, yp, c = (lax.axis_index(a) for a in ("zh", "yh", "yp", "c"))
    zl, x = lax.axis_index("zl"), lax.axis_index("x")
    weights = (w_query, w_key, w_value)
    way = 2 * c - 1
    entries = [zl * 4 + (x + i * way) % 4 for i in range(4)]
    entries += [(1 - zl) * 4 + (x + i * way) % 4 for i in range(4)]
    entries += [zh, yh, way, (yp * 2 + c) * SLOTS]
    place = jnp.stack(entries).astype(jnp.int32)
    mine = jnp.concatenate(
        [sel_index, jnp.broadcast_to(cache_offset[:, None], (SLOTS, SEL))], axis=0
    )
    theirs = py(mine)
    h = [hidden, ring_x(hidden)]
    z = [pz(hidden)]
    k1 = py(after(key_cache, theirs))
    v1 = py(after(value_cache, h[1]))
    for _ in range(2):
        h.append(ring_x(h[-1]))
    for _ in range(3):
        z.append(ring_x(z[-1]))
    cosine, sine, rot, sel_rows, valid = prepare(
        after(place, h[2]), span_count, span_key, cache_offset, sel_index, theirs
    )
    project = functools.partial(partial_project, place)
    acc = project((H_AT, H_AT + 1), (hidden, h[1]), weights)
    acc = project((H_AT + 2, Z_AT), (h[2], z[0]), weights, acc)
    acc = project((H_AT + 3, Z_AT + 1), (h[3], z[1]), weights, acc)
    acc, kept = project((Z_AT + 2, Z_AT + 3), (z[2],), weights, acc, ahead=1)
    acc = after(acc, k1, v1)
    query, fresh = last_project(z[3], kept, acc, cosine, sine)
    ring = [query]
    for _ in range(3):
        ring.append(ring_z(ring[-1]))
    jk, jv = join(key_cache, value_cache, k1, v1, fresh, py(fresh), sel_rows, rot)
    own = attend(0, valid, query, jk, jv, sel_rows)
    out = attend(1, valid, ring[1], jk, jv)
    for i in (2, 3):
        out = between(attend(i, valid, ring[i], jk, jv), ring_z(out))
    return merge(own, ring_z(out))


def solution(mesh):
    split = Mesh(mesh.devices.reshape(4, 2, 2, 2, 2, 4), AXES)
    seq, tp = AXES[:4], AXES[4:]
    placed = (
        P(seq, tp),
        P(None, tp),
        P(None, tp),
        P(None, tp),
        P(seq, tp),
        P(seq, tp),
        P(),
        P(),
        P(seq),
        P(seq, None),
    )
    return jax.shard_map(
        shards, mesh=split, in_specs=placed, out_specs=P(seq, tp), check_vma=False
    )
```

```python
import functools
import math

import jax
import jax.numpy as jnp
import numpy as np
from jax import lax
from jax.experimental import pallas as pl
from jax.experimental.pallas import tpu as pltpu
from jax.sharding import Mesh, PartitionSpec as P

HD = 128
HG = 4
R = 8
MAXCH = 8
SPAN = 1024
SEL = 128
SLOTS = 2
ROWS = SLOTS * SEL
QW = HG * HD
PACK = SEL + 16
DK = 896
PROJ = 16

rope_base = 5000000.0
low = -1.0e30
SCALE2 = math.log2(math.e) / math.sqrt(HD)

vmem = pl.BlockSpec(memory_space=pltpu.VMEM)
smem = pl.BlockSpec(memory_space=pltpu.SMEM)
hbm = pl.BlockSpec(memory_space=pltpu.HBM)
tiny = pl.CostEstimate(flops=1, bytes_accessed=1, transcendentals=0)


def work(microseconds):
    return pl.CostEstimate(
        flops=microseconds * 1000000000, bytes_accessed=1, transcendentals=0
    )


AXES = ("zh", "yh", "yp", "c", "zl", "x")


def opposite_ways(n):
    plus = [(i, (i + 1) % n) for i in range(n)]
    minus = [(n + i, n + (i - 1) % n) for i in range(n)]
    return plus + minus


def ring_x(v):
    return lax.ppermute(v, ("c", "x"), opposite_ways(4))


def ring_z(v):
    pairs = [(2 * i + c, 2 * ((i + 1 - 2 * c) % 4) + c) for i in range(4) for c in range(2)]
    return lax.ppermute(v, ("zh", "c"), pairs)


def pz(v):
    return lax.ppermute(v, "zl", [(0, 1), (1, 0)])


def py(v):
    return lax.ppermute(v, "yh", [(0, 1), (1, 0)])


H_AT, Z_AT, ZH_AT, YH_AT, WAY_AT, REQ_AT = 0, 4, 8, 9, 10, 11


def prepare_kernel(
    place, count, key, offset, sel_ref, theirs_ref, freq_ref,
    cos_ref, sin_ref, rot_ref, selr_ref, valid_ref,
):
    freq = freq_ref[0:1, :]
    sign = freq_ref[1:2, :]
    zh, yh, way = place[ZH_AT], place[YH_AT], place[WAY_AT]
    for r in range(SLOTS):
        request = place[REQ_AT] + r
        used = count[request]

        def rank(j, request=request, used=used):
            mine = key[request, j]
            total = jnp.int32(0)
            for k in range(MAXCH):
                smaller = (key[request, k] < mine) & (k < used)
                total += jnp.where(smaller, 1, 0)
            return total

        spans = (zh * 2 + yh, zh * 2 + 1 - yh)
        ranks = [rank(j) for j in spans]
        for shift in range(4):
            j = lax.rem(zh + shift * way + 4, 4) * 2 + yh
            mine = rank(j)
            for sp in range(2):
                good = (j < used) & (spans[sp] < used) & (ranks[sp] <= mine)
                valid_ref[shift * 4 + r * 2 + sp] = jnp.where(good, 1, 0)
        sel = sel_ref[r : r + 1, :]
        position = (sel + ranks[0] * SPAN).astype(jnp.float32)
        angle = jnp.broadcast_to(position, (SEL, HD)).T * freq
        cos_ref[r * SEL : (r + 1) * SEL, :] = jnp.cos(angle)
        sin_ref[r * SEL : (r + 1) * SEL, :] = jnp.sin(angle) * sign
        other = ranks[1] * SPAN - theirs_ref[SLOTS + r : SLOTS + r + 1, :]
        own = jnp.zeros((1, HD), jnp.int32) + (ranks[0] * SPAN - offset[r])
        for sp, delta in enumerate((own, other)):
            angle = delta.astype(jnp.float32) * freq
            rot_ref[r, sp : sp + 1, :] = jnp.cos(angle)
            rot_ref[r, sp + 2 : sp + 3, :] = jnp.sin(angle) * sign
        selr_ref[r, 0:1, :] = sel
        selr_ref[r, 1:2, :] = theirs_ref[r : r + 1, :]


def prepare(*args):
    half = np.arange(HD // 2) * 2.0 / HD
    freq = np.tile(rope_base**-half, 2)
    sign = np.repeat([-1.0, 1.0], HD // 2)
    table = jnp.asarray(np.stack([freq, sign]), jnp.float32)
    shape = jax.ShapeDtypeStruct
    return pl.pallas_call(
        prepare_kernel,
        out_shape=(
            shape((ROWS, HD), jnp.float32),
            shape((ROWS, HD), jnp.float32),
            shape((SLOTS, 4, HD), jnp.float32),
            shape((SLOTS, 2, SEL), jnp.int32),
            shape((16,), jnp.int32),
        ),
        in_specs=[smem] * 4 + [vmem] * 3,
        out_specs=(vmem,) * 4 + (smem,),
        compiler_params=pltpu.CompilerParams(vmem_limit_bytes=8 << 20),
        cost_estimate=work(2),
        name="prepare",
    )(*args, table)


def turned(v, cosine, sine):
    return v * cosine + pltpu.roll(v, HD // 2, 1) * sine


def weight_copies(sources, piece, i, to_ref, slot, sem):
    at = pl.ds(pl.multiple_of(piece * DK, DK), DK)
    start = 0
    for j, (w, width) in enumerate(zip(sources, (QW, HD, HD))):
        to = to_ref.at[slot, :, start : start + width]
        yield pltpu.make_async_copy(w.at[at, :], to, sem.at[i, j])
        start += width


def partial_kernel(which, ahead, carried, place, *refs):
    count = len(which) - ahead
    pieces, refs = refs[:count], refs[count:]
    sources, refs = refs[:3], refs[3:]
    if carried:
        acc_ref, refs = refs[0], refs[1:]
    out_ref, refs = refs[0], refs[1:]
    if ahead:
        next_ref, refs = refs[0], refs[1:]
    weight, sem = refs
    for i in range(count + ahead):
        to, slot = (weight, i) if i < count else (next_ref, i - count)
        for copy in weight_copies(sources, place[which[i]], i, to, slot, sem):
            copy.start()
    acc = acc_ref[...] if carried else None
    for i in range(count):
        for copy in weight_copies(sources, place[which[i]], i, weight, i, sem):
            copy.wait()
        d = jnp.dot(pieces[i][...], weight[i], preferred_element_type=jnp.float32)
        acc = d if acc is None else acc + d
    out_ref[...] = acc
    for i in range(count, count + ahead):
        for copy in weight_copies(sources, place[which[i]], i, next_ref, i - count, sem):
            copy.wait()


def partial_project(place, which, pieces, weights, acc=None, ahead=0):
    n = len(pieces)
    sums = jax.ShapeDtypeStruct((ROWS, QW + 2 * HD), jnp.float32)
    kept = jax.ShapeDtypeStruct((ahead, DK, QW + 2 * HD), jnp.bfloat16)
    extra = [] if acc is None else [acc]
    weights = [pltpu.with_memory_space_constraint(w, pltpu.HBM) for w in weights]
    return pl.pallas_call(
        functools.partial(partial_kernel, which, ahead, acc is not None),
        out_shape=(sums, kept) if ahead else sums,
        in_specs=[smem] + [vmem] * n + [hbm] * 3 + [vmem] * len(extra),
        out_specs=(vmem, vmem) if ahead else vmem,
        scratch_shapes=[
            pltpu.VMEM((n, DK, QW + 2 * HD), jnp.bfloat16),
            pltpu.SemaphoreType.DMA((n + ahead, 3)),
        ],
        compiler_params=pltpu.CompilerParams(vmem_limit_bytes=16 << 20),
        cost_estimate=work(6),
        name="project",
    )(place, *pieces, *weights, *extra)


def last_kernel(piece_ref, weight_ref, acc_ref, cos_ref, sin_ref, q_ref, n_ref):
    acc = acc_ref[...] + jnp.dot(
        piece_ref[...], weight_ref[0], preferred_element_type=jnp.float32
    )
    cosine, sine = cos_ref[...], sin_ref[...]
    for g in range(HG):
        at = slice(g * HD, (g + 1) * HD)
        q_ref[:, at] = turned(acc[:, at], cosine, sine).astype(jnp.bfloat16)
    n_ref[:ROWS, :] = turned(acc[:, QW : QW + HD], cosine, sine).astype(jnp.bfloat16)
    n_ref[ROWS:, :] = acc[:, QW + HD :].astype(jnp.bfloat16)


def last_project(*args):
    return pl.pallas_call(
        last_kernel,
        out_shape=(
            jax.ShapeDtypeStruct((ROWS, QW), jnp.bfloat16),
            jax.ShapeDtypeStruct((2 * ROWS, HD), jnp.bfloat16),
        ),
        in_specs=[vmem] * 5,
        out_specs=(vmem, vmem),
        compiler_params=pltpu.CompilerParams(vmem_limit_bytes=16 << 20),
        cost_estimate=tiny,
        name="project_last",
    )(*args)


def attend_block(at, q_ref, keys, vals, limit, m_ref, l_ref, acc_ref):
    s = lax.dot_general(
        q_ref[at, :], keys, (((1,), (1,)), ((), ())), preferred_element_type=jnp.float32
    )
    if limit is not None:
        col = lax.broadcasted_iota(jnp.int32, s.shape, 1)
        s = jnp.where(col <= limit, s, low)
    old = m_ref[at, :]
    new = jnp.maximum(old, jnp.max(s, axis=1, keepdims=True))
    factor = jnp.exp2((old - new) * SCALE2)
    weight = jnp.exp2((s - new) * SCALE2)
    l_ref[at, :] = l_ref[at, :] * factor + jnp.sum(weight, axis=1, keepdims=True)
    acc_ref[at, :] = acc_ref[at, :] * factor + jnp.dot(
        weight.astype(jnp.bfloat16), vals, preferred_element_type=jnp.float32
    )
    m_ref[at, :] = new


def attend_source(rows_ref, i, jk_ref, jv_ref, r, valid_ref, first, o_ref, state, limit_ref=None):
    m_ref, l_ref, acc_ref = state
    m_ref[...] = jnp.full_like(m_ref, low)
    l_ref[...] = jnp.zeros_like(l_ref)
    acc_ref[...] = jnp.zeros_like(acc_ref)

    def span(step, _):
        sp = step // 2

        @pl.when(valid_ref[first + sp] != 0)
        def _():
            at = pl.ds(pl.multiple_of((step % 2) * 2 * SEL, 2 * SEL), 2 * SEL)
            limit = None if limit_ref is None else jnp.where(sp == 0, limit_ref[at, :], SPAN)
            attend_block(
                at, rows_ref.at[i], jk_ref[r * 2 + sp], jv_ref[r * 2 + sp], limit,
                m_ref, l_ref, acc_ref,
            )

        return 0

    lax.fori_loop(0, 4, span, 0)
    l = l_ref[...]
    some = l > 0.0
    mixed = acc_ref[...] / jnp.where(some, l, 1.0)
    lse = jnp.where(some, m_ref[...] * SCALE2 + jnp.log2(jnp.where(some, l, 1.0)), low)
    lane = lax.broadcasted_iota(jnp.int32, (SEL, HD), 1)
    stat = jnp.zeros((SEL, HD), jnp.float32)
    for g in range(HG):
        o_ref[i, :SEL, g * HD : (g + 1) * HD] = mixed[g * SEL : (g + 1) * SEL].astype(jnp.bfloat16)
        rest = lse[g * SEL : (g + 1) * SEL]
        for k in range(3):
            part = rest.astype(jnp.bfloat16).astype(jnp.float32)
            stat = jnp.where(lane == k * HG + g, part, stat)
            rest = rest - part
    o_ref[i, SEL:, :HD] = stat.T[:16].astype(jnp.bfloat16)
    o_ref[i, SEL:, HD:] = jnp.zeros((16, QW - HD), jnp.bfloat16)


def spread(rows_ref, i, q):
    for g in range(HG):
        rows_ref[i, g * SEL : (g + 1) * SEL, :] = q[:, g * HD : (g + 1) * HD]


def join_kernel(k0, v0, k1, v1, n0, n1, selr_ref, rot_ref, jk_ref, jv_ref):
    def request(r, _):
        base = pl.ds(pl.multiple_of(r * SPAN, SPAN), SPAN)
        fresh_k = pl.ds(pl.multiple_of(r * SEL, SEL), SEL)
        fresh_v = pl.ds(pl.multiple_of(ROWS + r * SEL, SEL), SEL)
        for sp, (kr, vr, nr) in enumerate(((k0, v0, n0), (k1, v1, n1))):
            cached = turned(
                kr[base, :].astype(jnp.float32),
                rot_ref[r, sp : sp + 1, :],
                rot_ref[r, sp + 2 : sp + 3, :],
            )
            at = lax.broadcasted_iota(jnp.int32, (SPAN, SEL), 0)
            pick = (at == selr_ref[r, sp : sp + 1, :]).astype(jnp.float32).astype(jnp.bfloat16)
            ones = jnp.ones((SEL, HD), jnp.bfloat16)
            hit = jnp.dot(pick, ones, preferred_element_type=jnp.float32) > 0.5
            put_k = jnp.dot(pick, nr[fresh_k, :], preferred_element_type=jnp.float32)
            put_v = jnp.dot(pick, nr[fresh_v, :], preferred_element_type=jnp.float32)
            vals = vr[base, :].astype(jnp.float32)
            jk_ref[r * 2 + sp] = jnp.where(hit, put_k, cached).astype(jnp.bfloat16)
            jv_ref[r * 2 + sp] = jnp.where(hit, put_v, vals).astype(jnp.bfloat16)
        return 0

    lax.fori_loop(0, SLOTS, request, 0)


def attend_kernel(shift, valid_ref, q_ref, jk_ref, jv_ref, *refs):
    if shift == 0:
        selr_ref, o_ref, rows_ref, limit_ref = refs[:4]
        state = refs[4:]
    else:
        o_ref, rows_ref = refs[:2]
        limit_ref, state = None, refs[2:]
    for r in range(SLOTS):
        spread(rows_ref, r, q_ref[r * SEL : (r + 1) * SEL, :])

    def request(r, _):
        if shift == 0:
            sel = selr_ref[r, 0:1, :].astype(jnp.float32)
            column = jnp.broadcast_to(sel, (SEL, SEL)).T[:, :1].astype(jnp.int32)
            limit_ref[...] = jnp.concatenate([column] * HG, axis=0)
        attend_source(
            rows_ref, r, jk_ref, jv_ref, r, valid_ref, shift * 4 + r * 2, o_ref, state, limit_ref
        )
        return 0

    lax.fori_loop(0, SLOTS, request, 0)


joined_shape = jax.ShapeDtypeStruct((SLOTS * 2, SPAN, HD), jnp.bfloat16)
packed_shape = jax.ShapeDtypeStruct((SLOTS, PACK, QW), jnp.bfloat16)


def join(*args):
    return pl.pallas_call(
        join_kernel,
        out_shape=(joined_shape, joined_shape),
        in_specs=[vmem] * 8,
        out_specs=(vmem, vmem),
        compiler_params=pltpu.CompilerParams(vmem_limit_bytes=16 << 20),
        cost_estimate=work(3),
        name="join",
    )(*args)


def attend(shift, valid, *args):
    return pl.pallas_call(
        functools.partial(attend_kernel, shift),
        out_shape=packed_shape,
        in_specs=[smem] + [vmem] * len(args),
        out_specs=vmem,
        scratch_shapes=[pltpu.VMEM((SLOTS, HG * SEL, HD), jnp.bfloat16)]
        + ([pltpu.VMEM((HG * SEL, 1), jnp.int32)] if shift == 0 else [])
        + [
            pltpu.VMEM((HG * SEL, 1), jnp.float32),
            pltpu.VMEM((HG * SEL, 1), jnp.float32),
            pltpu.VMEM((HG * SEL, HD), jnp.float32),
        ],
        compiler_params=pltpu.CompilerParams(vmem_limit_bytes=16 << 20),
        cost_estimate=work(4),
        name="attend",
    )(valid, *args)


def merge_parts(parts, put, stat_put=None):
    lse = []
    for p in parts:
        stat = p[SEL:, :HD].astype(jnp.float32)
        lse.append(stat[0:4] + stat[4:8] + stat[8:12])
    top = functools.reduce(jnp.maximum, lse)
    weight = [jnp.exp2(v - top) for v in lse]
    total = functools.reduce(jnp.add, weight)
    pad = jnp.zeros((HD - HG, SEL), jnp.float32)
    weight = [jnp.concatenate([w / total, pad], axis=0).T for w in weight]
    for g in range(HG):
        at = slice(g * HD, (g + 1) * HD)
        mixed = jnp.zeros((SEL, HD), jnp.float32)
        for w, p in zip(weight, parts):
            mixed += w[:, g : g + 1] * p[:SEL, at].astype(jnp.float32)
        put(at, mixed.astype(jnp.bfloat16))
    if stat_put is not None:
        rest = top + jnp.log2(total)
        rows = []
        for _ in range(3):
            part = rest.astype(jnp.bfloat16).astype(jnp.float32)
            rows.append(part)
            rest = rest - part
        stat_put(jnp.concatenate(rows + [jnp.zeros_like(top)], axis=0).astype(jnp.bfloat16))


def between_kernel(a_ref, b_ref, o_ref):
    for r in range(SLOTS):

        def put(at, value, r=r):
            o_ref[r, :SEL, at] = value

        def stat_put(value, r=r):
            o_ref[r, SEL:, :HD] = value
            o_ref[r, SEL:, HD:] = jnp.zeros((16, QW - HD), jnp.bfloat16)

        merge_parts((a_ref.at[r], b_ref.at[r]), put, stat_put)


def between(*parts):
    return pl.pallas_call(
        between_kernel,
        out_shape=packed_shape,
        in_specs=[vmem] * 2,
        out_specs=vmem,
        compiler_params=pltpu.CompilerParams(vmem_limit_bytes=8 << 20),
        cost_estimate=work(1),
        name="merge_between",
    )(*parts)


def merge_kernel(a_ref, b_ref, o_ref):
    for r in range(SLOTS):

        def put(at, value, r=r):
            o_ref[r * SEL : (r + 1) * SEL, at] = value

        merge_parts((a_ref.at[r], b_ref.at[r]), put)


def merge(*parts):
    return pl.pallas_call(
        merge_kernel,
        out_shape=jax.ShapeDtypeStruct((ROWS, QW), jnp.bfloat16),
        in_specs=[vmem] * 2,
        out_specs=vmem,
        compiler_params=pltpu.CompilerParams(vmem_limit_bytes=8 << 20),
        cost_estimate=tiny,
        name="merge",
    )(*parts)


def after(value, *others):
    return lax.optimization_barrier((value, *others))[0]


def shards(
    hidden, w_query, w_key, w_value, key_cache, value_cache,
    span_count, span_key, cache_offset, sel_index,
):
    zh, yh, yp, c = (lax.axis_index(a) for a in ("zh", "yh", "yp", "c"))
    zl, x = lax.axis_index("zl"), lax.axis_index("x")
    weights = (w_query, w_key, w_value)
    way = 2 * c - 1
    entries = [zl * 4 + (x + i * way) % 4 for i in range(4)]
    entries += [(1 - zl) * 4 + (x + i * way) % 4 for i in range(4)]
    entries += [zh, yh, way, (yp * 2 + c) * SLOTS]
    place = jnp.stack(entries).astype(jnp.int32)
    mine = jnp.concatenate(
        [sel_index, jnp.broadcast_to(cache_offset[:, None], (SLOTS, SEL))], axis=0
    )
    h = [hidden, ring_x(hidden)]
    z = [pz(hidden)]
    k1 = py(key_cache)
    theirs = py(after(mine, h[1]))
    for _ in range(2):
        h.append(ring_x(h[-1]))
    for _ in range(2):
        z.append(ring_x(z[-1]))
    z.append(pz(h[3]))
    v1 = py(after(value_cache, h[2]))
    cosine, sine, rot, sel_rows, valid = prepare(
        after(place, h[3]), span_count, span_key, cache_offset, sel_index, theirs
    )
    project = functools.partial(partial_project, place)
    acc = project((H_AT, H_AT + 1), (hidden, h[1]), weights)
    acc = project((H_AT + 2, Z_AT), (h[2], z[0]), weights, acc)
    acc = project((H_AT + 3, Z_AT + 1), (h[3], z[1]), weights, acc)
    acc, kept = project((Z_AT + 2, Z_AT + 3), (z[2],), weights, acc, ahead=1)
    acc = after(acc, k1, v1)
    query, fresh = last_project(z[3], kept, acc, cosine, sine)
    ring = [query]
    for _ in range(3):
        ring.append(ring_z(ring[-1]))
    jk, jv = join(key_cache, value_cache, k1, v1, fresh, py(fresh), sel_rows, rot)
    own = attend(0, valid, query, jk, jv, sel_rows)
    out = attend(1, valid, ring[1], jk, jv)
    for i in (2, 3):
        out = between(attend(i, valid, ring[i], jk, jv), ring_z(out))
    return merge(own, ring_z(out))


def solution(mesh):
    split = Mesh(mesh.devices.reshape(4, 2, 2, 2, 2, 4), AXES)
    seq, tp = AXES[:4], AXES[4:]
    placed = (
        P(seq, tp),
        P(None, tp),
        P(None, tp),
        P(None, tp),
        P(seq, tp),
        P(seq, tp),
        P(),
        P(),
        P(seq),
        P(seq, None),
    )
    return jax.shard_map(
        shards, mesh=split, in_specs=placed, out_specs=P(seq, tp), check_vma=False
    )
```

```python
import functools
import math

import jax
import jax.numpy as jnp
import numpy as np
from jax import lax
from jax.experimental import pallas as pl
from jax.experimental.pallas import tpu as pltpu
from jax.sharding import Mesh, PartitionSpec as P

HD = 128
HG = 4
R = 8
MAXCH = 8
SPAN = 1024
SEL = 128
SLOTS = 2
ROWS = SLOTS * SEL
QW = HG * HD
PACK = SEL + 16
DK = 896
FRESH = 32
SEND = SEL + 2 * FRESH
HELD = 2 * SPAN + 16
PROJ = 16

rope_base = 5000000.0
low = -1.0e30
SCALE2 = math.log2(math.e) / math.sqrt(HD)

vmem = pl.BlockSpec(memory_space=pltpu.VMEM)
smem = pl.BlockSpec(memory_space=pltpu.SMEM)
hbm = pl.BlockSpec(memory_space=pltpu.HBM)
tiny = pl.CostEstimate(flops=1, bytes_accessed=1, transcendentals=0)


def work(microseconds):
    return pl.CostEstimate(
        flops=microseconds * 1000000000, bytes_accessed=1, transcendentals=0
    )


AXES = ("zh", "yh", "yp", "c", "zl", "x")


def opposite_ways(n):
    plus = [(i, (i + 1) % n) for i in range(n)]
    minus = [(n + i, n + (i - 1) % n) for i in range(n)]
    return plus + minus


def ring_x(v):
    return lax.ppermute(v, ("c", "x"), opposite_ways(4))


def ring_z(v):
    pairs = [(2 * i + c, 2 * ((i + 1 - 2 * c) % 4) + c) for i in range(4) for c in range(2)]
    return lax.ppermute(v, ("zh", "c"), pairs)


def pz(v):
    return lax.ppermute(v, "zl", [(0, 1), (1, 0)])


def py(v):
    return lax.ppermute(v, "yh", [(0, 1), (1, 0)])


H_AT, Z_AT, ZH_AT, YH_AT, WAY_AT, REQ_AT = 0, 4, 8, 9, 10, 11


def prepare_kernel(place, count, key, sel_ref, freq_ref, cos_ref, sin_ref, rank_ref, valid_ref):
    freq = freq_ref[0:1, :]
    sign = freq_ref[1:2, :]
    zh, yh, way = place[ZH_AT], place[YH_AT], place[WAY_AT]
    along = [lax.rem(zh + i * way + 4, 4) * 2 + yh for i in range(4)]
    beside = zh * 2 + 1 - yh
    for r in range(SLOTS):
        request = place[REQ_AT] + r
        used = count[request]

        def rank(j, request=request, used=used):
            mine = key[request, j]
            total = jnp.int32(0)
            for k in range(MAXCH):
                smaller = (key[request, k] < mine) & (k < used)
                total += jnp.where(smaller, 1, 0)
            return total

        ranks = [rank(j) for j in along]
        rank_beside = rank(beside)
        if r == 0:
            queries = list(zip(along, ranks))
            spans = [(along[0], ranks[0]), (beside, rank_beside)]
            rank_ref[0] = ranks[0]
            rank_ref[1] = rank_beside
            pairs = [(i * 2 + sp, q, k) for i, q in enumerate(queries) for sp, k in enumerate(spans)]
        else:
            queries = [(along[0], ranks[0]), (beside, rank_beside)]
            spans = list(zip(along, ranks))
            for i in range(4):
                rank_ref[2 + i] = ranks[i]
            pairs = [
                (8 + i * 2 + n, q, k) for i, k in enumerate(spans) for n, q in enumerate(queries)
            ]
        for at, (qj, q_rank), (kj, k_rank) in pairs:
            good = (qj < used) & (kj < used) & (k_rank <= q_rank)
            valid_ref[at] = jnp.where(good, 1, 0)
        position = (sel_ref[r : r + 1, :] + ranks[0] * SPAN).astype(jnp.float32)
        angle = jnp.broadcast_to(position, (SEL, HD)).T * freq
        cos_ref[r * SEL : (r + 1) * SEL, :] = jnp.cos(angle)
        sin_ref[r * SEL : (r + 1) * SEL, :] = jnp.sin(angle) * sign


def prepare(*args):
    shape = jax.ShapeDtypeStruct
    return pl.pallas_call(
        prepare_kernel,
        out_shape=(
            shape((ROWS, HD), jnp.float32),
            shape((ROWS, HD), jnp.float32),
            shape((6,), jnp.int32),
            shape((16,), jnp.int32),
        ),
        in_specs=[smem] * 3 + [vmem] * 2,
        out_specs=(vmem, vmem, smem, smem),
        compiler_params=pltpu.CompilerParams(vmem_limit_bytes=8 << 20),
        cost_estimate=work(2),
        name="prepare",
    )(*args)


def turned(v, cosine, sine):
    return v * cosine + pltpu.roll(v, HD // 2, 1) * sine


def weight_copies(sources, piece, i, to_ref, slot, sem):
    at = pl.ds(pl.multiple_of(piece * DK, DK), DK)
    start = 0
    for j, (w, width) in enumerate(zip(sources, (QW, HD, HD))):
        to = to_ref.at[slot, :, start : start + width]
        yield pltpu.make_async_copy(w.at[at, :], to, sem.at[i, j])
        start += width


def partial_kernel(which, ahead, carried, place, *refs):
    count = len(which) - ahead
    pieces, refs = refs[:count], refs[count:]
    sources, refs = refs[:3], refs[3:]
    if carried:
        acc_ref, refs = refs[0], refs[1:]
    out_ref, refs = refs[0], refs[1:]
    if ahead:
        next_ref, refs = refs[0], refs[1:]
    weight, sem = refs
    for i in range(count + ahead):
        to, slot = (weight, i) if i < count else (next_ref, i - count)
        for copy in weight_copies(sources, place[which[i]], i, to, slot, sem):
            copy.start()
    acc = acc_ref[...] if carried else None
    for i in range(count):
        for copy in weight_copies(sources, place[which[i]], i, weight, i, sem):
            copy.wait()
        d = jnp.dot(pieces[i][...], weight[i], preferred_element_type=jnp.float32)
        acc = d if acc is None else acc + d
    out_ref[...] = acc
    for i in range(count, count + ahead):
        for copy in weight_copies(sources, place[which[i]], i, next_ref, i - count, sem):
            copy.wait()


def partial_project(place, which, pieces, weights, acc=None, ahead=0):
    n = len(pieces)
    sums = jax.ShapeDtypeStruct((ROWS, QW + 2 * HD), jnp.float32)
    kept = jax.ShapeDtypeStruct((ahead, DK, QW + 2 * HD), jnp.bfloat16)
    extra = [] if acc is None else [acc]
    weights = [pltpu.with_memory_space_constraint(w, pltpu.HBM) for w in weights]
    return pl.pallas_call(
        functools.partial(partial_kernel, which, ahead, acc is not None),
        out_shape=(sums, kept) if ahead else sums,
        in_specs=[smem] + [vmem] * n + [hbm] * 3 + [vmem] * len(extra),
        out_specs=(vmem, vmem) if ahead else vmem,
        scratch_shapes=[
            pltpu.VMEM((n, DK, QW + 2 * HD), jnp.bfloat16),
            pltpu.SemaphoreType.DMA((n + ahead, 3)),
        ],
        compiler_params=pltpu.CompilerParams(vmem_limit_bytes=16 << 20),
        cost_estimate=work(6),
        name="project",
    )(place, *pieces, *weights, *extra)


def packed(n):
    parts = [n[g * FRESH : (g + 1) * FRESH, :] for g in range(HG)]
    return jnp.concatenate(parts, axis=1).astype(jnp.bfloat16)


def unpacked(n):
    return jnp.concatenate([n[:, g * HD : (g + 1) * HD] for g in range(HG)], axis=0)


def last_kernel(piece_ref, weight_ref, acc_ref, cos_ref, sin_ref, ring_ref, side_ref):
    acc = acc_ref[...] + jnp.dot(
        piece_ref[...], weight_ref[0], preferred_element_type=jnp.float32
    )
    for r, q_ref, n_ref in ((0, ring_ref, side_ref), (1, side_ref, ring_ref)):
        mine = acc[r * SEL : (r + 1) * SEL, :]
        cosine = cos_ref[r * SEL : (r + 1) * SEL, :]
        sine = sin_ref[r * SEL : (r + 1) * SEL, :]
        for g in range(HG):
            at = slice(g * HD, (g + 1) * HD)
            q_ref[:SEL, at] = turned(mine[:, at], cosine, sine).astype(jnp.bfloat16)
        n_ref[SEL : SEL + FRESH, :] = packed(turned(mine[:, QW : QW + HD], cosine, sine))
        n_ref[SEL + FRESH :, :] = packed(mine[:, QW + HD :])


def last_project(*args):
    shape = jax.ShapeDtypeStruct((SEND, QW), jnp.bfloat16)
    return pl.pallas_call(
        last_kernel,
        out_shape=(shape, shape),
        in_specs=[vmem] * 5,
        out_specs=(vmem, vmem),
        compiler_params=pltpu.CompilerParams(vmem_limit_bytes=16 << 20),
        cost_estimate=tiny,
        name="project_last",
    )(*args)


def attend_block(at, q_ref, keys, vals, limit, m_ref, l_ref, acc_ref):
    s = lax.dot_general(
        q_ref[at, :], keys, (((1,), (1,)), ((), ())), preferred_element_type=jnp.float32
    )
    if limit is not None:
        col = lax.broadcasted_iota(jnp.int32, s.shape, 1)
        s = jnp.where(col <= limit, s, low)
    old = m_ref[at, :]
    new = jnp.maximum(old, jnp.max(s, axis=1, keepdims=True))
    factor = jnp.exp2((old - new) * SCALE2)
    weight = jnp.exp2((s - new) * SCALE2)
    l_ref[at, :] = l_ref[at, :] * factor + jnp.sum(weight, axis=1, keepdims=True)
    acc_ref[at, :] = acc_ref[at, :] * factor + jnp.dot(
        weight.astype(jnp.bfloat16), vals, preferred_element_type=jnp.float32
    )
    m_ref[at, :] = new


def attend_source(rows_ref, i, jk_ref, jv_ref, spans, valid_ref, first, o_ref, state, limit_ref):
    m_ref, l_ref, acc_ref = state
    m_ref[...] = jnp.full_like(m_ref, low)
    l_ref[...] = jnp.zeros_like(l_ref)
    acc_ref[...] = jnp.zeros_like(acc_ref)

    def span(step, _):
        sp = step // 2

        @pl.when(valid_ref[first + sp] != 0)
        def _():
            at = pl.ds(pl.multiple_of((step % 2) * 2 * SEL, 2 * SEL), 2 * SEL)
            limit = None
            if limit_ref is not None:
                limit = jnp.where((sp == 0) & (i == 0), limit_ref[at, :], SPAN)
            attend_block(
                at, rows_ref.at[i], jk_ref[sp], jv_ref[sp], limit, m_ref, l_ref, acc_ref
            )

        return 0

    lax.fori_loop(0, 2 * spans, span, 0)
    l = l_ref[...]
    some = l > 0.0
    mixed = acc_ref[...] / jnp.where(some, l, 1.0)
    lse = jnp.where(some, m_ref[...] * SCALE2 + jnp.log2(jnp.where(some, l, 1.0)), low)
    lane = lax.broadcasted_iota(jnp.int32, (SEL, HD), 1)
    stat = jnp.zeros((SEL, HD), jnp.float32)
    for g in range(HG):
        o_ref[i, :SEL, g * HD : (g + 1) * HD] = mixed[g * SEL : (g + 1) * SEL].astype(jnp.bfloat16)
        rest = lse[g * SEL : (g + 1) * SEL]
        for k in range(3):
            part = rest.astype(jnp.bfloat16).astype(jnp.float32)
            stat = jnp.where(lane == k * HG + g, part, stat)
            rest = rest - part
    o_ref[i, SEL:, :HD] = stat.T[:16].astype(jnp.bfloat16)
    o_ref[i, SEL:, HD:] = jnp.zeros((16, QW - HD), jnp.bfloat16)


def spread(rows_ref, i, q):
    for g in range(HG):
        rows_ref[i, g * SEL : (g + 1) * SEL, :] = q[:, g * HD : (g + 1) * HD]


def join_span(kv_ref, n_ref, rank, freq_ref, jk_ref, jv_ref, sp):
    freq = freq_ref[0:1, :]
    sign = freq_ref[1:2, :]
    extra = kv_ref[2 * SPAN :, :].astype(jnp.float32)
    sel = (extra[0:1, :] * 8.0 + extra[1:2, :]).astype(jnp.int32)
    offset = (extra[2:3, :] * 64.0 + extra[3:4, :]).astype(jnp.int32)
    angle = (rank * SPAN - offset).astype(jnp.float32) * freq
    cached = turned(kv_ref[:SPAN, :].astype(jnp.float32), jnp.cos(angle), jnp.sin(angle) * sign)
    at = lax.broadcasted_iota(jnp.int32, (SPAN, SEL), 0)
    pick = (at == sel).astype(jnp.float32).astype(jnp.bfloat16)
    ones = jnp.ones((SEL, HD), jnp.bfloat16)
    hit = jnp.dot(pick, ones, preferred_element_type=jnp.float32) > 0.5
    fresh_k = unpacked(n_ref[SEL : SEL + FRESH, :])
    fresh_v = unpacked(n_ref[SEL + FRESH :, :])
    put_k = jnp.dot(pick, fresh_k, preferred_element_type=jnp.float32)
    put_v = jnp.dot(pick, fresh_v, preferred_element_type=jnp.float32)
    vals = kv_ref[SPAN : 2 * SPAN, :].astype(jnp.float32)
    jk_ref[sp] = jnp.where(hit, put_k, cached).astype(jnp.bfloat16)
    jv_ref[sp] = jnp.where(hit, put_v, vals).astype(jnp.bfloat16)


def set_limit(sel_ref, r, limit_ref):
    sel = sel_ref[r : r + 1, :].astype(jnp.float32)
    column = jnp.broadcast_to(sel, (SEL, SEL)).T[:, :1].astype(jnp.int32)
    limit_ref[...] = jnp.concatenate([column] * HG, axis=0)


def join_kernel(rank_ref, kv0, kv1, n0, n1, freq_ref, jk_ref, jv_ref):
    join_span(kv0, n0, rank_ref[0], freq_ref, jk_ref, jv_ref, 0)
    join_span(kv1, n1, rank_ref[1], freq_ref, jk_ref, jv_ref, 1)


def attend_kernel(shift, valid_ref, q_ref, jk_ref, jv_ref, *refs):
    limit_ref = None
    if shift == 0:
        sel_ref, refs = refs[0], refs[1:]
        limit_ref, refs = refs[-1], refs[:-1]
        set_limit(sel_ref, 0, limit_ref)
    o_ref, rows_ref, state = refs[0], refs[1], refs[2:]
    spread(rows_ref, 0, q_ref[:SEL, :])
    attend_source(
        rows_ref, 0, jk_ref, jv_ref, 2, valid_ref, shift * 2, o_ref, state, limit_ref
    )


def cover_kernel(step, valid_ref, rank_ref, q0, q1, kv_ref, n_ref, freq_ref, *refs):
    limit_ref = None
    if step == 0:
        sel_ref, refs = refs[0], refs[1:]
        limit_ref, refs = refs[-1], refs[:-1]
        set_limit(sel_ref, 1, limit_ref)
    o_ref, jk_ref, jv_ref, rows_ref, state = *refs[:4], refs[4:]
    join_span(kv_ref, n_ref, rank_ref[2 + step], freq_ref, jk_ref, jv_ref, 0)
    for i, q in enumerate((q0, q1)):
        spread(rows_ref, i, q[:SEL, :])

    def source(i, _):
        attend_source(
            rows_ref, i, jk_ref, jv_ref, 1, valid_ref, 8 + step * 2 + i, o_ref, state, limit_ref
        )
        return 0

    lax.fori_loop(0, 2, source, 0)


joined_shape = jax.ShapeDtypeStruct((2, SPAN, HD), jnp.bfloat16)
one_packed = jax.ShapeDtypeStruct((1, PACK, QW), jnp.bfloat16)
two_packed = jax.ShapeDtypeStruct((2, PACK, QW), jnp.bfloat16)
state_scratch = [
    pltpu.VMEM((HG * SEL, 1), jnp.float32),
    pltpu.VMEM((HG * SEL, 1), jnp.float32),
    pltpu.VMEM((HG * SEL, HD), jnp.float32),
]
limit_scratch = [pltpu.VMEM((HG * SEL, 1), jnp.int32)]


def join(*args):
    return pl.pallas_call(
        join_kernel,
        out_shape=(joined_shape, joined_shape),
        in_specs=[smem] + [vmem] * 5,
        out_specs=(vmem, vmem),
        compiler_params=pltpu.CompilerParams(vmem_limit_bytes=16 << 20),
        cost_estimate=work(1),
        name="join",
    )(*args)


def attend(shift, valid, *args):
    return pl.pallas_call(
        functools.partial(attend_kernel, shift),
        out_shape=one_packed,
        in_specs=[smem] + [vmem] * len(args),
        out_specs=vmem,
        scratch_shapes=[pltpu.VMEM((1, HG * SEL, HD), jnp.bfloat16)]
        + state_scratch
        + (limit_scratch if shift == 0 else []),
        compiler_params=pltpu.CompilerParams(vmem_limit_bytes=16 << 20),
        cost_estimate=work(4),
        name="attend",
    )(valid, *args)


def cover(step, *args):
    return pl.pallas_call(
        functools.partial(cover_kernel, step),
        out_shape=two_packed,
        in_specs=[smem] * 2 + [vmem] * (len(args) - 2),
        out_specs=vmem,
        scratch_shapes=[
            pltpu.VMEM((1, SPAN, HD), jnp.bfloat16),
            pltpu.VMEM((1, SPAN, HD), jnp.bfloat16),
            pltpu.VMEM((2, HG * SEL, HD), jnp.bfloat16),
        ]
        + state_scratch
        + (limit_scratch if step == 0 else []),
        compiler_params=pltpu.CompilerParams(vmem_limit_bytes=16 << 20),
        cost_estimate=tiny,
        name="cover",
    )(*args)


def merge_parts(parts, put, stat_put=None):
    lse = []
    for p in parts:
        stat = p[SEL:, :HD].astype(jnp.float32)
        lse.append(stat[0:4] + stat[4:8] + stat[8:12])
    top = functools.reduce(jnp.maximum, lse)
    weight = [jnp.exp2(v - top) for v in lse]
    total = functools.reduce(jnp.add, weight)
    pad = jnp.zeros((HD - HG, SEL), jnp.float32)
    weight = [jnp.concatenate([w / total, pad], axis=0).T for w in weight]
    for g in range(HG):
        at = slice(g * HD, (g + 1) * HD)
        mixed = jnp.zeros((SEL, HD), jnp.float32)
        for w, p in zip(weight, parts):
            mixed += w[:, g : g + 1] * p[:SEL, at].astype(jnp.float32)
        put(at, mixed.astype(jnp.bfloat16))
    if stat_put is not None:
        rest = top + jnp.log2(total)
        rows = []
        for _ in range(3):
            part = rest.astype(jnp.bfloat16).astype(jnp.float32)
            rows.append(part)
            rest = rest - part
        stat_put(jnp.concatenate(rows + [jnp.zeros_like(top)], axis=0).astype(jnp.bfloat16))


def between_kernel(at, *refs):
    o_ref = refs[-1]

    def put(lanes, value):
        o_ref[0, :SEL, lanes] = value

    def stat_put(value):
        o_ref[0, SEL:, :HD] = value
        o_ref[0, SEL:, HD:] = jnp.zeros((16, QW - HD), jnp.bfloat16)

    merge_parts([p.at[at] for p in refs[:-1]], put, stat_put)


def between(at, *parts):
    return pl.pallas_call(
        functools.partial(between_kernel, at),
        out_shape=one_packed,
        in_specs=[vmem] * len(parts),
        out_specs=vmem,
        compiler_params=pltpu.CompilerParams(vmem_limit_bytes=8 << 20),
        cost_estimate=work(1),
        name="merge_between",
    )(*parts)


def merge_kernel(*refs):
    o_ref = refs[-1]
    for r, parts in enumerate((refs[:2], refs[2:-1])):

        def put(at, value, r=r):
            o_ref[r * SEL : (r + 1) * SEL, at] = value

        merge_parts([p.at[0] for p in parts], put)


def merge(*parts):
    return pl.pallas_call(
        merge_kernel,
        out_shape=jax.ShapeDtypeStruct((ROWS, QW), jnp.bfloat16),
        in_specs=[vmem] * len(parts),
        out_specs=vmem,
        compiler_params=pltpu.CompilerParams(vmem_limit_bytes=8 << 20),
        cost_estimate=tiny,
        name="merge",
    )(*parts)


def after(value, *others):
    return lax.optimization_barrier((value, *others))[0]


def shards(
    hidden, w_query, w_key, w_value, key_cache, value_cache,
    span_count, span_key, cache_offset, sel_index,
):
    zh, yh, yp, c = (lax.axis_index(a) for a in ("zh", "yh", "yp", "c"))
    zl, x = lax.axis_index("zl"), lax.axis_index("x")
    weights = (w_query, w_key, w_value)
    way = 2 * c - 1
    entries = [zl * 4 + (x + i * way) % 4 for i in range(4)]
    entries += [(1 - zl) * 4 + (x + i * way) % 4 for i in range(4)]
    entries += [zh, yh, way, (yp * 2 + c) * SLOTS]
    place = jnp.stack(entries).astype(jnp.int32)
    half = np.arange(HD // 2) * 2.0 / HD
    freq = jnp.asarray(
        np.stack([np.tile(rope_base**-half, 2), np.repeat([-1.0, 1.0], HD // 2)]), jnp.float32
    )

    def held(r):
        sel = sel_index[r]
        offset = jnp.broadcast_to(cache_offset[r], (SEL,))
        extra = jnp.stack([sel // 8, sel % 8, offset // 64, offset % 64])
        extra = jnp.concatenate([extra, jnp.zeros((12, SEL), jnp.int32)], axis=0)
        rows = slice(r * SPAN, (r + 1) * SPAN)
        return jnp.concatenate(
            [key_cache[rows], value_cache[rows], extra.astype(jnp.bfloat16)], axis=0
        )

    h = [hidden, ring_x(hidden)]
    z = [pz(hidden)]
    kv_ring = [held(1)]
    for _ in range(3):
        kv_ring.append(ring_z(kv_ring[-1]))
    for _ in range(2):
        h.append(ring_x(h[-1]))
    for _ in range(3):
        z.append(ring_x(z[-1]))
    kv0 = held(0)
    kv1 = py(after(kv0, h[2]))
    cosine, sine, ranks, valid = prepare(
        after(place, h[2]), span_count, span_key, sel_index, freq
    )
    project = functools.partial(partial_project, place)
    acc = project((H_AT, H_AT + 1), (hidden, h[1]), weights)
    acc = project((H_AT + 2, Z_AT), (h[2], z[0]), weights, acc)
    acc = project((H_AT + 3, Z_AT + 1), (h[3], z[1]), weights, acc)
    acc = after(acc, kv_ring[2])
    acc, kept = project((Z_AT + 2, Z_AT + 3), (z[2],), weights, acc, ahead=1)
    acc = after(acc, kv1)
    send, side = last_project(z[3], kept, acc, cosine, sine)
    ring = [send]
    for _ in range(3):
        ring.append(ring_z(ring[-1]))
    side1 = py(side)
    jk, jv = join(ranks, kv0, kv1, side, side1, freq)
    own = attend(0, valid, after(send, kv_ring[3]), jk, jv, sel_index)
    out = attend(1, valid, after(ring[1], own), jk, jv)
    for i in (2, 3):
        out = between(0, attend(i, valid, ring[i], jk, jv), ring_z(out))
    covered = [
        cover(i, valid, ranks, side, side1, kv_ring[i], ring[i], freq, *([sel_index] * (i == 0)))
        for i in range(4)
    ]
    back = py(between(1, *covered))
    return merge(own, ring_z(out), *covered, back)


def solution(mesh):
    split = Mesh(mesh.devices.reshape(4, 2, 2, 2, 2, 4), AXES)
    seq, tp = AXES[:4], AXES[4:]
    placed = (
        P(seq, tp),
        P(None, tp),
        P(None, tp),
        P(None, tp),
        P(seq, tp),
        P(seq, tp),
        P(),
        P(),
        P(seq),
        P(seq, None),
    )
    return jax.shard_map(
        shards, mesh=split, in_specs=placed, out_specs=P(seq, tp), check_vma=False
    )
```

```python
import functools
import math

import jax
import jax.numpy as jnp
import numpy as np
from jax import lax
from jax.experimental import pallas as pl
from jax.experimental.pallas import tpu as pltpu
from jax.sharding import Mesh, PartitionSpec as P

HD = 128
HG = 4
R = 8
MAXCH = 8
SPAN = 1024
SEL = 128
SLOTS = 2
ROWS = SLOTS * SEL
QW = HG * HD
PACK = SEL + 16
DK = 896
PROJ = 16

rope_base = 5000000.0
low = -1.0e30
SCALE2 = math.log2(math.e) / math.sqrt(HD)

vmem = pl.BlockSpec(memory_space=pltpu.VMEM)
smem = pl.BlockSpec(memory_space=pltpu.SMEM)
hbm = pl.BlockSpec(memory_space=pltpu.HBM)
tiny = pl.CostEstimate(flops=1, bytes_accessed=1, transcendentals=0)


def work(microseconds):
    return pl.CostEstimate(
        flops=microseconds * 1000000000, bytes_accessed=1, transcendentals=0
    )


AXES = ("zh", "yh", "yp", "c", "zl", "x")


def opposite_ways(n):
    plus = [(i, (i + 1) % n) for i in range(n)]
    minus = [(n + i, n + (i - 1) % n) for i in range(n)]
    return plus + minus


def ring_x(v):
    return lax.ppermute(v, ("c", "x"), opposite_ways(4))


def ring_z(v):
    pairs = [(2 * i + c, 2 * ((i + 1 - 2 * c) % 4) + c) for i in range(4) for c in range(2)]
    return lax.ppermute(v, ("zh", "c"), pairs)


def pz(v):
    return lax.ppermute(v, "zl", [(0, 1), (1, 0)])


def py(v):
    return lax.ppermute(v, "yh", [(0, 1), (1, 0)])


H_AT, Z_AT, ZH_AT, YH_AT, WAY_AT, REQ_AT = 0, 4, 8, 9, 10, 11


def prepare_kernel(
    place, count, key, offset, sel_ref, theirs_ref, freq_ref,
    cos_ref, sin_ref, rot_ref, selr_ref, valid_ref,
):
    freq = freq_ref[0:1, :]
    sign = freq_ref[1:2, :]
    zh, yh, way = place[ZH_AT], place[YH_AT], place[WAY_AT]
    for r in range(SLOTS):
        request = place[REQ_AT] + r
        used = count[request]

        def rank(j, request=request, used=used):
            mine = key[request, j]
            total = jnp.int32(0)
            for k in range(MAXCH):
                smaller = (key[request, k] < mine) & (k < used)
                total += jnp.where(smaller, 1, 0)
            return total

        spans = (zh * 2 + yh, zh * 2 + 1 - yh)
        ranks = [rank(j) for j in spans]
        for shift in range(4):
            j = lax.rem(zh + shift * way + 4, 4) * 2 + yh
            mine = rank(j)
            for sp in range(2):
                good = (j < used) & (spans[sp] < used) & (ranks[sp] <= mine)
                valid_ref[shift * 4 + r * 2 + sp] = jnp.where(good, 1, 0)
        sel = sel_ref[r : r + 1, :]
        position = (sel + ranks[0] * SPAN).astype(jnp.float32)
        angle = jnp.broadcast_to(position, (SEL, HD)).T * freq
        cos_ref[r * SEL : (r + 1) * SEL, :] = jnp.cos(angle)
        sin_ref[r * SEL : (r + 1) * SEL, :] = jnp.sin(angle) * sign
        other = ranks[1] * SPAN - theirs_ref[SLOTS + r : SLOTS + r + 1, :]
        own = jnp.zeros((1, HD), jnp.int32) + (ranks[0] * SPAN - offset[r])
        for sp, delta in enumerate((own, other)):
            angle = delta.astype(jnp.float32) * freq
            rot_ref[r, sp : sp + 1, :] = jnp.cos(angle)
            rot_ref[r, sp + 2 : sp + 3, :] = jnp.sin(angle) * sign
        selr_ref[r, 0:1, :] = sel
        selr_ref[r, 1:2, :] = theirs_ref[r : r + 1, :]


def prepare(*args):
    half = np.arange(HD // 2) * 2.0 / HD
    freq = np.tile(rope_base**-half, 2)
    sign = np.repeat([-1.0, 1.0], HD // 2)
    table = jnp.asarray(np.stack([freq, sign]), jnp.float32)
    shape = jax.ShapeDtypeStruct
    return pl.pallas_call(
        prepare_kernel,
        out_shape=(
            shape((ROWS, HD), jnp.float32),
            shape((ROWS, HD), jnp.float32),
            shape((SLOTS, 4, HD), jnp.float32),
            shape((SLOTS, 2, SEL), jnp.int32),
            shape((16,), jnp.int32),
        ),
        in_specs=[smem] * 4 + [vmem] * 3,
        out_specs=(vmem,) * 4 + (smem,),
        compiler_params=pltpu.CompilerParams(vmem_limit_bytes=8 << 20),
        cost_estimate=work(2),
        name="prepare",
    )(*args, table)


def turned(v, cosine, sine):
    return v * cosine + pltpu.roll(v, HD // 2, 1) * sine


def weight_copies(sources, piece, i, to_ref, slot, sem):
    at = pl.ds(pl.multiple_of(piece * DK, DK), DK)
    start = 0
    for j, (w, width) in enumerate(zip(sources, (QW, HD, HD))):
        to = to_ref.at[slot, :, start : start + width]
        yield pltpu.make_async_copy(w.at[at, :], to, sem.at[i, j])
        start += width


def partial_kernel(which, ahead, carried, place, *refs):
    count = len(which) - ahead
    pieces, refs = refs[:count], refs[count:]
    sources, refs = refs[:3], refs[3:]
    if carried:
        acc_ref, refs = refs[0], refs[1:]
    out_ref, refs = refs[0], refs[1:]
    if ahead:
        next_ref, refs = refs[0], refs[1:]
    weight, sem = refs
    for i in range(count + ahead):
        to, slot = (weight, i) if i < count else (next_ref, i - count)
        for copy in weight_copies(sources, place[which[i]], i, to, slot, sem):
            copy.start()
    acc = acc_ref[...] if carried else None
    for i in range(count):
        for copy in weight_copies(sources, place[which[i]], i, weight, i, sem):
            copy.wait()
        d = jnp.dot(pieces[i][...], weight[i], preferred_element_type=jnp.float32)
        acc = d if acc is None else acc + d
    out_ref[...] = acc
    for i in range(count, count + ahead):
        for copy in weight_copies(sources, place[which[i]], i, next_ref, i - count, sem):
            copy.wait()


def partial_project(place, which, pieces, weights, acc=None, ahead=0):
    n = len(pieces)
    sums = jax.ShapeDtypeStruct((ROWS, QW + 2 * HD), jnp.float32)
    kept = jax.ShapeDtypeStruct((ahead, DK, QW + 2 * HD), jnp.bfloat16)
    extra = [] if acc is None else [acc]
    weights = [pltpu.with_memory_space_constraint(w, pltpu.HBM) for w in weights]
    return pl.pallas_call(
        functools.partial(partial_kernel, which, ahead, acc is not None),
        out_shape=(sums, kept) if ahead else sums,
        in_specs=[smem] + [vmem] * n + [hbm] * 3 + [vmem] * len(extra),
        out_specs=(vmem, vmem) if ahead else vmem,
        scratch_shapes=[
            pltpu.VMEM((n, DK, QW + 2 * HD), jnp.bfloat16),
            pltpu.SemaphoreType.DMA((n + ahead, 3)),
        ],
        compiler_params=pltpu.CompilerParams(vmem_limit_bytes=16 << 20),
        cost_estimate=work(6),
        name="project",
    )(place, *pieces, *weights, *extra)


def last_kernel(piece_ref, weight_ref, acc_ref, cos_ref, sin_ref, q_ref, n_ref):
    acc = acc_ref[...] + jnp.dot(
        piece_ref[...], weight_ref[0], preferred_element_type=jnp.float32
    )
    cosine, sine = cos_ref[...], sin_ref[...]
    for g in range(HG):
        at = slice(g * HD, (g + 1) * HD)
        q_ref[:, at] = turned(acc[:, at], cosine, sine).astype(jnp.bfloat16)
    n_ref[:ROWS, :] = turned(acc[:, QW : QW + HD], cosine, sine).astype(jnp.bfloat16)
    n_ref[ROWS:, :] = acc[:, QW + HD :].astype(jnp.bfloat16)


def last_project(*args):
    return pl.pallas_call(
        last_kernel,
        out_shape=(
            jax.ShapeDtypeStruct((ROWS, QW), jnp.bfloat16),
            jax.ShapeDtypeStruct((2 * ROWS, HD), jnp.bfloat16),
        ),
        in_specs=[vmem] * 5,
        out_specs=(vmem, vmem),
        compiler_params=pltpu.CompilerParams(vmem_limit_bytes=16 << 20),
        cost_estimate=tiny,
        name="project_last",
    )(*args)


def attend_block(q, keys, vals, limit, m_ref, l_ref, acc_ref):
    s = lax.dot_general(keys, q, (((1,), (1,)), ((), ())), preferred_element_type=jnp.float32)
    if limit is not None:
        at = lax.broadcasted_iota(jnp.int32, s.shape, 0)
        s = jnp.where(at <= limit, s, low)
    old = m_ref[...]
    new = jnp.maximum(old, jnp.max(s, axis=0, keepdims=True))
    factor = jnp.exp2((old - new) * SCALE2)
    weight = jnp.exp2((s - new) * SCALE2)
    l_ref[...] = l_ref[...] * factor + jnp.sum(weight, axis=0, keepdims=True)
    acc_ref[...] = acc_ref[...] * factor + lax.dot_general(
        vals,
        weight.astype(jnp.bfloat16),
        (((0,), (0,)), ((), ())),
        preferred_element_type=jnp.float32,
    )
    m_ref[...] = new


def attend_source(rows_ref, i, jk_ref, jv_ref, r, valid_ref, first, o_ref, state, limit_ref=None):
    m_ref, l_ref, acc_ref = state
    m_ref[...] = jnp.full_like(m_ref, low)
    l_ref[...] = jnp.zeros_like(l_ref)
    acc_ref[...] = jnp.zeros_like(acc_ref)

    def span(sp, _):
        @pl.when(valid_ref[first + sp] != 0)
        def _():
            limit = None if limit_ref is None else jnp.where(sp == 0, limit_ref[...], SPAN)
            attend_block(
                rows_ref[i], jk_ref[r * 2 + sp], jv_ref[r * 2 + sp], limit, m_ref, l_ref, acc_ref
            )

        return 0

    lax.fori_loop(0, 2, span, 0)
    l = l_ref[...]
    some = l > 0.0
    mixed = acc_ref[...] / jnp.where(some, l, 1.0)
    rest = jnp.where(some, m_ref[...] * SCALE2 + jnp.log2(jnp.where(some, l, 1.0)), low)
    rows = []
    for k in range(3):
        part = rest.astype(jnp.bfloat16).astype(jnp.float32)
        rows += [part[:, g * SEL : (g + 1) * SEL] for g in range(HG)]
        rest = rest - part
    for g in range(HG):
        at = slice(g * SEL, (g + 1) * SEL)
        o_ref[i, :SEL, g * HD : (g + 1) * HD] = mixed[:, at].T.astype(jnp.bfloat16)
    stat = jnp.concatenate(rows + [jnp.zeros((HG, SEL), jnp.float32)], axis=0)
    o_ref[i, SEL:, :HD] = stat.astype(jnp.bfloat16)
    o_ref[i, SEL:, HD:] = jnp.zeros((16, QW - HD), jnp.bfloat16)


def spread(rows_ref, i, q):
    for g in range(HG):
        rows_ref[i, g * SEL : (g + 1) * SEL, :] = q[:, g * HD : (g + 1) * HD]


def join_kernel(k0, v0, k1, v1, n0, n1, selr_ref, rot_ref, jk_ref, jv_ref):
    def request(r, _):
        base = pl.ds(pl.multiple_of(r * SPAN, SPAN), SPAN)
        fresh_k = pl.ds(pl.multiple_of(r * SEL, SEL), SEL)
        fresh_v = pl.ds(pl.multiple_of(ROWS + r * SEL, SEL), SEL)
        for sp, (kr, vr, nr) in enumerate(((k0, v0, n0), (k1, v1, n1))):
            cached = turned(
                kr[base, :].astype(jnp.float32),
                rot_ref[r, sp : sp + 1, :],
                rot_ref[r, sp + 2 : sp + 3, :],
            )
            at = lax.broadcasted_iota(jnp.int32, (SPAN, SEL), 0)
            pick = (at == selr_ref[r, sp : sp + 1, :]).astype(jnp.float32).astype(jnp.bfloat16)
            ones = jnp.ones((SEL, HD), jnp.bfloat16)
            hit = jnp.dot(pick, ones, preferred_element_type=jnp.float32) > 0.5
            put_k = jnp.dot(pick, nr[fresh_k, :], preferred_element_type=jnp.float32)
            put_v = jnp.dot(pick, nr[fresh_v, :], preferred_element_type=jnp.float32)
            vals = vr[base, :].astype(jnp.float32)
            jk_ref[r * 2 + sp] = jnp.where(hit, put_k, cached).astype(jnp.bfloat16)
            jv_ref[r * 2 + sp] = jnp.where(hit, put_v, vals).astype(jnp.bfloat16)
        return 0

    lax.fori_loop(0, SLOTS, request, 0)


def attend_kernel(shift, valid_ref, q_ref, jk_ref, jv_ref, *refs):
    if shift == 0:
        selr_ref, o_ref, rows_ref, limit_ref = refs[:4]
        state = refs[4:]
    else:
        o_ref, rows_ref = refs[:2]
        limit_ref, state = None, refs[2:]
    for r in range(SLOTS):
        spread(rows_ref, r, q_ref[r * SEL : (r + 1) * SEL, :])

    def request(r, _):
        if shift == 0:
            limit_ref[...] = jnp.concatenate([selr_ref[r, 0:1, :]] * HG, axis=1)
        attend_source(
            rows_ref, r, jk_ref, jv_ref, r, valid_ref, shift * 4 + r * 2, o_ref, state, limit_ref
        )
        return 0

    lax.fori_loop(0, SLOTS, request, 0)


joined_shape = jax.ShapeDtypeStruct((SLOTS * 2, SPAN, HD), jnp.bfloat16)
packed_shape = jax.ShapeDtypeStruct((SLOTS, PACK, QW), jnp.bfloat16)


def join(*args):
    return pl.pallas_call(
        join_kernel,
        out_shape=(joined_shape, joined_shape),
        in_specs=[vmem] * 8,
        out_specs=(vmem, vmem),
        compiler_params=pltpu.CompilerParams(vmem_limit_bytes=16 << 20),
        cost_estimate=work(3),
        name="join",
    )(*args)


def attend(shift, valid, *args):
    return pl.pallas_call(
        functools.partial(attend_kernel, shift),
        out_shape=packed_shape,
        in_specs=[smem] + [vmem] * len(args),
        out_specs=vmem,
        scratch_shapes=[pltpu.VMEM((SLOTS, HG * SEL, HD), jnp.bfloat16)]
        + ([pltpu.VMEM((1, HG * SEL), jnp.int32)] if shift == 0 else [])
        + [
            pltpu.VMEM((1, HG * SEL), jnp.float32),
            pltpu.VMEM((1, HG * SEL), jnp.float32),
            pltpu.VMEM((HD, HG * SEL), jnp.float32),
        ],
        compiler_params=pltpu.CompilerParams(vmem_limit_bytes=16 << 20),
        cost_estimate=work(4),
        name="attend",
    )(valid, *args)


def merge_parts(parts, put, stat_put=None):
    lse = []
    for p in parts:
        stat = p[SEL:, :HD].astype(jnp.float32)
        lse.append(stat[0:4] + stat[4:8] + stat[8:12])
    top = functools.reduce(jnp.maximum, lse)
    weight = [jnp.exp2(v - top) for v in lse]
    total = functools.reduce(jnp.add, weight)
    pad = jnp.zeros((HD - HG, SEL), jnp.float32)
    weight = [jnp.concatenate([w / total, pad], axis=0).T for w in weight]
    for g in range(HG):
        at = slice(g * HD, (g + 1) * HD)
        mixed = jnp.zeros((SEL, HD), jnp.float32)
        for w, p in zip(weight, parts):
            mixed += w[:, g : g + 1] * p[:SEL, at].astype(jnp.float32)
        put(at, mixed.astype(jnp.bfloat16))
    if stat_put is not None:
        rest = top + jnp.log2(total)
        rows = []
        for _ in range(3):
            part = rest.astype(jnp.bfloat16).astype(jnp.float32)
            rows.append(part)
            rest = rest - part
        stat_put(jnp.concatenate(rows + [jnp.zeros_like(top)], axis=0).astype(jnp.bfloat16))


def between_kernel(a_ref, b_ref, o_ref):
    for r in range(SLOTS):

        def put(at, value, r=r):
            o_ref[r, :SEL, at] = value

        def stat_put(value, r=r):
            o_ref[r, SEL:, :HD] = value
            o_ref[r, SEL:, HD:] = jnp.zeros((16, QW - HD), jnp.bfloat16)

        merge_parts((a_ref.at[r], b_ref.at[r]), put, stat_put)


def between(*parts):
    return pl.pallas_call(
        between_kernel,
        out_shape=packed_shape,
        in_specs=[vmem] * 2,
        out_specs=vmem,
        compiler_params=pltpu.CompilerParams(vmem_limit_bytes=8 << 20),
        cost_estimate=work(1),
        name="merge_between",
    )(*parts)


def merge_kernel(a_ref, b_ref, o_ref):
    for r in range(SLOTS):

        def put(at, value, r=r):
            o_ref[r * SEL : (r + 1) * SEL, at] = value

        merge_parts((a_ref.at[r], b_ref.at[r]), put)


def merge(*parts):
    return pl.pallas_call(
        merge_kernel,
        out_shape=jax.ShapeDtypeStruct((ROWS, QW), jnp.bfloat16),
        in_specs=[vmem] * 2,
        out_specs=vmem,
        compiler_params=pltpu.CompilerParams(vmem_limit_bytes=8 << 20),
        cost_estimate=tiny,
        name="merge",
    )(*parts)


def after(value, *others):
    return lax.optimization_barrier((value, *others))[0]


def shards(
    hidden, w_query, w_key, w_value, key_cache, value_cache,
    span_count, span_key, cache_offset, sel_index,
):
    zh, yh, yp, c = (lax.axis_index(a) for a in ("zh", "yh", "yp", "c"))
    zl, x = lax.axis_index("zl"), lax.axis_index("x")
    weights = (w_query, w_key, w_value)
    way = 2 * c - 1
    entries = [zl * 4 + (x + i * way) % 4 for i in range(4)]
    entries += [(1 - zl) * 4 + (x + i * way) % 4 for i in range(4)]
    entries += [zh, yh, way, (yp * 2 + c) * SLOTS]
    place = jnp.stack(entries).astype(jnp.int32)
    mine = jnp.concatenate(
        [sel_index, jnp.broadcast_to(cache_offset[:, None], (SLOTS, SEL))], axis=0
    )
    h = [hidden, ring_x(hidden)]
    z = [pz(hidden)]
    k1 = py(key_cache)
    project = functools.partial(partial_project, place)
    acc = project((H_AT, H_AT + 1), (hidden, h[1]), weights)
    for _ in range(2):
        h.append(ring_x(h[-1]))
    z.append(ring_x(after(z[0], acc)))
    z.append(ring_x(z[1]))
    z.append(pz(h[3]))
    theirs = py(after(mine, h[2]))
    v1 = py(after(value_cache, k1))
    cosine, sine, rot, sel_rows, valid = prepare(
        after(place, h[3]), span_count, span_key, cache_offset, sel_index, theirs
    )
    acc = project((H_AT + 2, Z_AT), (h[2], z[0]), weights, acc)
    acc = project((H_AT + 3, Z_AT + 1), (h[3], z[1]), weights, acc)
    acc, kept = project((Z_AT + 2, Z_AT + 3), (z[2],), weights, acc, ahead=1)
    acc = after(acc, k1, v1)
    query, fresh = last_project(z[3], kept, acc, cosine, sine)
    ring = [query]
    for _ in range(3):
        ring.append(ring_z(ring[-1]))
    jk, jv = join(key_cache, value_cache, k1, v1, fresh, py(fresh), sel_rows, rot)
    own = attend(0, valid, query, jk, jv, sel_rows)
    out = attend(1, valid, ring[1], jk, jv)
    for i in (2, 3):
        out = between(attend(i, valid, ring[i], jk, jv), ring_z(out))
    return merge(own, ring_z(out))


def solution(mesh):
    split = Mesh(mesh.devices.reshape(4, 2, 2, 2, 2, 4), AXES)
    seq, tp = AXES[:4], AXES[4:]
    placed = (
        P(seq, tp),
        P(None, tp),
        P(None, tp),
        P(None, tp),
        P(seq, tp),
        P(seq, tp),
        P(),
        P(),
        P(seq),
        P(seq, None),
    )
    return jax.shard_map(
        shards, mesh=split, in_specs=placed, out_specs=P(seq, tp), check_vma=False
    )
```

```python
import functools
import math

import jax
import jax.numpy as jnp
import numpy as np
from jax import lax
from jax.experimental import pallas as pl
from jax.experimental.pallas import tpu as pltpu
from jax.sharding import Mesh, PartitionSpec as P

HD = 128
HG = 4
R = 8
MAXCH = 8
SPAN = 1024
SEL = 128
SLOTS = 2
ROWS = SLOTS * SEL
QW = HG * HD
PACK = SEL + 16
DK = 896
PROJ = 16

rope_base = 5000000.0
low = -1.0e30
SCALE2 = math.log2(math.e) / math.sqrt(HD)

vmem = pl.BlockSpec(memory_space=pltpu.VMEM)
smem = pl.BlockSpec(memory_space=pltpu.SMEM)
hbm = pl.BlockSpec(memory_space=pltpu.HBM)
tiny = pl.CostEstimate(flops=1, bytes_accessed=1, transcendentals=0)


def work(microseconds):
    return pl.CostEstimate(
        flops=microseconds * 1000000000, bytes_accessed=1, transcendentals=0
    )


AXES = ("zh", "yh", "yp", "c", "zl", "x")


def opposite_ways(n):
    plus = [(i, (i + 1) % n) for i in range(n)]
    minus = [(n + i, n + (i - 1) % n) for i in range(n)]
    return plus + minus


def ring_x(v):
    return lax.ppermute(v, ("c", "x"), opposite_ways(4))


def ring_z(v):
    pairs = [(2 * i + c, 2 * ((i + 1 - 2 * c) % 4) + c) for i in range(4) for c in range(2)]
    return lax.ppermute(v, ("zh", "c"), pairs)


def back_z(v):
    pairs = [(2 * i + c, 2 * ((i - 1 + 2 * c) % 4) + c) for i in range(4) for c in range(2)]
    return lax.ppermute(v, ("zh", "c"), pairs)


def far_z(v):
    return lax.ppermute(v, "zh", [(i, (i + 2) % 4) for i in range(4)])


def pz(v):
    return lax.ppermute(v, "zl", [(0, 1), (1, 0)])


def py(v):
    return lax.ppermute(v, "yh", [(0, 1), (1, 0)])


H_AT, Z_AT, ZH_AT, YH_AT, WAY_AT, REQ_AT = 0, 4, 8, 9, 10, 11


def prepare_kernel(place, count, key, sel_ref, freq_ref, cos_ref, sin_ref, rank_ref, valid_ref):
    freq = freq_ref[0:1, :]
    sign = freq_ref[1:2, :]
    zh, yh, way = place[ZH_AT], place[YH_AT], place[WAY_AT]
    for r in range(SLOTS):
        request = place[REQ_AT] + r
        used = count[request]

        def rank(j, request=request, used=used):
            mine = key[request, j]
            total = jnp.int32(0)
            for k in range(MAXCH):
                smaller = (key[request, k] < mine) & (k < used)
                total += jnp.where(smaller, 1, 0)
            return total

        spans = (zh * 2 + yh, zh * 2 + 1 - yh)
        ranks = [rank(j) for j in spans]
        for sp in range(2):
            rank_ref[r * 2 + sp] = ranks[sp]
        for shift in range(4):
            j = lax.rem(zh + shift * way + 4, 4) * 2 + yh
            mine = rank(j)
            for sp in range(2):
                good = (j < used) & (spans[sp] < used) & (ranks[sp] <= mine)
                valid_ref[shift * 4 + r * 2 + sp] = jnp.where(good, 1, 0)
        position = (sel_ref[r : r + 1, :] + ranks[0] * SPAN).astype(jnp.float32)
        angle = jnp.broadcast_to(position, (SEL, HD)).T * freq
        cos_ref[r * SEL : (r + 1) * SEL, :] = jnp.cos(angle)
        sin_ref[r * SEL : (r + 1) * SEL, :] = jnp.sin(angle) * sign


def prepare(*args):
    shape = jax.ShapeDtypeStruct
    return pl.pallas_call(
        prepare_kernel,
        out_shape=(
            shape((ROWS, HD), jnp.float32),
            shape((ROWS, HD), jnp.float32),
            shape((4,), jnp.int32),
            shape((16,), jnp.int32),
        ),
        in_specs=[smem] * 3 + [vmem] * 2,
        out_specs=(vmem, vmem, smem, smem),
        compiler_params=pltpu.CompilerParams(vmem_limit_bytes=8 << 20),
        cost_estimate=work(2),
        name="prepare",
    )(*args)


def turned(v, cosine, sine):
    return v * cosine + pltpu.roll(v, HD // 2, 1) * sine


def weight_copies(sources, piece, i, to_ref, slot, sem):
    at = pl.ds(pl.multiple_of(piece * DK, DK), DK)
    start = 0
    for j, (w, width) in enumerate(zip(sources, (QW, HD, HD))):
        to = to_ref.at[slot, :, start : start + width]
        yield pltpu.make_async_copy(w.at[at, :], to, sem.at[i, j])
        start += width


def partial_kernel(which, ahead, carried, place, *refs):
    count = len(which) - ahead
    pieces, refs = refs[:count], refs[count:]
    sources, refs = refs[:3], refs[3:]
    if carried:
        acc_ref, refs = refs[0], refs[1:]
    out_ref, refs = refs[0], refs[1:]
    if ahead:
        next_ref, refs = refs[0], refs[1:]
    weight, sem = refs
    for i in range(count + ahead):
        to, slot = (weight, i) if i < count else (next_ref, i - count)
        for copy in weight_copies(sources, place[which[i]], i, to, slot, sem):
            copy.start()
    acc = acc_ref[...] if carried else None
    for i in range(count):
        for copy in weight_copies(sources, place[which[i]], i, weight, i, sem):
            copy.wait()
        d = jnp.dot(pieces[i][...], weight[i], preferred_element_type=jnp.float32)
        acc = d if acc is None else acc + d
    out_ref[...] = acc
    for i in range(count, count + ahead):
        for copy in weight_copies(sources, place[which[i]], i, next_ref, i - count, sem):
            copy.wait()


def partial_project(place, which, pieces, weights, acc=None, ahead=0):
    n = len(pieces)
    sums = jax.ShapeDtypeStruct((ROWS, QW + 2 * HD), jnp.float32)
    kept = jax.ShapeDtypeStruct((ahead, DK, QW + 2 * HD), jnp.bfloat16)
    extra = [] if acc is None else [acc]
    weights = [pltpu.with_memory_space_constraint(w, pltpu.HBM) for w in weights]
    return pl.pallas_call(
        functools.partial(partial_kernel, which, ahead, acc is not None),
        out_shape=(sums, kept) if ahead else sums,
        in_specs=[smem] + [vmem] * n + [hbm] * 3 + [vmem] * len(extra),
        out_specs=(vmem, vmem) if ahead else vmem,
        scratch_shapes=[
            pltpu.VMEM((n, DK, QW + 2 * HD), jnp.bfloat16),
            pltpu.SemaphoreType.DMA((n + ahead, 3)),
        ],
        compiler_params=pltpu.CompilerParams(vmem_limit_bytes=16 << 20),
        cost_estimate=work(6),
        name="project",
    )(place, *pieces, *weights, *extra)


def last_kernel(piece_ref, weight_ref, acc_ref, cos_ref, sin_ref, q_ref, n_ref):
    acc = acc_ref[...] + jnp.dot(
        piece_ref[...], weight_ref[0], preferred_element_type=jnp.float32
    )
    cosine, sine = cos_ref[...], sin_ref[...]
    for g in range(HG):
        at = slice(g * HD, (g + 1) * HD)
        q_ref[:, at] = turned(acc[:, at], cosine, sine).astype(jnp.bfloat16)
    n_ref[:ROWS, :] = turned(acc[:, QW : QW + HD], cosine, sine).astype(jnp.bfloat16)
    n_ref[ROWS:, :] = acc[:, QW + HD :].astype(jnp.bfloat16)


def last_project(*args):
    return pl.pallas_call(
        last_kernel,
        out_shape=(
            jax.ShapeDtypeStruct((ROWS, QW), jnp.bfloat16),
            jax.ShapeDtypeStruct((2 * ROWS, HD), jnp.bfloat16),
        ),
        in_specs=[vmem] * 5,
        out_specs=(vmem, vmem),
        compiler_params=pltpu.CompilerParams(vmem_limit_bytes=16 << 20),
        cost_estimate=tiny,
        name="project_last",
    )(*args)


def attend_block(q, keys, vals, limit, m_ref, l_ref, acc_ref):
    s = lax.dot_general(keys, q, (((1,), (1,)), ((), ())), preferred_element_type=jnp.float32)
    if limit is not None:
        at = lax.broadcasted_iota(jnp.int32, s.shape, 0)
        s = jnp.where(at <= limit, s, low)
    old = m_ref[...]
    new = jnp.maximum(old, jnp.max(s, axis=0, keepdims=True))
    factor = jnp.exp2((old - new) * SCALE2)
    weight = jnp.exp2((s - new) * SCALE2)
    l_ref[...] = l_ref[...] * factor + jnp.sum(weight, axis=0, keepdims=True)
    acc_ref[...] = acc_ref[...] * factor + lax.dot_general(
        vals,
        weight.astype(jnp.bfloat16),
        (((0,), (0,)), ((), ())),
        preferred_element_type=jnp.float32,
    )
    m_ref[...] = new


def attend_source(rows_ref, i, jk_ref, jv_ref, r, valid_ref, first, o_ref, state, limit_ref=None):
    m_ref, l_ref, acc_ref = state
    m_ref[...] = jnp.full_like(m_ref, low)
    l_ref[...] = jnp.zeros_like(l_ref)
    acc_ref[...] = jnp.zeros_like(acc_ref)

    def span(sp, _):
        @pl.when(valid_ref[first + sp] != 0)
        def _():
            limit = None if limit_ref is None else jnp.where(sp == 0, limit_ref[...], SPAN)
            attend_block(
                rows_ref[i], jk_ref[r * 2 + sp], jv_ref[r * 2 + sp], limit, m_ref, l_ref, acc_ref
            )

        return 0

    lax.fori_loop(0, 2, span, 0)
    l = l_ref[...]
    some = l > 0.0
    mixed = acc_ref[...] / jnp.where(some, l, 1.0)
    rest = jnp.where(some, m_ref[...] * SCALE2 + jnp.log2(jnp.where(some, l, 1.0)), low)
    rows = []
    for k in range(3):
        part = rest.astype(jnp.bfloat16).astype(jnp.float32)
        rows += [part[:, g * SEL : (g + 1) * SEL] for g in range(HG)]
        rest = rest - part
    for g in range(HG):
        at = slice(g * SEL, (g + 1) * SEL)
        o_ref[i, :SEL, g * HD : (g + 1) * HD] = mixed[:, at].T.astype(jnp.bfloat16)
    stat = jnp.concatenate(rows + [jnp.zeros((HG, SEL), jnp.float32)], axis=0)
    o_ref[i, SEL:, :HD] = stat.astype(jnp.bfloat16)
    o_ref[i, SEL:, HD:] = jnp.zeros((16, QW - HD), jnp.bfloat16)


def spread(rows_ref, i, q):
    for g in range(HG):
        rows_ref[i, g * SEL : (g + 1) * SEL, :] = q[:, g * HD : (g + 1) * HD]


def join_kernel(rank_ref, k0, v0, k1, v1, n0, n1, mine, theirs, freq_ref, jk_ref, jv_ref):
    freq = freq_ref[0:1, :]
    sign = freq_ref[1:2, :]
    for r in range(SLOTS):
        rows = slice(r * SPAN, (r + 1) * SPAN)
        for sp, (kr, vr, nr, here) in enumerate(((k0, v0, n0, mine), (k1, v1, n1, theirs))):
            offset = here[SLOTS + r : SLOTS + r + 1, :]
            angle = (rank_ref[r * 2 + sp] * SPAN - offset).astype(jnp.float32) * freq
            raw = kr[rows, :].astype(jnp.float32)
            cached = turned(raw, jnp.cos(angle), jnp.sin(angle) * sign)
            at = lax.broadcasted_iota(jnp.int32, (SPAN, SEL), 0)
            pick = (at == here[r : r + 1, :]).astype(jnp.float32).astype(jnp.bfloat16)
            ones = jnp.ones((SEL, HD), jnp.bfloat16)
            hit = jnp.dot(pick, ones, preferred_element_type=jnp.float32) > 0.5
            fresh_k = nr[r * SEL : (r + 1) * SEL, :]
            fresh_v = nr[ROWS + r * SEL : ROWS + (r + 1) * SEL, :]
            put_k = jnp.dot(pick, fresh_k, preferred_element_type=jnp.float32)
            put_v = jnp.dot(pick, fresh_v, preferred_element_type=jnp.float32)
            vals = vr[rows, :].astype(jnp.float32)
            jk_ref[r * 2 + sp] = jnp.where(hit, put_k, cached).astype(jnp.bfloat16)
            jv_ref[r * 2 + sp] = jnp.where(hit, put_v, vals).astype(jnp.bfloat16)


def attend_kernel(shift, valid_ref, q_ref, jk_ref, jv_ref, *refs):
    if shift == 0:
        sel_ref, o_ref, rows_ref, limit_ref = refs[:4]
        state = refs[4:]
    else:
        o_ref, rows_ref = refs[:2]
        limit_ref, state = None, refs[2:]
    for r in range(SLOTS):
        spread(rows_ref, r, q_ref[r * SEL : (r + 1) * SEL, :])

    def request(r, _):
        if shift == 0:
            limit_ref[...] = jnp.concatenate([sel_ref[pl.ds(r, 1), :]] * HG, axis=1)
        attend_source(
            rows_ref, r, jk_ref, jv_ref, r, valid_ref, shift * 4 + r * 2, o_ref, state, limit_ref
        )
        return 0

    lax.fori_loop(0, SLOTS, request, 0)


joined_shape = jax.ShapeDtypeStruct((SLOTS * 2, SPAN, HD), jnp.bfloat16)
packed_shape = jax.ShapeDtypeStruct((SLOTS, PACK, QW), jnp.bfloat16)


def join(*args):
    return pl.pallas_call(
        join_kernel,
        out_shape=(joined_shape, joined_shape),
        in_specs=[smem] + [vmem] * 9,
        out_specs=(vmem, vmem),
        compiler_params=pltpu.CompilerParams(vmem_limit_bytes=16 << 20),
        cost_estimate=work(3),
        name="join",
    )(*args)


def attend(shift, valid, *args):
    return pl.pallas_call(
        functools.partial(attend_kernel, shift),
        out_shape=packed_shape,
        in_specs=[smem] + [vmem] * len(args),
        out_specs=vmem,
        scratch_shapes=[pltpu.VMEM((SLOTS, HG * SEL, HD), jnp.bfloat16)]
        + ([pltpu.VMEM((1, HG * SEL), jnp.int32)] if shift == 0 else [])
        + [
            pltpu.VMEM((1, HG * SEL), jnp.float32),
            pltpu.VMEM((1, HG * SEL), jnp.float32),
            pltpu.VMEM((HD, HG * SEL), jnp.float32),
        ],
        compiler_params=pltpu.CompilerParams(vmem_limit_bytes=16 << 20),
        cost_estimate=work(1),
        name="attend",
    )(valid, *args)


def merge_parts(parts, put):
    lse = []
    for p in parts:
        stat = p[SEL:, :HD].astype(jnp.float32)
        lse.append(stat[0:4] + stat[4:8] + stat[8:12])
    top = functools.reduce(jnp.maximum, lse)
    weight = [jnp.exp2(v - top) for v in lse]
    total = functools.reduce(jnp.add, weight)
    pad = jnp.zeros((HD - HG, SEL), jnp.float32)
    weight = [jnp.concatenate([w / total, pad], axis=0).T for w in weight]
    for g in range(HG):
        at = slice(g * HD, (g + 1) * HD)
        mixed = jnp.zeros((SEL, HD), jnp.float32)
        for w, p in zip(weight, parts):
            mixed += w[:, g : g + 1] * p[:SEL, at].astype(jnp.float32)
        put(at, mixed.astype(jnp.bfloat16))


def merge_kernel(*refs):
    o_ref = refs[-1]
    for r in range(SLOTS):

        def put(at, value, r=r):
            o_ref[r * SEL : (r + 1) * SEL, at] = value

        merge_parts([p.at[r] for p in refs[:-1]], put)


def merge(*parts):
    return pl.pallas_call(
        merge_kernel,
        out_shape=jax.ShapeDtypeStruct((ROWS, QW), jnp.bfloat16),
        in_specs=[vmem] * len(parts),
        out_specs=vmem,
        compiler_params=pltpu.CompilerParams(vmem_limit_bytes=8 << 20),
        cost_estimate=tiny,
        name="merge",
    )(*parts)


def after(value, *others):
    return lax.optimization_barrier((value, *others))[0]


def shards(
    hidden, w_query, w_key, w_value, key_cache, value_cache,
    span_count, span_key, cache_offset, sel_index,
):
    zh, yh, yp, c = (lax.axis_index(a) for a in ("zh", "yh", "yp", "c"))
    zl, x = lax.axis_index("zl"), lax.axis_index("x")
    weights = (w_query, w_key, w_value)
    way = 2 * c - 1
    entries = [zl * 4 + (x + i * way) % 4 for i in range(4)]
    entries += [(1 - zl) * 4 + (x + i * way) % 4 for i in range(4)]
    entries += [zh, yh, way, (yp * 2 + c) * SLOTS]
    place = jnp.stack(entries).astype(jnp.int32)
    mine = jnp.concatenate(
        [sel_index, jnp.broadcast_to(cache_offset[:, None], (SLOTS, SEL))], axis=0
    )
    half = np.arange(HD // 2) * 2.0 / HD
    freq = jnp.asarray(
        np.stack([np.tile(rope_base**-half, 2), np.repeat([-1.0, 1.0], HD // 2)]), jnp.float32
    )
    cosine, sine, ranks, valid = prepare(place, span_count, span_key, sel_index, freq)
    h = [hidden, ring_x(hidden)]
    z = [pz(hidden)]
    k1 = py(key_cache)
    project = functools.partial(partial_project, place)
    acc = project((H_AT, H_AT + 1), (hidden, h[1]), weights)
    h.append(ring_x(after(h[1], cosine)))
    h.append(ring_x(h[2]))
    z.append(ring_x(after(z[0], acc)))
    z.append(ring_x(z[1]))
    z.append(pz(h[3]))
    theirs = py(after(mine, h[3]))
    v1 = py(after(value_cache, k1, h[2]))
    acc = project((H_AT + 2, Z_AT), (h[2], z[0]), weights, acc)
    acc = project((H_AT + 3, Z_AT + 1), (h[3], z[1]), weights, acc)
    acc, kept = project((Z_AT + 2, Z_AT + 3), (z[2],), weights, acc, ahead=1)
    acc = after(acc, k1, v1, theirs)
    query, fresh = last_project(z[3], kept, acc, cosine, sine)
    near, behind = ring_z(query), back_z(query)
    far = ring_z(near)
    jk, jv = join(ranks, key_cache, value_cache, k1, v1, fresh, py(fresh), mine, theirs, freq)
    out_near = back_z(attend(1, valid, near, jk, jv))
    out_behind = ring_z(attend(3, valid, behind, jk, jv))
    out_far = far_z(attend(2, valid, far, jk, jv))
    own = attend(0, valid, query, jk, jv, mine)
    return merge(own, out_near, out_behind, out_far)


def solution(mesh):
    split = Mesh(mesh.devices.reshape(4, 2, 2, 2, 2, 4), AXES)
    seq, tp = AXES[:4], AXES[4:]
    placed = (
        P(seq, tp),
        P(None, tp),
        P(None, tp),
        P(None, tp),
        P(seq, tp),
        P(seq, tp),
        P(),
        P(),
        P(seq),
        P(seq, None),
    )
    return jax.shard_map(
        shards, mesh=split, in_specs=placed, out_specs=P(seq, tp), check_vma=False
    )
```

```python
import functools
import math

import jax
import jax.numpy as jnp
import numpy as np
from jax import lax
from jax.experimental import pallas as pl
from jax.experimental.pallas import tpu as pltpu
from jax.sharding import Mesh, PartitionSpec as P

HD = 128
HG = 4
R = 8
MAXCH = 8
SPAN = 1024
SEL = 128
SLOTS = 2
ROWS = SLOTS * SEL
QW = HG * HD
PACK = SEL + 16
DK = 896
PROJ = 16

rope_base = 5000000.0
low = -1.0e30
SCALE2 = math.log2(math.e) / math.sqrt(HD)

vmem = pl.BlockSpec(memory_space=pltpu.VMEM)
smem = pl.BlockSpec(memory_space=pltpu.SMEM)
hbm = pl.BlockSpec(memory_space=pltpu.HBM)
tiny = pl.CostEstimate(flops=1, bytes_accessed=1, transcendentals=0)


def work(microseconds):
    return pl.CostEstimate(
        flops=microseconds * 1000000000, bytes_accessed=1, transcendentals=0
    )


AXES = ("zh", "yh", "yp", "c", "zl", "x")


def opposite_ways(n):
    plus = [(i, (i + 1) % n) for i in range(n)]
    minus = [(n + i, n + (i - 1) % n) for i in range(n)]
    return plus + minus


def ring_x(v):
    return lax.ppermute(v, ("c", "x"), opposite_ways(4))


def back_x(v):
    pairs = [(4 * c + i, 4 * c + (i - 1 + 2 * c) % 4) for c in range(2) for i in range(4)]
    return lax.ppermute(v, ("c", "x"), pairs)


def ring_z(v):
    pairs = [(2 * i + c, 2 * ((i + 1 - 2 * c) % 4) + c) for i in range(4) for c in range(2)]
    return lax.ppermute(v, ("zh", "c"), pairs)


def back_z(v):
    pairs = [(2 * i + c, 2 * ((i - 1 + 2 * c) % 4) + c) for i in range(4) for c in range(2)]
    return lax.ppermute(v, ("zh", "c"), pairs)


def far_z(v):
    return lax.ppermute(v, "zh", [(i, (i + 2) % 4) for i in range(4)])


def pz(v):
    return lax.ppermute(v, "zl", [(0, 1), (1, 0)])


def py(v):
    return lax.ppermute(v, "yh", [(0, 1), (1, 0)])


H_AT, Z_AT, ZH_AT, YH_AT, WAY_AT, REQ_AT = 0, 4, 8, 9, 10, 11


def prepare_kernel(place, count, key, sel_ref, freq_ref, cos_ref, sin_ref, rank_ref, valid_ref):
    freq = freq_ref[0:1, :]
    sign = freq_ref[1:2, :]
    zh, yh, way = place[ZH_AT], place[YH_AT], place[WAY_AT]
    for r in range(SLOTS):
        request = place[REQ_AT] + r
        used = count[request]

        def rank(j, request=request, used=used):
            mine = key[request, j]
            total = jnp.int32(0)
            for k in range(MAXCH):
                smaller = (key[request, k] < mine) & (k < used)
                total += jnp.where(smaller, 1, 0)
            return total

        spans = (zh * 2 + yh, zh * 2 + 1 - yh)
        ranks = [rank(j) for j in spans]
        for sp in range(2):
            rank_ref[r * 2 + sp] = ranks[sp]
        for shift in range(4):
            j = lax.rem(zh + shift * way + 4, 4) * 2 + yh
            mine = rank(j)
            for sp in range(2):
                good = (j < used) & (spans[sp] < used) & (ranks[sp] <= mine)
                valid_ref[shift * 4 + r * 2 + sp] = jnp.where(good, 1, 0)
        position = (sel_ref[r : r + 1, :] + ranks[0] * SPAN).astype(jnp.float32)
        angle = jnp.broadcast_to(position, (SEL, HD)).T * freq
        cos_ref[r * SEL : (r + 1) * SEL, :] = jnp.cos(angle)
        sin_ref[r * SEL : (r + 1) * SEL, :] = jnp.sin(angle) * sign


def prepare(*args):
    shape = jax.ShapeDtypeStruct
    return pl.pallas_call(
        prepare_kernel,
        out_shape=(
            shape((ROWS, HD), jnp.float32),
            shape((ROWS, HD), jnp.float32),
            shape((4,), jnp.int32),
            shape((16,), jnp.int32),
        ),
        in_specs=[smem] * 3 + [vmem] * 2,
        out_specs=(vmem, vmem, smem, smem),
        compiler_params=pltpu.CompilerParams(vmem_limit_bytes=8 << 20),
        cost_estimate=work(2),
        name="prepare",
    )(*args)


def turned(v, cosine, sine):
    return v * cosine + pltpu.roll(v, HD // 2, 1) * sine


def weight_copies(sources, piece, i, to_ref, slot, sem):
    at = pl.ds(pl.multiple_of(piece * DK, DK), DK)
    start = 0
    for j, (w, width) in enumerate(zip(sources, (QW, HD, HD))):
        to = to_ref.at[slot, :, start : start + width]
        yield pltpu.make_async_copy(w.at[at, :], to, sem.at[i, j])
        start += width


def partial_kernel(which, ahead, carried, place, *refs):
    count = len(which) - ahead
    pieces, refs = refs[:count], refs[count:]
    sources, refs = refs[:3], refs[3:]
    if carried:
        acc_ref, refs = refs[0], refs[1:]
    out_ref, refs = refs[0], refs[1:]
    if ahead:
        next_ref, refs = refs[0], refs[1:]
    weight, sem = refs
    for i in range(count + ahead):
        to, slot = (weight, i) if i < count else (next_ref, i - count)
        for copy in weight_copies(sources, place[which[i]], i, to, slot, sem):
            copy.start()
    acc = acc_ref[...] if carried else None
    for i in range(count):
        for copy in weight_copies(sources, place[which[i]], i, weight, i, sem):
            copy.wait()
        d = jnp.dot(pieces[i][...], weight[i], preferred_element_type=jnp.float32)
        acc = d if acc is None else acc + d
    out_ref[...] = acc
    for i in range(count, count + ahead):
        for copy in weight_copies(sources, place[which[i]], i, next_ref, i - count, sem):
            copy.wait()


def partial_project(place, which, pieces, weights, acc=None, ahead=0):
    n = len(pieces)
    sums = jax.ShapeDtypeStruct((ROWS, QW + 2 * HD), jnp.float32)
    kept = jax.ShapeDtypeStruct((ahead, DK, QW + 2 * HD), jnp.bfloat16)
    extra = [] if acc is None else [acc]
    weights = [pltpu.with_memory_space_constraint(w, pltpu.HBM) for w in weights]
    return pl.pallas_call(
        functools.partial(partial_kernel, which, ahead, acc is not None),
        out_shape=(sums, kept) if ahead else sums,
        in_specs=[smem] + [vmem] * n + [hbm] * 3 + [vmem] * len(extra),
        out_specs=(vmem, vmem) if ahead else vmem,
        scratch_shapes=[
            pltpu.VMEM((n, DK, QW + 2 * HD), jnp.bfloat16),
            pltpu.SemaphoreType.DMA((n + ahead, 3)),
        ],
        compiler_params=pltpu.CompilerParams(vmem_limit_bytes=16 << 20),
        cost_estimate=work(6),
        name="project",
    )(place, *pieces, *weights, *extra)


def last_kernel(piece_ref, weight_ref, acc_ref, cos_ref, sin_ref, mine_ref, q_ref, n_ref):
    acc = acc_ref[...] + jnp.dot(
        piece_ref[...], weight_ref[0], preferred_element_type=jnp.float32
    )
    cosine, sine = cos_ref[...], sin_ref[...]
    for g in range(HG):
        at = slice(g * HD, (g + 1) * HD)
        q_ref[:, at] = turned(acc[:, at], cosine, sine).astype(jnp.bfloat16)
    n_ref[:ROWS, :] = turned(acc[:, QW : QW + HD], cosine, sine).astype(jnp.bfloat16)
    n_ref[ROWS : 2 * ROWS, :] = acc[:, QW + HD :].astype(jnp.bfloat16)
    mine = mine_ref[...]
    high = lax.shift_right_logical(mine, 6)
    both = jnp.concatenate([high, mine - high * 64, jnp.zeros((8, SEL), jnp.int32)], axis=0)
    n_ref[2 * ROWS :, :] = both.astype(jnp.float32).astype(jnp.bfloat16)


def last_project(*args):
    return pl.pallas_call(
        last_kernel,
        out_shape=(
            jax.ShapeDtypeStruct((ROWS, QW), jnp.bfloat16),
            jax.ShapeDtypeStruct((2 * ROWS + 16, HD), jnp.bfloat16),
        ),
        in_specs=[vmem] * 6,
        out_specs=(vmem, vmem),
        compiler_params=pltpu.CompilerParams(vmem_limit_bytes=16 << 20),
        cost_estimate=tiny,
        name="project_last",
    )(*args)


def attend_block(q, keys, vals, limit, m_ref, l_ref, acc_ref):
    s = lax.dot_general(keys, q, (((1,), (1,)), ((), ())), preferred_element_type=jnp.float32)
    if limit is not None:
        at = lax.broadcasted_iota(jnp.int32, s.shape, 0)
        s = jnp.where(at <= limit, s, low)
    old = m_ref[...]
    new = jnp.maximum(old, jnp.max(s, axis=0, keepdims=True))
    factor = jnp.exp2((old - new) * SCALE2)
    weight = jnp.exp2((s - new) * SCALE2)
    l_ref[...] = l_ref[...] * factor + jnp.sum(weight, axis=0, keepdims=True)
    acc_ref[...] = acc_ref[...] * factor + lax.dot_general(
        vals,
        weight.astype(jnp.bfloat16),
        (((0,), (0,)), ((), ())),
        preferred_element_type=jnp.float32,
    )
    m_ref[...] = new


def attend_source(rows_ref, i, jk_ref, jv_ref, r, valid_ref, first, o_ref, state, limit_ref=None):
    m_ref, l_ref, acc_ref = state
    m_ref[...] = jnp.full_like(m_ref, low)
    l_ref[...] = jnp.zeros_like(l_ref)
    acc_ref[...] = jnp.zeros_like(acc_ref)

    def span(sp, _):
        @pl.when(valid_ref[first + sp] != 0)
        def _():
            limit = None if limit_ref is None else jnp.where(sp == 0, limit_ref[...], SPAN)
            attend_block(
                rows_ref[i], jk_ref[r * 2 + sp], jv_ref[r * 2 + sp], limit, m_ref, l_ref, acc_ref
            )

        return 0

    lax.fori_loop(0, 2, span, 0)
    l = l_ref[...]
    some = l > 0.0
    mixed = acc_ref[...] / jnp.where(some, l, 1.0)
    rest = jnp.where(some, m_ref[...] * SCALE2 + jnp.log2(jnp.where(some, l, 1.0)), low)
    rows = []
    for k in range(3):
        part = rest.astype(jnp.bfloat16).astype(jnp.float32)
        rows += [part[:, g * SEL : (g + 1) * SEL] for g in range(HG)]
        rest = rest - part
    for g in range(HG):
        at = slice(g * SEL, (g + 1) * SEL)
        o_ref[i, :SEL, g * HD : (g + 1) * HD] = mixed[:, at].T.astype(jnp.bfloat16)
    stat = jnp.concatenate(rows + [jnp.zeros((HG, SEL), jnp.float32)], axis=0)
    o_ref[i, SEL:, :HD] = stat.astype(jnp.bfloat16)
    o_ref[i, SEL:, HD:] = jnp.zeros((16, QW - HD), jnp.bfloat16)


def spread(rows_ref, i, q):
    for g in range(HG):
        rows_ref[i, g * SEL : (g + 1) * SEL, :] = q[:, g * HD : (g + 1) * HD]


def join_kernel(rank_ref, k0, v0, k1, v1, n0, n1, mine_ref, freq_ref, jk_ref, jv_ref):
    freq = freq_ref[0:1, :]
    sign = freq_ref[1:2, :]
    mine = mine_ref[...]
    both = n1[2 * ROWS :, :].astype(jnp.float32)
    theirs = (both[0:4] * 64.0 + both[4:8]).astype(jnp.int32)
    for r in range(SLOTS):
        rows = slice(r * SPAN, (r + 1) * SPAN)
        for sp, (kr, vr, nr, here) in enumerate(((k0, v0, n0, mine), (k1, v1, n1, theirs))):
            offset = here[SLOTS + r : SLOTS + r + 1, :]
            angle = (rank_ref[r * 2 + sp] * SPAN - offset).astype(jnp.float32) * freq
            raw = kr[rows, :].astype(jnp.float32)
            cached = turned(raw, jnp.cos(angle), jnp.sin(angle) * sign)
            at = lax.broadcasted_iota(jnp.int32, (SPAN, SEL), 0)
            pick = (at == here[r : r + 1, :]).astype(jnp.float32).astype(jnp.bfloat16)
            ones = jnp.ones((SEL, HD), jnp.bfloat16)
            hit = jnp.dot(pick, ones, preferred_element_type=jnp.float32) > 0.5
            fresh_k = nr[r * SEL : (r + 1) * SEL, :]
            fresh_v = nr[ROWS + r * SEL : ROWS + (r + 1) * SEL, :]
            put_k = jnp.dot(pick, fresh_k, preferred_element_type=jnp.float32)
            put_v = jnp.dot(pick, fresh_v, preferred_element_type=jnp.float32)
            vals = vr[rows, :].astype(jnp.float32)
            jk_ref[r * 2 + sp] = jnp.where(hit, put_k, cached).astype(jnp.bfloat16)
            jv_ref[r * 2 + sp] = jnp.where(hit, put_v, vals).astype(jnp.bfloat16)


def attend_kernel(shift, valid_ref, q_ref, jk_ref, jv_ref, *refs):
    if shift == 0:
        sel_ref, o_ref, rows_ref, limit_ref = refs[:4]
        state = refs[4:]
    else:
        o_ref, rows_ref = refs[:2]
        limit_ref, state = None, refs[2:]
    for r in range(SLOTS):
        spread(rows_ref, r, q_ref[r * SEL : (r + 1) * SEL, :])

    def request(r, _):
        if shift == 0:
            limit_ref[...] = jnp.concatenate([sel_ref[pl.ds(r, 1), :]] * HG, axis=1)
        attend_source(
            rows_ref, r, jk_ref, jv_ref, r, valid_ref, shift * 4 + r * 2, o_ref, state, limit_ref
        )
        return 0

    lax.fori_loop(0, SLOTS, request, 0)


joined_shape = jax.ShapeDtypeStruct((SLOTS * 2, SPAN, HD), jnp.bfloat16)
packed_shape = jax.ShapeDtypeStruct((SLOTS, PACK, QW), jnp.bfloat16)


def join(*args):
    return pl.pallas_call(
        join_kernel,
        out_shape=(joined_shape, joined_shape),
        in_specs=[smem] + [vmem] * 8,
        out_specs=(vmem, vmem),
        compiler_params=pltpu.CompilerParams(vmem_limit_bytes=16 << 20),
        cost_estimate=work(3),
        name="join",
    )(*args)


def attend(shift, valid, *args):
    return pl.pallas_call(
        functools.partial(attend_kernel, shift),
        out_shape=packed_shape,
        in_specs=[smem] + [vmem] * len(args),
        out_specs=vmem,
        scratch_shapes=[pltpu.VMEM((SLOTS, HG * SEL, HD), jnp.bfloat16)]
        + ([pltpu.VMEM((1, HG * SEL), jnp.int32)] if shift == 0 else [])
        + [
            pltpu.VMEM((1, HG * SEL), jnp.float32),
            pltpu.VMEM((1, HG * SEL), jnp.float32),
            pltpu.VMEM((HD, HG * SEL), jnp.float32),
        ],
        compiler_params=pltpu.CompilerParams(vmem_limit_bytes=16 << 20),
        cost_estimate=work(1),
        name="attend",
    )(valid, *args)


def merge_parts(parts, put):
    lse = []
    for p in parts:
        stat = p[SEL:, :HD].astype(jnp.float32)
        lse.append(stat[0:4] + stat[4:8] + stat[8:12])
    top = functools.reduce(jnp.maximum, lse)
    weight = [jnp.exp2(v - top) for v in lse]
    total = functools.reduce(jnp.add, weight)
    pad = jnp.zeros((HD - HG, SEL), jnp.float32)
    weight = [jnp.concatenate([w / total, pad], axis=0).T for w in weight]
    for g in range(HG):
        at = slice(g * HD, (g + 1) * HD)
        mixed = jnp.zeros((SEL, HD), jnp.float32)
        for w, p in zip(weight, parts):
            mixed += w[:, g : g + 1] * p[:SEL, at].astype(jnp.float32)
        put(at, mixed.astype(jnp.bfloat16))


def merge_kernel(*refs):
    o_ref = refs[-1]
    for r in range(SLOTS):

        def put(at, value, r=r):
            o_ref[r * SEL : (r + 1) * SEL, at] = value

        merge_parts([p.at[r] for p in refs[:-1]], put)


def merge(*parts):
    return pl.pallas_call(
        merge_kernel,
        out_shape=jax.ShapeDtypeStruct((ROWS, QW), jnp.bfloat16),
        in_specs=[vmem] * len(parts),
        out_specs=vmem,
        compiler_params=pltpu.CompilerParams(vmem_limit_bytes=8 << 20),
        cost_estimate=tiny,
        name="merge",
    )(*parts)


def after(value, *others):
    return lax.optimization_barrier((value, *others))[0]


def shards(
    hidden, w_query, w_key, w_value, key_cache, value_cache,
    span_count, span_key, cache_offset, sel_index,
):
    zh, yh, yp, c = (lax.axis_index(a) for a in ("zh", "yh", "yp", "c"))
    zl, x = lax.axis_index("zl"), lax.axis_index("x")
    weights = (w_query, w_key, w_value)
    way = 2 * c - 1
    entries = [zl * 4 + (x + i * way) % 4 for i in range(4)]
    entries += [(1 - zl) * 4 + (x + i * way) % 4 for i in range(4)]
    entries += [zh, yh, way, (yp * 2 + c) * SLOTS]
    place = jnp.stack(entries).astype(jnp.int32)
    mine = jnp.concatenate(
        [sel_index, jnp.broadcast_to(cache_offset[:, None], (SLOTS, SEL))], axis=0
    )
    half = np.arange(HD // 2) * 2.0 / HD
    freq = jnp.asarray(
        np.stack([np.tile(rope_base**-half, 2), np.repeat([-1.0, 1.0], HD // 2)]), jnp.float32
    )
    cosine, sine, ranks, valid = prepare(place, span_count, span_key, sel_index, freq)
    h1, h3, z0 = ring_x(hidden), back_x(hidden), pz(hidden)
    k1 = py(key_cache)
    project = functools.partial(partial_project, place)
    acc = project((H_AT,), (hidden,), weights)
    h2 = ring_x(after(h1, cosine, acc))
    z1 = ring_x(z0)
    z3 = pz(h3)
    v1 = py(after(value_cache, k1))
    acc = project((H_AT + 1, H_AT + 3), (h1, h3), weights, acc)
    z2 = ring_x(z1)
    acc = project((Z_AT, H_AT + 2), (z0, h2), weights, acc)
    acc, kept = project(
        (Z_AT + 3, Z_AT + 1, Z_AT + 2), (z3, z1), weights, acc, ahead=1
    )
    acc = after(acc, k1, v1)
    query, fresh = last_project(z2, kept, acc, cosine, sine, mine)
    near, behind = ring_z(query), back_z(query)
    far = ring_z(near)
    jk, jv = join(ranks, key_cache, value_cache, k1, v1, fresh, py(fresh), mine, freq)
    out_near = back_z(attend(1, valid, near, jk, jv))
    out_behind = ring_z(attend(3, valid, behind, jk, jv))
    out_far = far_z(attend(2, valid, far, jk, jv))
    own = attend(0, valid, query, jk, jv, mine)
    return merge(own, out_near, out_behind, out_far)


def solution(mesh):
    split = Mesh(mesh.devices.reshape(4, 2, 2, 2, 2, 4), AXES)
    seq, tp = AXES[:4], AXES[4:]
    placed = (
        P(seq, tp),
        P(None, tp),
        P(None, tp),
        P(None, tp),
        P(seq, tp),
        P(seq, tp),
        P(),
        P(),
        P(seq),
        P(seq, None),
    )
    return jax.shard_map(
        shards, mesh=split, in_specs=placed, out_specs=P(seq, tp), check_vma=False
    )
```

```python
import functools
import math

import jax
import jax.numpy as jnp
import numpy as np
from jax import lax
from jax.experimental import pallas as pl
from jax.experimental.pallas import tpu as pltpu
from jax.sharding import Mesh, PartitionSpec as P

HD = 128
HG = 4
R = 8
MAXCH = 8
SPAN = 1024
SEL = 128
SLOTS = 2
ROWS = SLOTS * SEL
QW = HG * HD
PACK = SEL + 16
DK = 896
PROJ = 16

rope_base = 5000000.0
low = -1.0e30
SCALE2 = math.log2(math.e) / math.sqrt(HD)

vmem = pl.BlockSpec(memory_space=pltpu.VMEM)
smem = pl.BlockSpec(memory_space=pltpu.SMEM)
hbm = pl.BlockSpec(memory_space=pltpu.HBM)
tiny = pl.CostEstimate(flops=1, bytes_accessed=1, transcendentals=0)


def work(microseconds):
    return pl.CostEstimate(
        flops=microseconds * 1000000000, bytes_accessed=1, transcendentals=0
    )


AXES = ("zh", "yh", "yp", "c", "zl", "x")


def opposite_ways(n):
    plus = [(i, (i + 1) % n) for i in range(n)]
    minus = [(n + i, n + (i - 1) % n) for i in range(n)]
    return plus + minus


def ring_x(v):
    return lax.ppermute(v, ("c", "x"), opposite_ways(4))


def back_x(v):
    pairs = [(4 * c + i, 4 * c + (i - 1 + 2 * c) % 4) for c in range(2) for i in range(4)]
    return lax.ppermute(v, ("c", "x"), pairs)


def ring_z(v):
    pairs = [(2 * i + c, 2 * ((i + 1 - 2 * c) % 4) + c) for i in range(4) for c in range(2)]
    return lax.ppermute(v, ("zh", "c"), pairs)


def back_z(v):
    pairs = [(2 * i + c, 2 * ((i - 1 + 2 * c) % 4) + c) for i in range(4) for c in range(2)]
    return lax.ppermute(v, ("zh", "c"), pairs)


def far_z(v):
    return lax.ppermute(v, "zh", [(i, (i + 2) % 4) for i in range(4)])


def pz(v):
    return lax.ppermute(v, "zl", [(0, 1), (1, 0)])


def py(v):
    return lax.ppermute(v, "yh", [(0, 1), (1, 0)])


H_AT, Z_AT, ZH_AT, YH_AT, WAY_AT, REQ_AT = 0, 4, 8, 9, 10, 11


def prepare_kernel(place, count, key, sel_ref, freq_ref, cos_ref, sin_ref, rank_ref, valid_ref):
    freq = freq_ref[0:1, :]
    sign = freq_ref[1:2, :]
    zh, yh, way = place[ZH_AT], place[YH_AT], place[WAY_AT]
    for r in range(SLOTS):
        request = place[REQ_AT] + r
        used = count[request]

        def rank(j, request=request, used=used):
            mine = key[request, j]
            total = jnp.int32(0)
            for k in range(MAXCH):
                smaller = (key[request, k] < mine) & (k < used)
                total += jnp.where(smaller, 1, 0)
            return total

        spans = (zh * 2 + yh, zh * 2 + 1 - yh)
        ranks = [rank(j) for j in spans]
        for sp in range(2):
            rank_ref[r * 2 + sp] = ranks[sp]
        for shift in range(4):
            j = lax.rem(zh + shift * way + 4, 4) * 2 + yh
            mine = rank(j)
            for sp in range(2):
                good = (j < used) & (spans[sp] < used) & (ranks[sp] <= mine)
                valid_ref[shift * 4 + r * 2 + sp] = jnp.where(good, 1, 0)
        position = (sel_ref[r : r + 1, :] + ranks[0] * SPAN).astype(jnp.float32)
        angle = jnp.broadcast_to(position, (SEL, HD)).T * freq
        cos_ref[r * SEL : (r + 1) * SEL, :] = jnp.cos(angle)
        sin_ref[r * SEL : (r + 1) * SEL, :] = jnp.sin(angle) * sign


def prepare(*args):
    shape = jax.ShapeDtypeStruct
    return pl.pallas_call(
        prepare_kernel,
        out_shape=(
            shape((ROWS, HD), jnp.float32),
            shape((ROWS, HD), jnp.float32),
            shape((4,), jnp.int32),
            shape((16,), jnp.int32),
        ),
        in_specs=[smem] * 3 + [vmem] * 2,
        out_specs=(vmem, vmem, smem, smem),
        compiler_params=pltpu.CompilerParams(vmem_limit_bytes=8 << 20),
        cost_estimate=work(2),
        name="prepare",
    )(*args)


def turned(v, cosine, sine):
    return v * cosine + pltpu.roll(v, HD // 2, 1) * sine


def weight_copies(sources, piece, i, to_ref, slot, sem):
    at = pl.ds(pl.multiple_of(piece * DK, DK), DK)
    start = 0
    for j, (w, width) in enumerate(zip(sources, (QW, HD, HD))):
        to = to_ref.at[slot, :, start : start + width]
        yield pltpu.make_async_copy(w.at[at, :], to, sem.at[i, j])
        start += width


def partial_kernel(which, ahead, carried, place, *refs):
    count = len(which) - ahead
    pieces, refs = refs[:count], refs[count:]
    sources, refs = refs[:3], refs[3:]
    if carried:
        acc_ref, refs = refs[0], refs[1:]
    out_ref, refs = refs[0], refs[1:]
    if ahead:
        next_ref, refs = refs[0], refs[1:]
    weight, sem = refs
    for i in range(count + ahead):
        to, slot = (weight, i) if i < count else (next_ref, i - count)
        for copy in weight_copies(sources, place[which[i]], i, to, slot, sem):
            copy.start()
    acc = acc_ref[...] if carried else None
    for i in range(count):
        for copy in weight_copies(sources, place[which[i]], i, weight, i, sem):
            copy.wait()
        d = jnp.dot(pieces[i][...], weight[i], preferred_element_type=jnp.float32)
        acc = d if acc is None else acc + d
    out_ref[...] = acc
    for i in range(count, count + ahead):
        for copy in weight_copies(sources, place[which[i]], i, next_ref, i - count, sem):
            copy.wait()


def partial_project(place, which, pieces, weights, acc=None, ahead=0):
    n = len(pieces)
    sums = jax.ShapeDtypeStruct((ROWS, QW + 2 * HD), jnp.float32)
    kept = jax.ShapeDtypeStruct((ahead, DK, QW + 2 * HD), jnp.bfloat16)
    extra = [] if acc is None else [acc]
    weights = [pltpu.with_memory_space_constraint(w, pltpu.HBM) for w in weights]
    return pl.pallas_call(
        functools.partial(partial_kernel, which, ahead, acc is not None),
        out_shape=(sums, kept) if ahead else sums,
        in_specs=[smem] + [vmem] * n + [hbm] * 3 + [vmem] * len(extra),
        out_specs=(vmem, vmem) if ahead else vmem,
        scratch_shapes=[
            pltpu.VMEM((n, DK, QW + 2 * HD), jnp.bfloat16),
            pltpu.SemaphoreType.DMA((n + ahead, 3)),
        ],
        compiler_params=pltpu.CompilerParams(vmem_limit_bytes=16 << 20),
        cost_estimate=work(6),
        name="project",
    )(place, *pieces, *weights, *extra)


def last_kernel(
    first_ref, second_ref, weight_ref, acc_ref, cos_ref, sin_ref, mine_ref, q_ref, n_ref
):
    acc = acc_ref[...]
    for i, piece in enumerate((first_ref, second_ref)):
        acc += jnp.dot(piece[...], weight_ref[i], preferred_element_type=jnp.float32)
    cosine, sine = cos_ref[...], sin_ref[...]
    for g in range(HG):
        at = slice(g * HD, (g + 1) * HD)
        q_ref[:, at] = turned(acc[:, at], cosine, sine).astype(jnp.bfloat16)
    n_ref[:ROWS, :] = turned(acc[:, QW : QW + HD], cosine, sine).astype(jnp.bfloat16)
    n_ref[ROWS : 2 * ROWS, :] = acc[:, QW + HD :].astype(jnp.bfloat16)
    mine = mine_ref[...]
    high = lax.shift_right_logical(mine, 6)
    both = jnp.concatenate([high, mine - high * 64, jnp.zeros((8, SEL), jnp.int32)], axis=0)
    n_ref[2 * ROWS :, :] = both.astype(jnp.float32).astype(jnp.bfloat16)


def last_project(*args):
    return pl.pallas_call(
        last_kernel,
        out_shape=(
            jax.ShapeDtypeStruct((ROWS, QW), jnp.bfloat16),
            jax.ShapeDtypeStruct((2 * ROWS + 16, HD), jnp.bfloat16),
        ),
        in_specs=[vmem] * 7,
        out_specs=(vmem, vmem),
        compiler_params=pltpu.CompilerParams(vmem_limit_bytes=16 << 20),
        cost_estimate=tiny,
        name="project_last",
    )(*args)


def attend_block(q, keys, vals, limit, m_ref, l_ref, acc_ref):
    s = lax.dot_general(keys, q, (((1,), (1,)), ((), ())), preferred_element_type=jnp.float32)
    if limit is not None:
        at = lax.broadcasted_iota(jnp.int32, s.shape, 0)
        s = jnp.where(at <= limit, s, low)
    old = m_ref[...]
    new = jnp.maximum(old, jnp.max(s, axis=0, keepdims=True))
    factor = jnp.exp2((old - new) * SCALE2)
    weight = jnp.exp2((s - new) * SCALE2)
    l_ref[...] = l_ref[...] * factor + jnp.sum(weight, axis=0, keepdims=True)
    acc_ref[...] = acc_ref[...] * factor + lax.dot_general(
        vals,
        weight.astype(jnp.bfloat16),
        (((0,), (0,)), ((), ())),
        preferred_element_type=jnp.float32,
    )
    m_ref[...] = new


def attend_source(rows_ref, i, jk_ref, jv_ref, r, valid_ref, first, o_ref, state, limit_ref=None):
    m_ref, l_ref, acc_ref = state
    m_ref[...] = jnp.full_like(m_ref, low)
    l_ref[...] = jnp.zeros_like(l_ref)
    acc_ref[...] = jnp.zeros_like(acc_ref)

    def span(sp, _):
        @pl.when(valid_ref[first + sp] != 0)
        def _():
            limit = None if limit_ref is None else jnp.where(sp == 0, limit_ref[...], SPAN)
            attend_block(
                rows_ref[i], jk_ref[r * 2 + sp], jv_ref[r * 2 + sp], limit, m_ref, l_ref, acc_ref
            )

        return 0

    lax.fori_loop(0, 2, span, 0)
    l = l_ref[...]
    some = l > 0.0
    mixed = acc_ref[...] / jnp.where(some, l, 1.0)
    rest = jnp.where(some, m_ref[...] * SCALE2 + jnp.log2(jnp.where(some, l, 1.0)), low)
    rows = []
    for k in range(3):
        part = rest.astype(jnp.bfloat16).astype(jnp.float32)
        rows += [part[:, g * SEL : (g + 1) * SEL] for g in range(HG)]
        rest = rest - part
    for g in range(HG):
        at = slice(g * SEL, (g + 1) * SEL)
        o_ref[i, :SEL, g * HD : (g + 1) * HD] = mixed[:, at].T.astype(jnp.bfloat16)
    stat = jnp.concatenate(rows + [jnp.zeros((HG, SEL), jnp.float32)], axis=0)
    o_ref[i, SEL:, :HD] = stat.astype(jnp.bfloat16)
    o_ref[i, SEL:, HD:] = jnp.zeros((16, QW - HD), jnp.bfloat16)


def spread(rows_ref, i, q):
    for g in range(HG):
        rows_ref[i, g * SEL : (g + 1) * SEL, :] = q[:, g * HD : (g + 1) * HD]


def join_kernel(rank_ref, k0, v0, k1, v1, n0, n1, mine_ref, freq_ref, jk_ref, jv_ref):
    freq = freq_ref[0:1, :]
    sign = freq_ref[1:2, :]
    mine = mine_ref[...]
    both = n1[2 * ROWS :, :].astype(jnp.float32)
    theirs = (both[0:4] * 64.0 + both[4:8]).astype(jnp.int32)
    for r in range(SLOTS):
        rows = slice(r * SPAN, (r + 1) * SPAN)
        for sp, (kr, vr, nr, here) in enumerate(((k0, v0, n0, mine), (k1, v1, n1, theirs))):
            offset = here[SLOTS + r : SLOTS + r + 1, :]
            angle = (rank_ref[r * 2 + sp] * SPAN - offset).astype(jnp.float32) * freq
            raw = kr[rows, :].astype(jnp.float32)
            cached = turned(raw, jnp.cos(angle), jnp.sin(angle) * sign)
            at = lax.broadcasted_iota(jnp.int32, (SPAN, SEL), 0)
            pick = (at == here[r : r + 1, :]).astype(jnp.float32).astype(jnp.bfloat16)
            ones = jnp.ones((SEL, HD), jnp.bfloat16)
            hit = jnp.dot(pick, ones, preferred_element_type=jnp.float32) > 0.5
            fresh_k = nr[r * SEL : (r + 1) * SEL, :]
            fresh_v = nr[ROWS + r * SEL : ROWS + (r + 1) * SEL, :]
            put_k = jnp.dot(pick, fresh_k, preferred_element_type=jnp.float32)
            put_v = jnp.dot(pick, fresh_v, preferred_element_type=jnp.float32)
            vals = vr[rows, :].astype(jnp.float32)
            jk_ref[r * 2 + sp] = jnp.where(hit, put_k, cached).astype(jnp.bfloat16)
            jv_ref[r * 2 + sp] = jnp.where(hit, put_v, vals).astype(jnp.bfloat16)


def attend_kernel(shift, valid_ref, q_ref, jk_ref, jv_ref, *refs):
    if shift == 0:
        sel_ref, o_ref, rows_ref, limit_ref = refs[:4]
        state = refs[4:]
    else:
        o_ref, rows_ref = refs[:2]
        limit_ref, state = None, refs[2:]
    for r in range(SLOTS):
        spread(rows_ref, r, q_ref[r * SEL : (r + 1) * SEL, :])

    def request(r, _):
        if shift == 0:
            limit_ref[...] = jnp.concatenate([sel_ref[pl.ds(r, 1), :]] * HG, axis=1)
        attend_source(
            rows_ref, r, jk_ref, jv_ref, r, valid_ref, shift * 4 + r * 2, o_ref, state, limit_ref
        )
        return 0

    lax.fori_loop(0, SLOTS, request, 0)


joined_shape = jax.ShapeDtypeStruct((SLOTS * 2, SPAN, HD), jnp.bfloat16)
packed_shape = jax.ShapeDtypeStruct((SLOTS, PACK, QW), jnp.bfloat16)


def join(*args):
    return pl.pallas_call(
        join_kernel,
        out_shape=(joined_shape, joined_shape),
        in_specs=[smem] + [vmem] * 8,
        out_specs=(vmem, vmem),
        compiler_params=pltpu.CompilerParams(vmem_limit_bytes=16 << 20),
        cost_estimate=work(3),
        name="join",
    )(*args)


def attend(shift, valid, *args):
    return pl.pallas_call(
        functools.partial(attend_kernel, shift),
        out_shape=packed_shape,
        in_specs=[smem] + [vmem] * len(args),
        out_specs=vmem,
        scratch_shapes=[pltpu.VMEM((SLOTS, HG * SEL, HD), jnp.bfloat16)]
        + ([pltpu.VMEM((1, HG * SEL), jnp.int32)] if shift == 0 else [])
        + [
            pltpu.VMEM((1, HG * SEL), jnp.float32),
            pltpu.VMEM((1, HG * SEL), jnp.float32),
            pltpu.VMEM((HD, HG * SEL), jnp.float32),
        ],
        compiler_params=pltpu.CompilerParams(vmem_limit_bytes=16 << 20),
        cost_estimate=work(1),
        name="attend",
    )(valid, *args)


def merge_parts(parts, put):
    lse = []
    for p in parts:
        stat = p[SEL:, :HD].astype(jnp.float32)
        lse.append(stat[0:4] + stat[4:8] + stat[8:12])
    top = functools.reduce(jnp.maximum, lse)
    weight = [jnp.exp2(v - top) for v in lse]
    total = functools.reduce(jnp.add, weight)
    pad = jnp.zeros((HD - HG, SEL), jnp.float32)
    weight = [jnp.concatenate([w / total, pad], axis=0).T for w in weight]
    for g in range(HG):
        at = slice(g * HD, (g + 1) * HD)
        mixed = jnp.zeros((SEL, HD), jnp.float32)
        for w, p in zip(weight, parts):
            mixed += w[:, g : g + 1] * p[:SEL, at].astype(jnp.float32)
        put(at, mixed.astype(jnp.bfloat16))


def merge_kernel(*refs):
    o_ref = refs[-1]
    for r in range(SLOTS):

        def put(at, value, r=r):
            o_ref[r * SEL : (r + 1) * SEL, at] = value

        merge_parts([p.at[r] for p in refs[:-1]], put)


def merge(*parts):
    return pl.pallas_call(
        merge_kernel,
        out_shape=jax.ShapeDtypeStruct((ROWS, QW), jnp.bfloat16),
        in_specs=[vmem] * len(parts),
        out_specs=vmem,
        compiler_params=pltpu.CompilerParams(vmem_limit_bytes=8 << 20),
        cost_estimate=tiny,
        name="merge",
    )(*parts)


def after(value, *others):
    return lax.optimization_barrier((value, *others))[0]


def shards(
    hidden, w_query, w_key, w_value, key_cache, value_cache,
    span_count, span_key, cache_offset, sel_index,
):
    zh, yh, yp, c = (lax.axis_index(a) for a in ("zh", "yh", "yp", "c"))
    zl, x = lax.axis_index("zl"), lax.axis_index("x")
    weights = (w_query, w_key, w_value)
    way = 2 * c - 1
    entries = [zl * 4 + (x + i * way) % 4 for i in range(4)]
    entries += [(1 - zl) * 4 + (x + i * way) % 4 for i in range(4)]
    entries += [zh, yh, way, (yp * 2 + c) * SLOTS]
    place = jnp.stack(entries).astype(jnp.int32)
    mine = jnp.concatenate(
        [sel_index, jnp.broadcast_to(cache_offset[:, None], (SLOTS, SEL))], axis=0
    )
    half = np.arange(HD // 2) * 2.0 / HD
    freq = jnp.asarray(
        np.stack([np.tile(rope_base**-half, 2), np.repeat([-1.0, 1.0], HD // 2)]), jnp.float32
    )
    cosine, sine, ranks, valid = prepare(place, span_count, span_key, sel_index, freq)
    h1, h3, z0 = ring_x(hidden), back_x(hidden), pz(hidden)
    k1 = py(key_cache)
    project = functools.partial(partial_project, place)
    acc = project((H_AT,), (hidden,), weights)
    z1 = ring_x(after(z0, cosine, acc))
    z3 = pz(h3)
    v1 = py(after(value_cache, k1))
    acc = project((H_AT + 1, H_AT + 3), (h1, h3), weights, acc)
    z2 = ring_x(z1)
    h2 = ring_x(after(h1, z1))
    acc = project((Z_AT, Z_AT + 1), (z0, z1), weights, acc)
    acc, kept = project((Z_AT + 3, Z_AT + 2, H_AT + 2), (z3,), weights, acc, ahead=2)
    acc = after(acc, k1, v1)
    query, fresh = last_project(z2, h2, kept, acc, cosine, sine, mine)
    near, behind = ring_z(query), back_z(query)
    far = ring_z(near)
    jk, jv = join(ranks, key_cache, value_cache, k1, v1, fresh, py(fresh), mine, freq)
    out_near = back_z(attend(1, valid, near, jk, jv))
    out_behind = ring_z(attend(3, valid, behind, jk, jv))
    out_far = far_z(attend(2, valid, far, jk, jv))
    own = attend(0, valid, query, jk, jv, mine)
    return merge(own, out_near, out_behind, out_far)


def solution(mesh):
    split = Mesh(mesh.devices.reshape(4, 2, 2, 2, 2, 4), AXES)
    seq, tp = AXES[:4], AXES[4:]
    placed = (
        P(seq, tp),
        P(None, tp),
        P(None, tp),
        P(None, tp),
        P(seq, tp),
        P(seq, tp),
        P(),
        P(),
        P(seq),
        P(seq, None),
    )
    return jax.shard_map(
        shards, mesh=split, in_specs=placed, out_specs=P(seq, tp), check_vma=False
    )
```

```python
import functools
import math

import jax
import jax.numpy as jnp
import numpy as np
from jax import lax
from jax.experimental import pallas as pl
from jax.experimental.pallas import tpu as pltpu
from jax.sharding import Mesh, PartitionSpec as P

HD = 128
HG = 4
R = 8
MAXCH = 8
SPAN = 1024
SEL = 128
SLOTS = 2
ROWS = SLOTS * SEL
QW = HG * HD
PACK = SEL + 16
DK = 896
PROJ = 16

rope_base = 5000000.0
low = -1.0e30
SCALE2 = math.log2(math.e) / math.sqrt(HD)

vmem = pl.BlockSpec(memory_space=pltpu.VMEM)
smem = pl.BlockSpec(memory_space=pltpu.SMEM)
hbm = pl.BlockSpec(memory_space=pltpu.HBM)
tiny = pl.CostEstimate(flops=1, bytes_accessed=1, transcendentals=0)


def work(microseconds):
    return pl.CostEstimate(
        flops=microseconds * 1000000000, bytes_accessed=1, transcendentals=0
    )


AXES = ("zh", "yh", "yp", "c", "zl", "x")


def opposite_ways(n):
    plus = [(i, (i + 1) % n) for i in range(n)]
    minus = [(n + i, n + (i - 1) % n) for i in range(n)]
    return plus + minus


def ring_x(v):
    return lax.ppermute(v, ("c", "x"), opposite_ways(4))


def back_x(v):
    pairs = [(4 * c + i, 4 * c + (i - 1 + 2 * c) % 4) for c in range(2) for i in range(4)]
    return lax.ppermute(v, ("c", "x"), pairs)


def ring_z(v):
    pairs = [(2 * i + c, 2 * ((i + 1 - 2 * c) % 4) + c) for i in range(4) for c in range(2)]
    return lax.ppermute(v, ("zh", "c"), pairs)


def back_z(v):
    pairs = [(2 * i + c, 2 * ((i - 1 + 2 * c) % 4) + c) for i in range(4) for c in range(2)]
    return lax.ppermute(v, ("zh", "c"), pairs)


def far_z(v):
    return lax.ppermute(v, "zh", [(i, (i + 2) % 4) for i in range(4)])


def pz(v):
    return lax.ppermute(v, "zl", [(0, 1), (1, 0)])


def py(v):
    return lax.ppermute(v, "yh", [(0, 1), (1, 0)])


H_AT, Z_AT, ZH_AT, YH_AT, WAY_AT, REQ_AT = 0, 4, 8, 9, 10, 11


def prepare_kernel(place, count, key, sel_ref, freq_ref, cos_ref, sin_ref, rank_ref, valid_ref):
    freq = freq_ref[0:1, :]
    sign = freq_ref[1:2, :]
    zh, yh, way = place[ZH_AT], place[YH_AT], place[WAY_AT]
    for r in range(SLOTS):
        request = place[REQ_AT] + r
        used = count[request]

        def rank(j, request=request, used=used):
            mine = key[request, j]
            total = jnp.int32(0)
            for k in range(MAXCH):
                smaller = (key[request, k] < mine) & (k < used)
                total += jnp.where(smaller, 1, 0)
            return total

        spans = (zh * 2 + yh, zh * 2 + 1 - yh)
        ranks = [rank(j) for j in spans]
        for sp in range(2):
            rank_ref[r * 2 + sp] = ranks[sp]
        for shift in range(4):
            j = lax.rem(zh + shift * way + 4, 4) * 2 + yh
            mine = rank(j)
            for sp in range(2):
                good = (j < used) & (spans[sp] < used) & (ranks[sp] <= mine)
                valid_ref[shift * 4 + r * 2 + sp] = jnp.where(good, 1, 0)
        position = (sel_ref[r : r + 1, :] + ranks[0] * SPAN).astype(jnp.float32)
        angle = jnp.broadcast_to(position, (SEL, HD)).T * freq
        cos_ref[r * SEL : (r + 1) * SEL, :] = jnp.cos(angle)
        sin_ref[r * SEL : (r + 1) * SEL, :] = jnp.sin(angle) * sign


def prepare(*args):
    shape = jax.ShapeDtypeStruct
    return pl.pallas_call(
        prepare_kernel,
        out_shape=(
            shape((ROWS, HD), jnp.float32),
            shape((ROWS, HD), jnp.float32),
            shape((4,), jnp.int32),
            shape((16,), jnp.int32),
        ),
        in_specs=[smem] * 3 + [vmem] * 2,
        out_specs=(vmem, vmem, smem, smem),
        compiler_params=pltpu.CompilerParams(vmem_limit_bytes=8 << 20),
        cost_estimate=work(2),
        name="prepare",
    )(*args)


def turned(v, cosine, sine):
    return v * cosine + pltpu.roll(v, HD // 2, 1) * sine


def weight_copies(sources, piece, i, to_ref, slot, sem):
    at = pl.ds(pl.multiple_of(piece * DK, DK), DK)
    start = 0
    for j, (w, width) in enumerate(zip(sources, (QW, HD, HD))):
        to = to_ref.at[slot, :, start : start + width]
        yield pltpu.make_async_copy(w.at[at, :], to, sem.at[i, j])
        start += width


def partial_kernel(which, ahead, carried, place, *refs):
    count = len(which) - ahead
    pieces, refs = refs[:count], refs[count:]
    sources, refs = refs[:3], refs[3:]
    if carried:
        acc_ref, refs = refs[0], refs[1:]
    out_ref, refs = refs[0], refs[1:]
    if ahead:
        next_ref, refs = refs[0], refs[1:]
    weight, sem = refs
    for i in range(count + ahead):
        to, slot = (weight, i) if i < count else (next_ref, i - count)
        for copy in weight_copies(sources, place[which[i]], i, to, slot, sem):
            copy.start()
    acc = acc_ref[...] if carried else None
    for i in range(count):
        for copy in weight_copies(sources, place[which[i]], i, weight, i, sem):
            copy.wait()
        d = jnp.dot(pieces[i][...], weight[i], preferred_element_type=jnp.float32)
        acc = d if acc is None else acc + d
    out_ref[...] = acc
    for i in range(count, count + ahead):
        for copy in weight_copies(sources, place[which[i]], i, next_ref, i - count, sem):
            copy.wait()


def partial_project(place, which, pieces, weights, acc=None, ahead=0):
    n = len(pieces)
    sums = jax.ShapeDtypeStruct((ROWS, QW + 2 * HD), jnp.float32)
    kept = jax.ShapeDtypeStruct((ahead, DK, QW + 2 * HD), jnp.bfloat16)
    extra = [] if acc is None else [acc]
    weights = [pltpu.with_memory_space_constraint(w, pltpu.HBM) for w in weights]
    return pl.pallas_call(
        functools.partial(partial_kernel, which, ahead, acc is not None),
        out_shape=(sums, kept) if ahead else sums,
        in_specs=[smem] + [vmem] * n + [hbm] * 3 + [vmem] * len(extra),
        out_specs=(vmem, vmem) if ahead else vmem,
        scratch_shapes=[
            pltpu.VMEM((n, DK, QW + 2 * HD), jnp.bfloat16),
            pltpu.SemaphoreType.DMA((n + ahead, 3)),
        ],
        compiler_params=pltpu.CompilerParams(vmem_limit_bytes=16 << 20),
        cost_estimate=work(6),
        name="project",
    )(place, *pieces, *weights, *extra)


def last_kernel(
    first_ref, second_ref, weight_ref, acc_ref, cos_ref, sin_ref, mine_ref, q_ref, n_ref
):
    acc = acc_ref[...]
    for i, piece in enumerate((first_ref, second_ref)):
        acc += jnp.dot(piece[...], weight_ref[i], preferred_element_type=jnp.float32)
    cosine, sine = cos_ref[...], sin_ref[...]
    for g in range(HG):
        at = slice(g * HD, (g + 1) * HD)
        q_ref[:, at] = turned(acc[:, at], cosine, sine).astype(jnp.bfloat16)
    n_ref[:ROWS, :] = turned(acc[:, QW : QW + HD], cosine, sine).astype(jnp.bfloat16)
    n_ref[ROWS : 2 * ROWS, :] = acc[:, QW + HD :].astype(jnp.bfloat16)
    mine = mine_ref[...]
    high = lax.shift_right_logical(mine, 6)
    both = jnp.concatenate([high, mine - high * 64, jnp.zeros((8, SEL), jnp.int32)], axis=0)
    n_ref[2 * ROWS :, :] = both.astype(jnp.float32).astype(jnp.bfloat16)


def last_project(*args):
    return pl.pallas_call(
        last_kernel,
        out_shape=(
            jax.ShapeDtypeStruct((ROWS, QW), jnp.bfloat16),
            jax.ShapeDtypeStruct((2 * ROWS + 16, HD), jnp.bfloat16),
        ),
        in_specs=[vmem] * 7,
        out_specs=(vmem, vmem),
        compiler_params=pltpu.CompilerParams(vmem_limit_bytes=16 << 20),
        cost_estimate=tiny,
        name="project_last",
    )(*args)


def attend_block(q, keys, vals, limit, m_ref, l_ref, acc_ref):
    s = lax.dot_general(keys, q, (((1,), (1,)), ((), ())), preferred_element_type=jnp.float32)
    if limit is not None:
        at = lax.broadcasted_iota(jnp.int32, s.shape, 0)
        s = jnp.where(at <= limit, s, low)
    old = m_ref[...]
    new = jnp.maximum(old, jnp.max(s, axis=0, keepdims=True))
    factor = jnp.exp2((old - new) * SCALE2)
    weight = jnp.exp2((s - new) * SCALE2)
    l_ref[...] = l_ref[...] * factor + jnp.sum(weight, axis=0, keepdims=True)
    acc_ref[...] = acc_ref[...] * factor + lax.dot_general(
        vals,
        weight.astype(jnp.bfloat16),
        (((0,), (0,)), ((), ())),
        preferred_element_type=jnp.float32,
    )
    m_ref[...] = new


def attend_source(rows_ref, i, jk_ref, jv_ref, r, valid_ref, first, o_ref, state, limit_ref=None):
    m_ref, l_ref, acc_ref = state
    m_ref[...] = jnp.full_like(m_ref, low)
    l_ref[...] = jnp.zeros_like(l_ref)
    acc_ref[...] = jnp.zeros_like(acc_ref)

    def span(sp, _):
        @pl.when(valid_ref[first + sp] != 0)
        def _():
            limit = None if limit_ref is None else jnp.where(sp == 0, limit_ref[...], SPAN)
            attend_block(
                rows_ref[i], jk_ref[r * 2 + sp], jv_ref[r * 2 + sp], limit, m_ref, l_ref, acc_ref
            )

        return 0

    lax.fori_loop(0, 2, span, 0)
    l = l_ref[...]
    some = l > 0.0
    mixed = acc_ref[...] / jnp.where(some, l, 1.0)
    rest = jnp.where(some, m_ref[...] * SCALE2 + jnp.log2(jnp.where(some, l, 1.0)), low)
    rows = []
    for k in range(3):
        part = rest.astype(jnp.bfloat16).astype(jnp.float32)
        rows += [part[:, g * SEL : (g + 1) * SEL] for g in range(HG)]
        rest = rest - part
    for g in range(HG):
        at = slice(g * SEL, (g + 1) * SEL)
        o_ref[i, :SEL, g * HD : (g + 1) * HD] = mixed[:, at].T.astype(jnp.bfloat16)
    stat = jnp.concatenate(rows + [jnp.zeros((HG, SEL), jnp.float32)], axis=0)
    o_ref[i, SEL:, :HD] = stat.astype(jnp.bfloat16)
    o_ref[i, SEL:, HD:] = jnp.zeros((16, QW - HD), jnp.bfloat16)


def spread(rows_ref, i, q):
    for g in range(HG):
        rows_ref[i, g * SEL : (g + 1) * SEL, :] = q[:, g * HD : (g + 1) * HD]


def join_kernel(rank_ref, k0, v0, k1, v1, n0, n1, mine_ref, freq_ref, jk_ref, jv_ref):
    freq = freq_ref[0:1, :]
    sign = freq_ref[1:2, :]
    mine = mine_ref[...]
    both = n1[2 * ROWS :, :].astype(jnp.float32)
    theirs = (both[0:4] * 64.0 + both[4:8]).astype(jnp.int32)
    for r in range(SLOTS):
        rows = slice(r * SPAN, (r + 1) * SPAN)
        for sp, (kr, vr, nr, here) in enumerate(((k0, v0, n0, mine), (k1, v1, n1, theirs))):
            offset = here[SLOTS + r : SLOTS + r + 1, :]
            angle = (rank_ref[r * 2 + sp] * SPAN - offset).astype(jnp.float32) * freq
            raw = kr[rows, :].astype(jnp.float32)
            cached = turned(raw, jnp.cos(angle), jnp.sin(angle) * sign)
            at = lax.broadcasted_iota(jnp.int32, (SPAN, SEL), 0)
            pick = (at == here[r : r + 1, :]).astype(jnp.float32).astype(jnp.bfloat16)
            ones = jnp.ones((SEL, HD), jnp.bfloat16)
            hit = jnp.dot(pick, ones, preferred_element_type=jnp.float32) > 0.5
            fresh_k = nr[r * SEL : (r + 1) * SEL, :]
            fresh_v = nr[ROWS + r * SEL : ROWS + (r + 1) * SEL, :]
            put_k = jnp.dot(pick, fresh_k, preferred_element_type=jnp.float32)
            put_v = jnp.dot(pick, fresh_v, preferred_element_type=jnp.float32)
            vals = vr[rows, :].astype(jnp.float32)
            jk_ref[r * 2 + sp] = jnp.where(hit, put_k, cached).astype(jnp.bfloat16)
            jv_ref[r * 2 + sp] = jnp.where(hit, put_v, vals).astype(jnp.bfloat16)


def attend_kernel(shift, valid_ref, q_ref, jk_ref, jv_ref, *refs):
    if shift == 0:
        sel_ref, o_ref, rows_ref, limit_ref = refs[:4]
        state = refs[4:]
    else:
        o_ref, rows_ref = refs[:2]
        limit_ref, state = None, refs[2:]
    for r in range(SLOTS):
        spread(rows_ref, r, q_ref[r * SEL : (r + 1) * SEL, :])

    def request(r, _):
        if shift == 0:
            limit_ref[...] = jnp.concatenate([sel_ref[pl.ds(r, 1), :]] * HG, axis=1)
        attend_source(
            rows_ref, r, jk_ref, jv_ref, r, valid_ref, shift * 4 + r * 2, o_ref, state, limit_ref
        )
        return 0

    lax.fori_loop(0, SLOTS, request, 0)


joined_shape = jax.ShapeDtypeStruct((SLOTS * 2, SPAN, HD), jnp.bfloat16)
packed_shape = jax.ShapeDtypeStruct((SLOTS, PACK, QW), jnp.bfloat16)


def join(*args):
    return pl.pallas_call(
        join_kernel,
        out_shape=(joined_shape, joined_shape),
        in_specs=[smem] + [vmem] * 8,
        out_specs=(vmem, vmem),
        compiler_params=pltpu.CompilerParams(vmem_limit_bytes=16 << 20),
        cost_estimate=work(3),
        name="join",
    )(*args)


def attend(shift, valid, *args):
    return pl.pallas_call(
        functools.partial(attend_kernel, shift),
        out_shape=packed_shape,
        in_specs=[smem] + [vmem] * len(args),
        out_specs=vmem,
        scratch_shapes=[pltpu.VMEM((SLOTS, HG * SEL, HD), jnp.bfloat16)]
        + ([pltpu.VMEM((1, HG * SEL), jnp.int32)] if shift == 0 else [])
        + [
            pltpu.VMEM((1, HG * SEL), jnp.float32),
            pltpu.VMEM((1, HG * SEL), jnp.float32),
            pltpu.VMEM((HD, HG * SEL), jnp.float32),
        ],
        compiler_params=pltpu.CompilerParams(vmem_limit_bytes=16 << 20),
        cost_estimate=work(1),
        name="attend",
    )(valid, *args)


def merge_parts(parts, put):
    lse = []
    for p in parts:
        stat = p[SEL:, :HD].astype(jnp.float32)
        lse.append(stat[0:4] + stat[4:8] + stat[8:12])
    top = functools.reduce(jnp.maximum, lse)
    weight = [jnp.exp2(v - top) for v in lse]
    total = functools.reduce(jnp.add, weight)
    pad = jnp.zeros((HD - HG, SEL), jnp.float32)
    weight = [jnp.concatenate([w / total, pad], axis=0).T for w in weight]
    for g in range(HG):
        at = slice(g * HD, (g + 1) * HD)
        mixed = jnp.zeros((SEL, HD), jnp.float32)
        for w, p in zip(weight, parts):
            mixed += w[:, g : g + 1] * p[:SEL, at].astype(jnp.float32)
        put(at, mixed.astype(jnp.bfloat16))


def merge_kernel(*refs):
    o_ref = refs[-1]
    for r in range(SLOTS):

        def put(at, value, r=r):
            o_ref[r * SEL : (r + 1) * SEL, at] = value

        merge_parts([p.at[r] for p in refs[:-1]], put)


def merge(*parts):
    return pl.pallas_call(
        merge_kernel,
        out_shape=jax.ShapeDtypeStruct((ROWS, QW), jnp.bfloat16),
        in_specs=[vmem] * len(parts),
        out_specs=vmem,
        compiler_params=pltpu.CompilerParams(vmem_limit_bytes=8 << 20),
        cost_estimate=tiny,
        name="merge",
    )(*parts)


def after(value, *others):
    return lax.optimization_barrier((value, *others))[0]


def shards(
    hidden, w_query, w_key, w_value, key_cache, value_cache,
    span_count, span_key, cache_offset, sel_index,
):
    zh, yh, yp, c = (lax.axis_index(a) for a in ("zh", "yh", "yp", "c"))
    zl, x = lax.axis_index("zl"), lax.axis_index("x")
    weights = (w_query, w_key, w_value)
    way = 2 * c - 1
    entries = [zl * 4 + (x + i * way) % 4 for i in range(4)]
    entries += [(1 - zl) * 4 + (x + i * way) % 4 for i in range(4)]
    entries += [zh, yh, way, (yp * 2 + c) * SLOTS]
    place = jnp.stack(entries).astype(jnp.int32)
    mine = jnp.concatenate(
        [sel_index, jnp.broadcast_to(cache_offset[:, None], (SLOTS, SEL))], axis=0
    )
    half = np.arange(HD // 2) * 2.0 / HD
    freq = jnp.asarray(
        np.stack([np.tile(rope_base**-half, 2), np.repeat([-1.0, 1.0], HD // 2)]), jnp.float32
    )
    cosine, sine, ranks, valid = prepare(place, span_count, span_key, sel_index, freq)
    h1, h3, z0 = ring_x(hidden), back_x(hidden), pz(hidden)
    k1 = py(key_cache)
    project = functools.partial(partial_project, place)
    acc = project((H_AT,), (hidden,), weights)
    z1 = ring_x(after(z0, cosine, acc))
    z3 = pz(h3)
    v1 = py(after(value_cache, k1))
    acc = project((H_AT + 1, H_AT + 3), (h1, h3), weights, acc)
    z2 = ring_x(z1)
    h2 = ring_x(after(h1, z1))
    acc = project((Z_AT, Z_AT + 1), (z0, z1), weights, acc)
    acc, kept = project((Z_AT + 3, Z_AT + 2, H_AT + 2), (z3,), weights, acc, ahead=2)
    acc = after(acc, k1)
    query, fresh = last_project(z2, h2, kept, acc, cosine, sine, mine)
    near, behind = ring_z(query), back_z(query)
    far = ring_z(near)
    jk, jv = join(ranks, key_cache, value_cache, k1, v1, fresh, py(fresh), mine, freq)
    out_near = back_z(attend(1, valid, near, jk, jv))
    out_behind = ring_z(attend(3, valid, behind, jk, jv))
    out_far = far_z(attend(2, valid, far, jk, jv))
    own = attend(0, valid, query, jk, jv, mine)
    return merge(own, out_near, out_behind, out_far)


def solution(mesh):
    split = Mesh(mesh.devices.reshape(4, 2, 2, 2, 2, 4), AXES)
    seq, tp = AXES[:4], AXES[4:]
    placed = (
        P(seq, tp),
        P(None, tp),
        P(None, tp),
        P(None, tp),
        P(seq, tp),
        P(seq, tp),
        P(),
        P(),
        P(seq),
        P(seq, None),
    )
    return jax.shard_map(
        shards, mesh=split, in_specs=placed, out_specs=P(seq, tp), check_vma=False
    )
```

```python
import functools
import math

import jax
import jax.numpy as jnp
import numpy as np
from jax import lax
from jax.experimental import pallas as pl
from jax.experimental.pallas import tpu as pltpu
from jax.sharding import Mesh, PartitionSpec as P

HD = 128
HG = 4
R = 8
MAXCH = 8
SPAN = 1024
SEL = 128
SLOTS = 2
ROWS = SLOTS * SEL
QW = HG * HD
PACK = SEL + 16
DK = 896
PROJ = 16

rope_base = 5000000.0
low = -1.0e30
SCALE2 = math.log2(math.e) / math.sqrt(HD)

vmem = pl.BlockSpec(memory_space=pltpu.VMEM)
smem = pl.BlockSpec(memory_space=pltpu.SMEM)
hbm = pl.BlockSpec(memory_space=pltpu.HBM)
tiny = pl.CostEstimate(flops=1, bytes_accessed=1, transcendentals=0)


def work(microseconds):
    return pl.CostEstimate(
        flops=microseconds * 1000000000, bytes_accessed=1, transcendentals=0
    )


AXES = ("zh", "yh", "yp", "c", "zl", "x")


def opposite_ways(n):
    plus = [(i, (i + 1) % n) for i in range(n)]
    minus = [(n + i, n + (i - 1) % n) for i in range(n)]
    return plus + minus


def ring_x(v):
    return lax.ppermute(v, ("c", "x"), opposite_ways(4))


def back_x(v):
    pairs = [(4 * c + i, 4 * c + (i - 1 + 2 * c) % 4) for c in range(2) for i in range(4)]
    return lax.ppermute(v, ("c", "x"), pairs)


def ring_z(v):
    pairs = [(2 * i + c, 2 * ((i + 1 - 2 * c) % 4) + c) for i in range(4) for c in range(2)]
    return lax.ppermute(v, ("zh", "c"), pairs)


def back_z(v):
    pairs = [(2 * i + c, 2 * ((i - 1 + 2 * c) % 4) + c) for i in range(4) for c in range(2)]
    return lax.ppermute(v, ("zh", "c"), pairs)


def far_z(v):
    return lax.ppermute(v, "zh", [(i, (i + 2) % 4) for i in range(4)])


def pz(v):
    return lax.ppermute(v, "zl", [(0, 1), (1, 0)])


def py(v):
    return lax.ppermute(v, "yh", [(0, 1), (1, 0)])


H_AT, Z_AT, ZH_AT, YH_AT, WAY_AT, REQ_AT = 0, 4, 8, 9, 10, 11


def prepare_kernel(place, count, key, sel_ref, freq_ref, cos_ref, sin_ref, rank_ref, valid_ref):
    freq = freq_ref[0:1, :]
    sign = freq_ref[1:2, :]
    zh, yh, way = place[ZH_AT], place[YH_AT], place[WAY_AT]
    for r in range(SLOTS):
        request = place[REQ_AT] + r
        used = count[request]

        def rank(j, request=request, used=used):
            mine = key[request, j]
            total = jnp.int32(0)
            for k in range(MAXCH):
                smaller = (key[request, k] < mine) & (k < used)
                total += jnp.where(smaller, 1, 0)
            return total

        spans = (zh * 2 + yh, zh * 2 + 1 - yh)
        ranks = [rank(j) for j in spans]
        for sp in range(2):
            rank_ref[r * 2 + sp] = ranks[sp]
        for shift in range(4):
            j = lax.rem(zh + shift * way + 4, 4) * 2 + yh
            mine = rank(j)
            for sp in range(2):
                good = (j < used) & (spans[sp] < used) & (ranks[sp] <= mine)
                valid_ref[shift * 4 + r * 2 + sp] = jnp.where(good, 1, 0)
        position = (sel_ref[r : r + 1, :] + ranks[0] * SPAN).astype(jnp.float32)
        angle = jnp.broadcast_to(position, (SEL, HD)).T * freq
        cos_ref[r * SEL : (r + 1) * SEL, :] = jnp.cos(angle)
        sin_ref[r * SEL : (r + 1) * SEL, :] = jnp.sin(angle) * sign


def prepare(*args):
    shape = jax.ShapeDtypeStruct
    return pl.pallas_call(
        prepare_kernel,
        out_shape=(
            shape((ROWS, HD), jnp.float32),
            shape((ROWS, HD), jnp.float32),
            shape((4,), jnp.int32),
            shape((16,), jnp.int32),
        ),
        in_specs=[smem] * 3 + [vmem] * 2,
        out_specs=(vmem, vmem, smem, smem),
        compiler_params=pltpu.CompilerParams(vmem_limit_bytes=8 << 20),
        cost_estimate=work(2),
        name="prepare",
    )(*args)


def turned(v, cosine, sine):
    return v * cosine + pltpu.roll(v, HD // 2, 1) * sine


def weight_copies(sources, piece, i, to_ref, slot, sem):
    at = pl.ds(pl.multiple_of(piece * DK, DK), DK)
    start = 0
    for j, (w, width) in enumerate(zip(sources, (QW, HD, HD))):
        to = to_ref.at[slot, :, start : start + width]
        yield pltpu.make_async_copy(w.at[at, :], to, sem.at[i, j])
        start += width


def partial_kernel(which, ahead, carried, place, *refs):
    count = len(which) - ahead
    pieces, refs = refs[:count], refs[count:]
    sources, refs = refs[:3], refs[3:]
    if carried:
        acc_ref, refs = refs[0], refs[1:]
    out_ref, refs = refs[0], refs[1:]
    if ahead:
        next_ref, refs = refs[0], refs[1:]
    weight, sem = refs
    for i in range(count + ahead):
        to, slot = (weight, i) if i < count else (next_ref, i - count)
        for copy in weight_copies(sources, place[which[i]], i, to, slot, sem):
            copy.start()
    acc = acc_ref[...] if carried else None
    for i in range(count):
        for copy in weight_copies(sources, place[which[i]], i, weight, i, sem):
            copy.wait()
        d = jnp.dot(pieces[i][...], weight[i], preferred_element_type=jnp.float32)
        acc = d if acc is None else acc + d
    out_ref[...] = acc
    for i in range(count, count + ahead):
        for copy in weight_copies(sources, place[which[i]], i, next_ref, i - count, sem):
            copy.wait()


def partial_project(place, which, pieces, weights, acc=None, ahead=0):
    n = len(pieces)
    sums = jax.ShapeDtypeStruct((ROWS, QW + 2 * HD), jnp.float32)
    kept = jax.ShapeDtypeStruct((ahead, DK, QW + 2 * HD), jnp.bfloat16)
    extra = [] if acc is None else [acc]
    weights = [pltpu.with_memory_space_constraint(w, pltpu.HBM) for w in weights]
    return pl.pallas_call(
        functools.partial(partial_kernel, which, ahead, acc is not None),
        out_shape=(sums, kept) if ahead else sums,
        in_specs=[smem] + [vmem] * n + [hbm] * 3 + [vmem] * len(extra),
        out_specs=(vmem, vmem) if ahead else vmem,
        scratch_shapes=[
            pltpu.VMEM((n, DK, QW + 2 * HD), jnp.bfloat16),
            pltpu.SemaphoreType.DMA((n + ahead, 3)),
        ],
        compiler_params=pltpu.CompilerParams(vmem_limit_bytes=16 << 20),
        cost_estimate=work(6),
        name="project",
    )(place, *pieces, *weights, *extra)


def last_kernel(piece_ref, weight_ref, acc_ref, cos_ref, sin_ref, mine_ref, q_ref, n_ref):
    acc = acc_ref[...] + jnp.dot(
        piece_ref[...], weight_ref[0], preferred_element_type=jnp.float32
    )
    cosine, sine = cos_ref[...], sin_ref[...]
    for g in range(HG):
        at = slice(g * HD, (g + 1) * HD)
        q_ref[:, at] = turned(acc[:, at], cosine, sine).astype(jnp.bfloat16)
    n_ref[:ROWS, :] = turned(acc[:, QW : QW + HD], cosine, sine).astype(jnp.bfloat16)
    n_ref[ROWS : 2 * ROWS, :] = acc[:, QW + HD :].astype(jnp.bfloat16)
    mine = mine_ref[...]
    high = lax.shift_right_logical(mine, 6)
    both = jnp.concatenate([high, mine - high * 64, jnp.zeros((8, SEL), jnp.int32)], axis=0)
    n_ref[2 * ROWS :, :] = both.astype(jnp.float32).astype(jnp.bfloat16)


def last_project(*args):
    return pl.pallas_call(
        last_kernel,
        out_shape=(
            jax.ShapeDtypeStruct((ROWS, QW), jnp.bfloat16),
            jax.ShapeDtypeStruct((2 * ROWS + 16, HD), jnp.bfloat16),
        ),
        in_specs=[vmem] * 6,
        out_specs=(vmem, vmem),
        compiler_params=pltpu.CompilerParams(vmem_limit_bytes=16 << 20),
        cost_estimate=tiny,
        name="project_last",
    )(*args)


def attend_block(q, keys, vals, limit, m_ref, l_ref, acc_ref):
    s = lax.dot_general(keys, q, (((1,), (1,)), ((), ())), preferred_element_type=jnp.float32)
    if limit is not None:
        at = lax.broadcasted_iota(jnp.int32, s.shape, 0)
        s = jnp.where(at <= limit, s, low)
    old = m_ref[...]
    new = jnp.maximum(old, jnp.max(s, axis=0, keepdims=True))
    factor = jnp.exp2((old - new) * SCALE2)
    weight = jnp.exp2((s - new) * SCALE2)
    l_ref[...] = l_ref[...] * factor + jnp.sum(weight, axis=0, keepdims=True)
    acc_ref[...] = acc_ref[...] * factor + lax.dot_general(
        vals,
        weight.astype(jnp.bfloat16),
        (((0,), (0,)), ((), ())),
        preferred_element_type=jnp.float32,
    )
    m_ref[...] = new


def attend_source(rows_ref, i, jk_ref, jv_ref, r, valid_ref, first, o_ref, state, limit_ref=None):
    m_ref, l_ref, acc_ref = state
    m_ref[...] = jnp.full_like(m_ref, low)
    l_ref[...] = jnp.zeros_like(l_ref)
    acc_ref[...] = jnp.zeros_like(acc_ref)

    def span(sp, _):
        @pl.when(valid_ref[first + sp] != 0)
        def _():
            limit = None if limit_ref is None else jnp.where(sp == 0, limit_ref[...], SPAN)
            attend_block(
                rows_ref[i], jk_ref[r * 2 + sp], jv_ref[r * 2 + sp], limit, m_ref, l_ref, acc_ref
            )

        return 0

    lax.fori_loop(0, 2, span, 0)
    l = l_ref[...]
    some = l > 0.0
    mixed = acc_ref[...] / jnp.where(some, l, 1.0)
    rest = jnp.where(some, m_ref[...] * SCALE2 + jnp.log2(jnp.where(some, l, 1.0)), low)
    rows = []
    for k in range(3):
        part = rest.astype(jnp.bfloat16).astype(jnp.float32)
        rows += [part[:, g * SEL : (g + 1) * SEL] for g in range(HG)]
        rest = rest - part
    for g in range(HG):
        at = slice(g * SEL, (g + 1) * SEL)
        o_ref[i, :SEL, g * HD : (g + 1) * HD] = mixed[:, at].T.astype(jnp.bfloat16)
    stat = jnp.concatenate(rows + [jnp.zeros((HG, SEL), jnp.float32)], axis=0)
    o_ref[i, SEL:, :HD] = stat.astype(jnp.bfloat16)
    o_ref[i, SEL:, HD:] = jnp.zeros((16, QW - HD), jnp.bfloat16)


def spread(rows_ref, i, q):
    for g in range(HG):
        rows_ref[i, g * SEL : (g + 1) * SEL, :] = q[:, g * HD : (g + 1) * HD]


def join_kernel(rank_ref, k0, v0, k1, v1, n0, n1, mine_ref, freq_ref, jk_ref, jv_ref):
    freq = freq_ref[0:1, :]
    sign = freq_ref[1:2, :]
    mine = mine_ref[...]
    both = n1[2 * ROWS :, :].astype(jnp.float32)
    theirs = (both[0:4] * 64.0 + both[4:8]).astype(jnp.int32)
    for r in range(SLOTS):
        rows = slice(r * SPAN, (r + 1) * SPAN)
        for sp, (kr, vr, nr, here) in enumerate(((k0, v0, n0, mine), (k1, v1, n1, theirs))):
            offset = here[SLOTS + r : SLOTS + r + 1, :]
            angle = (rank_ref[r * 2 + sp] * SPAN - offset).astype(jnp.float32) * freq
            raw = kr[rows, :].astype(jnp.float32)
            cached = turned(raw, jnp.cos(angle), jnp.sin(angle) * sign)
            at = lax.broadcasted_iota(jnp.int32, (SPAN, SEL), 0)
            pick = (at == here[r : r + 1, :]).astype(jnp.float32).astype(jnp.bfloat16)
            ones = jnp.ones((SEL, HD), jnp.bfloat16)
            hit = jnp.dot(pick, ones, preferred_element_type=jnp.float32) > 0.5
            fresh_k = nr[r * SEL : (r + 1) * SEL, :]
            fresh_v = nr[ROWS + r * SEL : ROWS + (r + 1) * SEL, :]
            put_k = jnp.dot(pick, fresh_k, preferred_element_type=jnp.float32)
            put_v = jnp.dot(pick, fresh_v, preferred_element_type=jnp.float32)
            vals = vr[rows, :].astype(jnp.float32)
            jk_ref[r * 2 + sp] = jnp.where(hit, put_k, cached).astype(jnp.bfloat16)
            jv_ref[r * 2 + sp] = jnp.where(hit, put_v, vals).astype(jnp.bfloat16)


def attend_kernel(shift, valid_ref, q_ref, jk_ref, jv_ref, *refs):
    if shift == 0:
        sel_ref, o_ref, rows_ref, limit_ref = refs[:4]
        state = refs[4:]
    else:
        o_ref, rows_ref = refs[:2]
        limit_ref, state = None, refs[2:]
    for r in range(SLOTS):
        spread(rows_ref, r, q_ref[r * SEL : (r + 1) * SEL, :])

    def request(r, _):
        if shift == 0:
            limit_ref[...] = jnp.concatenate([sel_ref[pl.ds(r, 1), :]] * HG, axis=1)
        attend_source(
            rows_ref, r, jk_ref, jv_ref, r, valid_ref, shift * 4 + r * 2, o_ref, state, limit_ref
        )
        return 0

    lax.fori_loop(0, SLOTS, request, 0)


joined_shape = jax.ShapeDtypeStruct((SLOTS * 2, SPAN, HD), jnp.bfloat16)
packed_shape = jax.ShapeDtypeStruct((SLOTS, PACK, QW), jnp.bfloat16)


def join(*args):
    return pl.pallas_call(
        join_kernel,
        out_shape=(joined_shape, joined_shape),
        in_specs=[smem] + [vmem] * 8,
        out_specs=(vmem, vmem),
        compiler_params=pltpu.CompilerParams(vmem_limit_bytes=16 << 20),
        cost_estimate=work(3),
        name="join",
    )(*args)


def attend(shift, valid, *args):
    return pl.pallas_call(
        functools.partial(attend_kernel, shift),
        out_shape=packed_shape,
        in_specs=[smem] + [vmem] * len(args),
        out_specs=vmem,
        scratch_shapes=[pltpu.VMEM((SLOTS, HG * SEL, HD), jnp.bfloat16)]
        + ([pltpu.VMEM((1, HG * SEL), jnp.int32)] if shift == 0 else [])
        + [
            pltpu.VMEM((1, HG * SEL), jnp.float32),
            pltpu.VMEM((1, HG * SEL), jnp.float32),
            pltpu.VMEM((HD, HG * SEL), jnp.float32),
        ],
        compiler_params=pltpu.CompilerParams(vmem_limit_bytes=16 << 20),
        cost_estimate=work(1),
        name="attend",
    )(valid, *args)


def merge_parts(parts, put):
    lse = []
    for p in parts:
        stat = p[SEL:, :HD].astype(jnp.float32)
        lse.append(stat[0:4] + stat[4:8] + stat[8:12])
    top = functools.reduce(jnp.maximum, lse)
    weight = [jnp.exp2(v - top) for v in lse]
    total = functools.reduce(jnp.add, weight)
    pad = jnp.zeros((HD - HG, SEL), jnp.float32)
    weight = [jnp.concatenate([w / total, pad], axis=0).T for w in weight]
    for g in range(HG):
        at = slice(g * HD, (g + 1) * HD)
        mixed = jnp.zeros((SEL, HD), jnp.float32)
        for w, p in zip(weight, parts):
            mixed += w[:, g : g + 1] * p[:SEL, at].astype(jnp.float32)
        put(at, mixed.astype(jnp.bfloat16))


def merge_kernel(*refs):
    o_ref = refs[-1]
    for r in range(SLOTS):

        def put(at, value, r=r):
            o_ref[r * SEL : (r + 1) * SEL, at] = value

        merge_parts([p.at[r] for p in refs[:-1]], put)


def merge(*parts):
    return pl.pallas_call(
        merge_kernel,
        out_shape=jax.ShapeDtypeStruct((ROWS, QW), jnp.bfloat16),
        in_specs=[vmem] * len(parts),
        out_specs=vmem,
        compiler_params=pltpu.CompilerParams(vmem_limit_bytes=8 << 20),
        cost_estimate=tiny,
        name="merge",
    )(*parts)


def after(value, *others):
    return lax.optimization_barrier((value, *others))[0]


def shards(
    hidden, w_query, w_key, w_value, key_cache, value_cache,
    span_count, span_key, cache_offset, sel_index,
):
    zh, yh, yp, c = (lax.axis_index(a) for a in ("zh", "yh", "yp", "c"))
    zl, x = lax.axis_index("zl"), lax.axis_index("x")
    weights = (w_query, w_key, w_value)
    way = 2 * c - 1
    entries = [zl * 4 + (x + i * way) % 4 for i in range(4)]
    entries += [(1 - zl) * 4 + (x + i * way) % 4 for i in range(4)]
    entries += [zh, yh, way, (yp * 2 + c) * SLOTS]
    place = jnp.stack(entries).astype(jnp.int32)
    mine = jnp.concatenate(
        [sel_index, jnp.broadcast_to(cache_offset[:, None], (SLOTS, SEL))], axis=0
    )
    half = np.arange(HD // 2) * 2.0 / HD
    freq = jnp.asarray(
        np.stack([np.tile(rope_base**-half, 2), np.repeat([-1.0, 1.0], HD // 2)]), jnp.float32
    )
    cosine, sine, ranks, valid = prepare(place, span_count, span_key, sel_index, freq)
    h1, h3, z0 = ring_x(hidden), back_x(hidden), pz(hidden)
    k1 = py(key_cache)
    project = functools.partial(partial_project, place)
    acc = project((H_AT,), (hidden,), weights)
    h2 = ring_x(after(h1, cosine, acc))
    z1 = ring_x(z0)
    z3 = pz(h3)
    v1 = py(after(value_cache, k1))
    acc = project((H_AT + 1, H_AT + 3), (h1, h3), weights, acc)
    z2 = ring_x(z1)
    acc = project((Z_AT, H_AT + 2), (z0, h2), weights, acc)
    acc, kept = project(
        (Z_AT + 3, Z_AT + 1, Z_AT + 2), (z3, z1), weights, acc, ahead=1
    )
    acc = after(acc, k1)
    query, fresh = last_project(z2, kept, acc, cosine, sine, mine)
    near, behind = ring_z(query), back_z(query)
    far = ring_z(near)
    jk, jv = join(ranks, key_cache, value_cache, k1, v1, fresh, py(fresh), mine, freq)
    out_near = back_z(attend(1, valid, near, jk, jv))
    out_behind = ring_z(attend(3, valid, behind, jk, jv))
    out_far = far_z(attend(2, valid, far, jk, jv))
    own = attend(0, valid, query, jk, jv, mine)
    return merge(own, out_near, out_behind, out_far)


def solution(mesh):
    split = Mesh(mesh.devices.reshape(4, 2, 2, 2, 2, 4), AXES)
    seq, tp = AXES[:4], AXES[4:]
    placed = (
        P(seq, tp),
        P(None, tp),
        P(None, tp),
        P(None, tp),
        P(seq, tp),
        P(seq, tp),
        P(),
        P(),
        P(seq),
        P(seq, None),
    )
    return jax.shard_map(
        shards, mesh=split, in_specs=placed, out_specs=P(seq, tp), check_vma=False
    )
```
